32 devices in a mesh: groups: 2 (over x), seq: 16 (over z, y, core).
Axes of the slice: x: 2, y: 2, z: 4, core: 2. Of those that a mesh axis runs over, the one named last changes fastest.
Arguments:
- query: bfloat16 [2048, 4096], P(('groups', 'seq')), parts along dimension 0, may hold values from -28 to 28
- keys: bfloat16 [2048, 512], P(('groups', 'seq')), parts along dimension 0, may hold values from -4 to 4
- values: bfloat16 [2048, 512], P(('groups', 'seq')), parts along dimension 0, may hold values from -6 to 6
- query_bias: bfloat16 [4096], P('seq'), may hold values from -3 to 3
- key_bias: bfloat16 [512], P('seq'), may hold values from -3 to 3
- value_projection_bias: bfloat16 [512], P('seq'), may hold values from -3 to 3
- frame_order: int32 [128], P(('groups', 'seq')), parts along dimension 0, may hold values from 0 to 63, each once
Outputs:
- attended: bfloat16 [2048, 4096], P(('groups', 'seq')), parts along dimension 0
The draws below stay inside these ranges and needn't reach their ends.
There are 2 independent parts, one for each index of `groups`. The reference program is written for one: setup_inputs(seed, part) draws one part's arguments, and reference() takes and returns one part's arrays. A program takes and returns all parts, laid end to end along the dimension named above; an argument that names none is the same for every part. Nothing has to cross between parts.
Inputs may be any that keep to these rules, and one draw needn't show every extreme that they name: `frame_order`: each of the 64 frames stands in exactly one slot.
All inputs are finite; a program needn't handle non-finite values.
Results may differ from the reference program's by a relative error of at most 0.011.
Values may be sent and summed in bfloat16 or wider, within the bound.
A program may use at most 64 MiB of HBM per device.

```python
import math
import jax
import jax.numpy as jnp
from jax import lax

HEAD_SIZE = 128
QH = 32
KVH = 4
GRID = 4
FRAME_TOK = 16
FRAMES = 64
VISUAL_TOKENS = 1024


def draw_keys(key, part):
    result = jnp.clip(jax.random.normal(jax.random.fold_in(key, 13), (VISUAL_TOKENS, KVH * HEAD_SIZE), jnp.float32), -4.0, 4.0)
    return result.astype(jnp.bfloat16)


def draw_query(key, part):
    result = jnp.clip(jax.random.normal(jax.random.fold_in(key, 19), (VISUAL_TOKENS, QH * HEAD_SIZE), jnp.float32), -4.0, 4.0)
    return result.astype(jnp.bfloat16)


def block_scale(rng, shape, cuts, low, largest):
    loudness = 1.0
    for axis_at, blocks in cuts:
        draws = jax.random.uniform(jax.random.fold_in(jax.random.fold_in(rng, 6), axis_at), (blocks,), jnp.float32, low / len(cuts), largest / len(cuts))
        loudness = loudness * jnp.repeat(jnp.exp(draws), shape[axis_at] // blocks).reshape((-1,) + (1,) * (len(shape) - 1 - axis_at))
    return loudness


def scatter_about(stream_key, shape, deviation, reach, shards=(), held_as=jnp.bfloat16):
    values = deviation * jax.random.normal(stream_key, shape, jnp.float32)
    if shards:
        values = values * block_scale(stream_key, shape, shards, -0.22, 0.18)
    return jnp.clip(values, -reach, reach).astype(held_as)


def setup_inputs(seed: int = 0, part: int = 0) -> dict:
    key_list = jax.random.split(jax.random.key(seed), 8)
    part_splits = jax.random.split(jax.random.fold_in(key_list[7], part), 8)
    query = draw_query(jax.random.fold_in(jax.random.fold_in(key_list[7], part), 71), part)
    keys = draw_keys(jax.random.fold_in(jax.random.fold_in(key_list[7], part), 71), part)
    values = scatter_about(part_splits[2], (VISUAL_TOKENS, KVH * HEAD_SIZE), 1.0, 6.0, ((0, 16),))
    query_bias = scatter_about(key_list[3], (QH * HEAD_SIZE,), 0.5, 3.0, ((0, 16),))
    key_bias = scatter_about(key_list[4], (KVH * HEAD_SIZE,), 0.5, 3.0, ((0, 16),))
    value_projection_bias = scatter_about(key_list[5], (KVH * HEAD_SIZE,), 0.5, 3.0, ((0, 16),))
    frame_order = jax.random.permutation(part_splits[6], FRAMES).astype(jnp.int32)
    return {"query": query, "keys": keys, "values": values, "query_bias": query_bias, "key_bias": key_bias, "value_projection_bias": value_projection_bias, "frame_order": frame_order}


def positions(frame_order):
    count = frame_order.shape[0]
    within = jnp.tile(jnp.arange(FRAME_TOK, dtype=jnp.int32), count)
    return jnp.repeat(frame_order, FRAME_TOK) * FRAME_TOK + within

def rotate(matrix, gpos, heads):
    rows = matrix.shape[0]
    half = HEAD_SIZE // 2
    frame = gpos // FRAME_TOK
    within = gpos % FRAME_TOK
    temporal = (2 * frame).astype(matrix.dtype)
    vertical = (within // GRID).astype(matrix.dtype)
    lateral = (within % GRID).astype(matrix.dtype)
    pair = jnp.arange(half).astype(matrix.dtype)
    freq = jnp.exp(-(2.0 * pair / HEAD_SIZE) * math.log(1000000.0))
    source = jnp.where(pair[None, :] < half // 4, temporal[:, None], jnp.where(pair[None, :] < half // 4 + 3 * half // 8, vertical[:, None], lateral[:, None]))
    angle = source * freq[None, :]
    cosine = jnp.concatenate([jnp.cos(angle), jnp.cos(angle)], axis=1)[:, None, :]
    sine = jnp.concatenate([jnp.sin(angle), jnp.sin(angle)], axis=1)[:, None, :]
    shaped = matrix.reshape(rows, heads, HEAD_SIZE)
    turned = jnp.concatenate([-shaped[..., half:], shaped[..., :half]], axis=2)
    return (shaped * cosine + turned * sine).reshape(rows, heads * HEAD_SIZE)

def reference(query, keys, values, query_bias, key_bias, value_projection_bias, frame_order):
    gpos = positions(frame_order)
    qrot = rotate(query.astype(jnp.float32) + query_bias.astype(jnp.float32), gpos, QH).astype(jnp.bfloat16)
    krot = rotate(keys.astype(jnp.float32) + key_bias.astype(jnp.float32), gpos, KVH).astype(jnp.bfloat16)
    value_addend = (values.astype(jnp.float32) + value_projection_bias.astype(jnp.float32)).astype(jnp.bfloat16)
    ratio = QH // KVH
    scale = 1.0 / math.sqrt(HEAD_SIZE)
    qblock = math.gcd(VISUAL_TOKENS, 2048)
    qcount = VISUAL_TOKENS // qblock

    def one_head(head):
        query_group = head // ratio
        k_head = lax.dynamic_slice_in_dim(krot, (query_group * HEAD_SIZE).astype(jnp.int32), HEAD_SIZE, 1)
        value_head_slice = lax.dynamic_slice_in_dim(value_addend, (query_group * HEAD_SIZE).astype(jnp.int32), HEAD_SIZE, 1)

        def one_block(index):
            first = (index * qblock).astype(jnp.int32)
            q_rows = lax.dynamic_slice(qrot, (first, (head * HEAD_SIZE).astype(jnp.int32)), (qblock, HEAD_SIZE))
            q_pos = lax.dynamic_slice_in_dim(gpos, first, qblock)
            visible = gpos[None, :] <= q_pos[:, None]
            scores = jnp.dot(q_rows, k_head.T, preferred_element_type=jnp.float32) * scale
            top = lax.optimization_barrier(jnp.max(jnp.where(visible, scores, -1e+30), axis=1))
            expo = jnp.where(visible, jnp.exp(scores - top[:, None]), 0.0)
            den = lax.optimization_barrier(jnp.sum(expo, axis=1))
            mixed = jnp.dot(expo.astype(jnp.bfloat16), value_head_slice, preferred_element_type=jnp.float32)
            return (mixed / den[:, None]).astype(jnp.bfloat16)
        blocks = lax.map(one_block, jnp.arange(qcount, dtype=jnp.int32))
        return blocks.reshape(VISUAL_TOKENS, HEAD_SIZE)
    heads = lax.map(one_head, jnp.arange(QH, dtype=jnp.int32))
    return heads.transpose(1, 0, 2).reshape(VISUAL_TOKENS, QH * HEAD_SIZE)
```

```python
import functools
import math

import jax
import jax.numpy as jnp
import numpy as np
from jax import lax
from jax.experimental import pallas as pl
from jax.experimental.pallas import tpu as pltpu
from jax.sharding import PartitionSpec as P

HEAD = 128
HALF = HEAD // 2
QH = 32
KVH = 4
RATIO = QH // KVH
GRID = 4
FRAME_TOK = 16
MESH = pl.DeviceIdType.MESH
NEG = -1e30
PIECES = 2
PAIRS_T = HALF // 4
PAIRS_R = HALF // 4 + 3 * HALF // 8


def tables():
    pair = np.arange(HEAD) % HALF
    freq = np.exp(-(2.0 * pair / HEAD) * math.log(1000000.0))
    tok = np.arange(FRAME_TOK)
    source = np.where(pair[None, :] < PAIRS_R, (tok // GRID)[:, None], (tok % GRID)[:, None])
    angle = source * freq[None, :]
    sign = np.where(np.arange(HEAD) < HALF, -1.0, 1.0)
    rows = np.zeros((40, HEAD), np.float32)
    rows[0:16] = np.cos(angle)
    rows[16:32] = np.sin(angle) * sign[None, :]
    rows[32] = 2.0 * freq
    return rows


def cos_sin(frames, spatial):
    angle = frames * spatial[32:33, :]
    turns = jnp.round(angle * (1.0 / (2.0 * math.pi)))
    angle = angle - turns * 6.28125
    angle = angle - turns * (2.0 * math.pi - 6.28125)
    lane = lax.broadcasted_iota(jnp.int32, (FRAME_TOK, HEAD), 1)
    temporal = lane % HALF < PAIRS_T
    sign = jnp.where(lane < HALF, -1.0, 1.0)
    cos_t, sin_t = jnp.cos(angle), jnp.sin(angle)
    cosines, sines = [], []
    for j in range(frames.shape[0]):
        cosines.append(jnp.where(temporal, cos_t[j : j + 1, :], spatial[0:16, :]))
        sines.append(jnp.where(temporal, sin_t[j : j + 1, :] * sign, spatial[16:32, :]))
    return jnp.concatenate(cosines, axis=0), jnp.concatenate(sines, axis=0)


def spin(x, cosine, sine):
    return x * cosine + pltpu.roll(x, HALF, 1) * sine


def kernel(
    A, B, n, qper,
    q_hbm, k_hbm, v_hbm, qb_hbm, kb_hbm, vb_hbm, order_hbm, tab_hbm,
    o_ref,
    qb_ref, kb_ref, vb_ref, order_ref, tab_ref,
    q_ref, pack_ref, kbuf, vbuf, pbuf, qs, acc, top, den, ksc, vsc, hide,
    recv, send, precv, psend, load,
):
    me = lax.axis_index("seq")
    rows = kbuf.shape[1]
    frames = rows // FRAME_TOK
    cut = rows // (PIECES // 2)
    core = me % 2
    b = (me // 2) % B
    a = me // (2 * B)

    def piece(p, s):
        return (kbuf, vbuf)[p % 2].at[s, pl.ds((p // 2) * cut, cut)]

    def slot(x, y, z):
        return (x * B + y) * 2 + z

    ways = (
        (a + 1 < A, slot(a + 1, b, core)),
        (a > 0, slot(a - 1, b, core)),
        (b + 1 < B, slot(a, b + 1, core)),
        (b > 0, slot(a, b - 1, core)),
        (None, slot(a, b, 1 - core)),
    )

    def copy(t, s, way):
        return pltpu.make_async_remote_copy(
            src_ref=piece(t, s),
            dst_ref=piece(t, s),
            send_sem=send.at[t, way, s],
            recv_sem=recv.at[t, s],
            device_id={"seq": ways[way][1]},
            device_id_type=MESH,
        )

    def when(cond, act):
        if cond is None:
            act()
        else:
            pl.when(cond)(act)

    def fan(t, s, dirs, start):
        for way in dirs:
            c = copy(t, s, way)
            when(ways[way][0], c.start if start else c.wait_send)

    def arrive(t, s):
        copy(t, s, 4).wait_recv()

    def inside(i, size):
        return jnp.logical_and(i >= 0, i < size)

    def along_a(d, start):
        for t in range(PIECES):
            for sg in (1, -1):
                x = a + sg * d

                @pl.when(jnp.logical_and(inside(x, A), d < A))
                def _(x=x, sg=sg, t=t):
                    s = slot(x, b, core)
                    if start:
                        arrive(t, s)
                    fan(t, s, (1 if sg > 0 else 0, 2, 3, 4), start)

    def along_b(d, start):
        for e in range(1, B):
            for t in range(PIECES):
                for sg in (1, -1):
                    x = a + sg * d
                    ok = inside(x, A) if sg > 0 else jnp.logical_and(inside(x, A), d > 0)
                    for sb in (1, -1):
                        y = b + sb * e

                        @pl.when(jnp.logical_and(ok, inside(y, B)))
                        def _(x=x, y=y, sb=sb, t=t):
                            s = slot(x, y, core)
                            if start:
                                arrive(t, s)
                            fan(t, s, (3 if sb > 0 else 2, 4), start)

    barrier = pltpu.get_barrier_semaphore()

    def greet(i, _):
        pl.semaphore_signal(barrier, inc=1, device_id={"seq": lax.rem(me + i, n)}, device_id_type=MESH)
        return 0

    lax.fori_loop(1, n, greet, 0)
    k_load = pltpu.make_async_copy(k_hbm, kbuf.at[me], load.at[0])
    v_load = pltpu.make_async_copy(v_hbm, vbuf.at[me], load.at[1])
    q_load = pltpu.make_async_copy(q_hbm, q_ref, load.at[2])
    small = [
        pltpu.make_async_copy(src, dst, load.at[3 + i])
        for i, (src, dst) in enumerate((
            (order_hbm, order_ref), (qb_hbm, qb_ref), (kb_hbm, kb_ref), (vb_hbm, vb_ref), (tab_hbm, tab_ref),
        ))
    ]
    for c in small + [k_load, v_load, q_load]:
        c.start()

    lane = lax.broadcasted_iota(jnp.int32, (1, HEAD), 1)

    def placed(values):
        size = values.shape[1]
        spots = HEAD // size
        return jnp.where(lane // size == me % spots, jnp.concatenate([values] * spots, axis=1), 0.0)

    def row(ref):
        return ref[...].astype(jnp.float32)[None, :]

    for c in small:
        c.wait()
    pack_ref[...] = jnp.zeros_like(pack_ref)
    q_row = row(qb_ref)
    if qper >= HEAD:
        for i in range(qper // HEAD):
            pack_ref[i : i + 1, :] = q_row[:, i * HEAD : (i + 1) * HEAD]
    else:
        pack_ref[0:1, :] = placed(q_row)
    pack_ref[2:3, :] = placed(row(kb_ref))
    pack_ref[3:4, :] = placed(row(vb_ref))
    qpos = (lane % FRAME_TOK).astype(jnp.float32)
    for f in range(frames):
        frame = order_ref[f].astype(jnp.float32)
        pack_ref[8 - frames + f : 9 - frames + f, :] = jnp.full((1, HEAD), 1.0, jnp.float32) * frame
        qpos = qpos + jnp.where((lane % rows) // FRAME_TOK == f, frame * FRAME_TOK, 0.0)
    pbuf[me] = pack_ref[...]
    tab = tab_ref[...]
    q_cos, q_sin = cos_sin(pack_ref[8 - frames :, :], tab)
    fold = math.log2(math.e) / math.sqrt(HEAD)
    q_cos, q_sin = q_cos * fold, q_sin * fold
    k_load.wait()
    v_load.wait()
    pl.semaphore_wait(barrier, n - 1)

    def pack_copy(i, s):
        return pltpu.make_async_remote_copy(
            src_ref=pack_ref,
            dst_ref=pbuf.at[s],
            send_sem=psend.at[i],
            recv_sem=precv.at[s],
            device_id={"seq": lax.rem(me + i, n)},
            device_id_type=MESH,
        )

    def push(i, _):
        pack_copy(i, me).start()
        return 0

    lax.fori_loop(1, n, push, 0)
    for t in range(PIECES):
        fan(t, me, (0, 1, 2, 3, 4), True)

    acc[...] = jnp.zeros_like(acc)
    den[...] = jnp.zeros_like(den)
    top[...] = jnp.full_like(top, NEG)

    def pulled(i, _):
        pack_copy(i, lax.rem(me + i, n)).wait_recv()
        return 0

    lax.fori_loop(1, n, pulled, 0)
    q_load.wait()

    for h in range(QH):
        if qper >= HEAD:
            per = qper // HEAD
            bias = pbuf[h // per, h % per : h % per + 1, :]
        else:
            parts = HEAD // qper
            bias = sum(pbuf[h * parts + i, 0:1, :] for i in range(parts))
        x = q_ref[:, h * HEAD : (h + 1) * HEAD].astype(jnp.float32) + bias
        at = (h % RATIO) * rows
        qs[h // RATIO, at : at + rows, :] = spin(x, q_cos, q_sin).astype(jnp.bfloat16)
    share = n // KVH
    k_bias = [sum(pbuf[g * share + i, 2:3, :] for i in range(share)) for g in range(KVH)]
    v_bias = [sum(pbuf[g * share + i, 3:4, :] for i in range(share)) for g in range(KVH)]
    within = lax.broadcasted_iota(jnp.int32, (FRAME_TOK, HEAD), 0).astype(jnp.float32)

    def chunk(first):
        for j in range(4):
            s = first + j
            order = pbuf[s][8 - frames :, :]
            cosine, sine = cos_sin(order, tab)
            for f in range(frames):
                kpos = order[f : f + 1, :] * FRAME_TOK + within
                at = j * rows + f * FRAME_TOK
                hide[at : at + FRAME_TOK, :] = jnp.where(kpos <= qpos, 0.0, NEG)
            for g in range(KVH):
                cols = slice(g * HEAD, (g + 1) * HEAD)
                x = kbuf[s, :, cols].astype(jnp.float32) + k_bias[g]
                ksc[g, j * rows : (j + 1) * rows, :] = spin(x, cosine, sine).astype(jnp.bfloat16)
                y = vbuf[s, :, cols].astype(jnp.float32) + v_bias[g]
                vsc[g, j * rows : (j + 1) * rows, :] = y.astype(jnp.bfloat16)
        for g in range(KVH):
            scores = lax.dot_general(
                ksc[g], qs[g], (((1,), (1,)), ((), ())), preferred_element_type=jnp.float32
            )
            mask = hide[...]
            scores = scores + jnp.concatenate([mask] * (scores.shape[1] // HEAD), axis=1)
            old = top[g]
            new = jnp.maximum(old, jnp.max(scores, axis=0, keepdims=True))
            expo = jnp.exp2(scores - new)
            factor = jnp.exp2(old - new)
            top[g] = new
            den[g] = den[g] * factor + jnp.sum(expo, axis=0, keepdims=True)
            acc[g] = acc[g] * factor + lax.dot_general(
                vsc[g], expo.astype(jnp.bfloat16), (((0,), (0,)), ((), ())),
                preferred_element_type=jnp.float32,
            )

    low = a < A // 2
    mirror = jnp.where(low, a, A - 1 - a)

    def step(d, _):
        along_a(d + 1, True)
        along_b(d, True)
        near = jnp.where(d % 2 == 1, -((d + 1) // 2), d // 2)
        plane = mirror + jnp.where(d <= 2 * mirror, near, d - mirror)
        plane = jnp.where(low, plane, A - 1 - plane)
        for y in range(B):
            for t in range(PIECES):
                arrive(t, slot(plane, y, 1 - core))
        if 2 * B == 4:
            chunk(plane * 4)
        else:
            def part(i, _):
                chunk(plane * 2 * B + i * 4)
                return 0

            lax.fori_loop(0, 2 * B // 4, part, 0)
        return 0

    lax.fori_loop(0, A, step, 0)

    for g in range(KVH):
        mixed = acc[g] * (1.0 / den[g])
        flat = mixed.T.astype(jnp.bfloat16)
        for r in range(RATIO):
            h = g * RATIO + r
            o_ref[:, h * HEAD : (h + 1) * HEAD] = flat[r * rows : (r + 1) * rows, :]

    for t in range(PIECES):
        fan(t, me, (0, 1, 2, 3, 4), False)

    def drain(d, _):
        along_a(d + 1, False)
        along_b(d, False)
        return 0

    lax.fori_loop(0, A, drain, 0)

    def pushed(i, _):
        pack_copy(i, me).wait_send()
        return 0

    lax.fori_loop(1, n, pushed, 0)


def line_tables():
    rows = tables()
    pair = np.arange(HEAD) % HALF
    temporal = pair < PAIRS_T
    rows[0:32, temporal] = 0.0
    rows[32] = np.where(temporal, rows[32], 0.0)
    rows[33] = np.where(temporal, 1.0, 0.0)
    rows[34] = np.where(temporal, np.where(np.arange(HEAD) < HALF, -1.0, 1.0), 0.0)
    return rows


def circle(x):
    k = jnp.round(x * (2.0 / math.pi))
    r = x - k * 1.5703125
    r = r - k * (math.pi / 2.0 - 1.5703125)
    w = r * r
    s = r + r * w * (-1.6666654611e-1 + w * (8.3321608736e-3 - w * 1.9515295891e-4))
    c = 1.0 - 0.5 * w + w * w * (4.166664568298827e-2 + w * (-1.388731625493765e-3 + w * 2.443315711809948e-5))
    turn = k - 4.0 * jnp.floor(k * 0.25)
    odd = jnp.logical_or(turn == 1.0, turn == 3.0)
    cosine = jnp.where(odd, s, c)
    sine = jnp.where(odd, c, s)
    cosine = jnp.where(jnp.logical_or(turn == 1.0, turn == 2.0), -cosine, cosine)
    sine = jnp.where(turn >= 2.0, -sine, sine)
    return cosine, sine


def line_kernel(
    n,
    q_hbm, k_hbm, v_hbm, qb_hbm, kb_hbm, vb_hbm, order_hbm, tab_hbm,
    o_ref,
    qb_ref, kb_ref, vb_ref, order_ref, tab_ref,
    q_ref, kv, pbuf, ctab, stab, ftab, qs, acc, top, den, ksc, hide, obuf,
    recv, send, precv, psend, qsem, osem, load,
):
    me = lax.axis_index("seq")
    rows = k_hbm.shape[0]
    frames = rows // FRAME_TOK
    half = KVH // 2
    wide = half * HEAD
    qwide = QH * HEAD // 2
    core = me % 2
    y = (me // 2) % 2
    z = me // 4
    sib = me + 1 - 2 * core
    low = z < 2
    end = jnp.logical_or(z == 0, z == 3)
    mid = jnp.logical_not(end)

    def slot(a, b, c):
        return (a * 2 + b) * 2 + c

    def up(i):
        return jnp.where(low, i, 3 - i)

    Z0, Z1, Z2, Z3 = up(0), up(1), up(2), up(3)
    beside = jnp.where(end, Z1, Z0)

    def to(s):
        return dict(device_id={"seq": s}, device_id_type=MESH)

    def part(c, size):
        return pl.ds(pl.multiple_of(c * size, size), size)

    barrier = pltpu.get_barrier_semaphore()

    def greet(i, _):
        pl.semaphore_signal(barrier, inc=1, **to(lax.rem(me + i, n)))
        return 0

    lax.fori_loop(1, n, greet, 0)
    small = [
        pltpu.make_async_copy(src, dst, load.at[i])
        for i, (src, dst) in enumerate((
            (order_hbm, order_ref), (qb_hbm, qb_ref), (kb_hbm, kb_ref), (vb_hbm, vb_ref), (tab_hbm, tab_ref),
        ))
    ]
    mine = [
        pltpu.make_async_copy(k_hbm.at[:, part(core, wide)], kv.at[me], load.at[5]),
        pltpu.make_async_copy(v_hbm.at[:, part(core, wide)], kv.at[n + me], load.at[6]),
        pltpu.make_async_copy(q_hbm.at[:, part(core, qwide)], q_ref.at[0], load.at[7]),
    ]
    for c in small + mine:
        c.start()

    lane = lax.broadcasted_iota(jnp.int32, (1, HEAD), 1)
    group = lane // (HEAD // KVH)

    def row(ref):
        return ref[...].astype(jnp.float32)[None, :]

    def placed(values, at):
        return jnp.where(group == at % KVH, jnp.concatenate([values] * KVH, axis=1), 0.0)

    for c in small:
        c.wait()
    q_row = row(qb_ref)
    pbuf[0, pl.ds(me, 1), :] = q_row[:, :HEAD]
    pbuf[1, pl.ds(me, 1), :] = q_row[:, HEAD:]
    third = placed(row(kb_ref), me) + placed(row(vb_ref), me + 1)
    for f in range(frames):
        third = third + jnp.where(lane == (me + 2) % KVH * (HEAD // KVH) + f, order_ref[f].astype(jnp.float32), 0.0)
    pbuf[2, pl.ds(me, 1), :] = third
    pl.semaphore_wait(barrier, n - 1)

    def own(t, dz, dy, dc):
        return pltpu.make_async_remote_copy(
            src_ref=(k_hbm, v_hbm)[t].at[:, part(dc, wide)],
            dst_ref=kv.at[t * n + me],
            send_sem=send.at[0],
            recv_sem=recv.at[t * n + me],
            **to(slot(dz, dy, dc)),
        )

    def passed(t, s, dz, dy):
        return pltpu.make_async_remote_copy(
            src_ref=kv.at[t * n + s],
            dst_ref=kv.at[t * n + s],
            send_sem=send.at[1],
            recv_sem=recv.at[t * n + s],
            **to(slot(dz, dy, core)),
        )

    sent = {"end": [0, 0], "mid": [0, 0]}

    def own_to(roles, t, dz, dy):
        for dc in (core, 1 - core):
            own(t, dz, dy, dc).start()
        for r in roles:
            sent[r][0] += 2

    def pass_on(role, t, s, dz, dy):
        passed(t, s, dz, dy).start()
        sent[role][1] += 1

    def arrive(t, s):
        passed(t, s, z, y).wait_recv()

    def pack_copy(i, s):
        return pltpu.make_async_remote_copy(
            src_ref=pbuf.at[:, pl.ds(s, 1)],
            dst_ref=pbuf.at[:, pl.ds(s, 1)],
            send_sem=psend,
            recv_sem=precv.at[s],
            **to(lax.rem(me + i, n)),
        )

    def push(i, _):
        pack_copy(i, me).start()
        return 0

    def ways(t):
        own_to(("end", "mid"), t, beside, y)
        own_to(("end", "mid"), t, z, 1 - y)
        pl.when(mid)(lambda: own_to(("mid",), t, Z2, y))

    lax.fori_loop(1, n, push, 0)
    ways(0)
    q_send = pltpu.make_async_remote_copy(
        src_ref=q_hbm.at[:, part(1 - core, qwide)], dst_ref=q_ref.at[1],
        send_sem=qsem.at[0], recv_sem=qsem.at[1], **to(sib),
    )
    q_send.start()
    ways(1)
    for t in (0, 1):
        own(t, z, y, 1 - core).start()
        for r in sent:
            sent[r][0] += 1

    def pulled(i, _):
        pack_copy(i, lax.rem(me + i, n)).wait_recv()
        return 0

    lax.fori_loop(1, n, pulled, 0)
    tab = tab_ref[...]
    third = pbuf[2]
    at = lax.broadcasted_iota(jnp.int32, (n, HEAD), 0)
    spot = lax.broadcasted_iota(jnp.int32, (n, HEAD), 1) - (at + 2) % KVH * (HEAD // KVH)
    for f in range(frames):
        frame = jnp.sum(jnp.where(spot == f, third, 0.0), axis=1, keepdims=True)
        frame = jnp.broadcast_to(frame, (n, HEAD))
        cosine, sine = circle(frame * tab[32:33, :])
        ctab[f] = cosine * tab[33:34, :]
        stab[f] = sine * tab[34:35, :]
        ftab[f] = frame * FRAME_TOK

    def bias_row(g, turn):
        got = jnp.zeros((1, HEAD), jnp.float32)
        for i in range(KVH):
            piece = pbuf[2, pl.ds((core * half + g) * KVH + i, 1), :]
            got = got + jnp.where(group == (i + turn) % KVH, piece, 0.0)
        return got if turn == 0 else pltpu.roll(got, HEAD - turn * (HEAD // KVH), 1)

    k_bias = [bias_row(g, 0) for g in range(half)]
    v_bias = [bias_row(g, 1) for g in range(half)]

    def angles(s):
        cosines = [ctab[f, pl.ds(s, 1), :] + tab[0:16, :] for f in range(frames)]
        sines = [stab[f, pl.ds(s, 1), :] + tab[16:32, :] for f in range(frames)]
        return jnp.concatenate(cosines, axis=0), jnp.concatenate(sines, axis=0)

    fold = math.log2(math.e) / math.sqrt(HEAD)
    qpos = (lane % FRAME_TOK).astype(jnp.float32)
    q_cos, q_sin = [], []
    for k, s in enumerate((me, sib)):
        cosine, sine = angles(s)
        q_cos.append(cosine * fold)
        q_sin.append(sine * fold)
        for f in range(frames):
            qpos = qpos + jnp.where(lane // FRAME_TOK == k * frames + f, ftab[f, pl.ds(s, 1), :], 0.0)
    mine[2].wait()
    q_send.wait_recv()
    for k in range(2):
        for h in range(QH // 2):
            bias = pbuf[h % 2, pl.ds(core * (n // 2) + h // 2, 1), :]
            x = q_ref[k, :, h * HEAD : (h + 1) * HEAD].astype(jnp.float32) + bias
            r = (h % RATIO) * 2 * rows + k * rows
            qs[h // RATIO, r : r + rows, :] = spin(x, q_cos[k], q_sin[k]).astype(jnp.bfloat16)

    within = lax.broadcasted_iota(jnp.int32, (FRAME_TOK, HEAD), 0).astype(jnp.float32)

    def turn_keys(first, count, at):
        for j in range(count):
            s = first + j
            cosine, sine = angles(s)
            for f in range(frames):
                kpos = ftab[f, pl.ds(s, 1), :] + within
                r = at + j * rows + f * FRAME_TOK
                hide[r : r + FRAME_TOK, :] = jnp.where(kpos <= qpos, 0.0, NEG)
            for g in range(half):
                x = kv[s, :, g * HEAD : (g + 1) * HEAD].astype(jnp.float32) + k_bias[g]
                r = at + j * rows
                ksc[g, r : r + rows, :] = spin(x, cosine, sine).astype(jnp.bfloat16)

    block = 2 * HEAD

    def attend(g, first, count, at, fresh):
        keys = slice(at, at + count * rows)
        vals = kv[pl.ds(n + first, count), :, g * HEAD : (g + 1) * HEAD].reshape(count * rows, HEAD)
        mask = hide[keys, :]
        mask = jnp.concatenate([mask] * (block // HEAD), axis=1)
        for b in range(RATIO * 2 * rows // block):
            cols = slice(b * block, (b + 1) * block)
            scores = lax.dot_general(
                ksc[g, keys, :], qs[g, cols, :], (((1,), (1,)), ((), ())), preferred_element_type=jnp.float32
            )
            scores = scores + mask
            new = jnp.max(scores, axis=0, keepdims=True)
            if not fresh:
                old = top[g, :, cols]
                new = jnp.maximum(old, new)
            expo = jnp.exp2(scores - new)
            total = jnp.sum(expo, axis=0, keepdims=True)
            mixed = lax.dot_general(
                vals, expo.astype(jnp.bfloat16), (((0,), (0,)), ((), ())), preferred_element_type=jnp.float32
            )
            top[g, :, cols] = new
            if fresh:
                den[g, :, cols] = total
                acc[g, :, cols] = mixed
            else:
                factor = jnp.exp2(old - new)
                den[g, :, cols] = den[g, :, cols] * factor + total
                acc[g, :, cols] = acc[g, :, cols] * factor + mixed

    def role(cond, name, steps):
        def act():
            for t, s, targets in steps:
                arrive(t, s)
                for dz, dy in targets:
                    pass_on(name, t, s, dz, dy)

        pl.when(cond)(act)

    def both(t, dz, dy, targets):
        return [(t, slot(dz, dy, k), targets) for k in range(2)]

    across = (z, 1 - y)

    def gather(t, dz, dy):
        for k in range(2):
            arrive(t, slot(dz, dy, k))

    role(end, "end", both(0, Z1, y, [across]))
    role(mid, "mid", both(0, Z0, y, [(Z2, y), across]) + both(0, Z2, y, [(Z0, y), across]))
    for c in mine[:2]:
        c.wait()
    for t in (0, 1):
        arrive(t, sib)
    gather(0, z, 1 - y)
    turn_keys(z * 4, 4, 0)
    role(end, "end", both(1, Z1, y, [across]) + both(1, Z0, 1 - y, [(Z1, y), (Z2, y)]))
    role(mid, "mid", both(1, Z0, y, [(Z2, y)]) + both(1, Z2, y, [(Z0, y), across]) + both(1, z, 1 - y, []))
    for g in range(half):
        attend(g, z * 4, 4, 0, True)
    role(end, "end", both(0, Z2, y, [across]))
    role(mid, "mid", both(0, Z3, y, [(Z0, y), across]))
    role(end, "end", both(0, Z1, 1 - y, []))
    role(mid, "mid", both(0, Z2, 1 - y, []))
    second = jnp.where(end, Z1, Z2)
    third_plane = jnp.where(end, Z2, Z0)
    turn_keys(second * 4, 4, 4 * rows)
    role(end, "end", both(1, Z2, y, [across]))
    role(mid, "mid", both(1, Z3, y, [(Z0, y)]))
    role(end, "end", both(1, Z1, 1 - y, []))
    role(mid, "mid", both(1, Z2, 1 - y, []))
    attend(0, second * 4, 4, 4 * rows, False)
    role(end, "end", both(0, Z3, y, [across]))
    attend(1, second * 4, 4, 4 * rows, False)
    role(end, "end", both(0, Z2, 1 - y, []))
    role(mid, "mid", both(0, Z0, 1 - y, []))
    role(mid, "mid", both(1, Z3, 1 - y, [(Z0, y)]))
    turn_keys(third_plane * 4, 4, 8 * rows)
    role(end, "end", both(1, Z2, 1 - y, []))
    role(mid, "mid", both(1, Z0, 1 - y, []))
    for g in range(half):
        attend(g, third_plane * 4, 4, 8 * rows, False)
    gather(0, Z3, 1 - y)
    turn_keys(Z3 * 4, 4, 12 * rows)
    role(end, "end", both(1, Z3, y, []) + both(1, Z3, 1 - y, []))

    out = []
    for g in range(half):
        attend(g, Z3 * 4, 4, 12 * rows, False)
        for r in range(RATIO):
            cols = slice(r * 2 * rows, (r + 1) * 2 * rows)
            mixed = acc[g, :, cols] * (1.0 / den[g, :, cols])
            flat = (mixed.T + v_bias[g]).astype(jnp.bfloat16)
            h = g * RATIO + r
            o_ref[:, pl.ds(pl.multiple_of(core * qwide + h * HEAD, HEAD), HEAD)] = flat[:rows, :]
            obuf[g, :, r * HEAD : (r + 1) * HEAD] = flat[rows:, :]
        c = pltpu.make_async_remote_copy(
            src_ref=obuf.at[g],
            dst_ref=o_ref.at[:, pl.ds(pl.multiple_of(core * qwide + g * RATIO * HEAD, HEAD), RATIO * HEAD)],
            send_sem=osem.at[g], recv_sem=osem.at[half + g], **to(sib),
        )
        c.start()
        out.append(c)

    def drain(name):
        def act():
            for i in range(2):
                size = kv.at[pl.ds(0, sent[name][i])]
                pltpu.make_async_copy(size, size, send.at[i]).wait()

        return act

    pl.when(end)(drain("end"))
    pl.when(mid)(drain("mid"))
    size = pbuf.at[:, pl.ds(0, n - 1)]
    pltpu.make_async_copy(size, size, psend).wait()
    q_send.wait_send()
    for c in out:
        c.wait()


def on_line(n, query, keys, values, query_bias, key_bias, value_projection_bias, frame_order):
    rows = keys.shape[0]
    half = KVH // 2
    frames = rows // FRAME_TOK
    wide = RATIO * 2 * rows
    return pl.pallas_call(
        functools.partial(line_kernel, n),
        out_shape=jax.ShapeDtypeStruct(query.shape, jnp.bfloat16),
        in_specs=[pl.BlockSpec(memory_space=pltpu.HBM)] * 8,
        out_specs=pl.BlockSpec(memory_space=pltpu.VMEM),
        scratch_shapes=[
            pltpu.VMEM(query_bias.shape, jnp.bfloat16),
            pltpu.VMEM(key_bias.shape, jnp.bfloat16),
            pltpu.VMEM(key_bias.shape, jnp.bfloat16),
            pltpu.SMEM(frame_order.shape, jnp.int32),
            pltpu.VMEM((40, HEAD), jnp.float32),
            pltpu.VMEM((2, rows, QH * HEAD // 2), jnp.bfloat16),
            pltpu.VMEM((2 * n, rows, half * HEAD), jnp.bfloat16),
            pltpu.VMEM((3, n, HEAD), jnp.float32),
            pltpu.VMEM((frames, n, HEAD), jnp.float32),
            pltpu.VMEM((frames, n, HEAD), jnp.float32),
            pltpu.VMEM((frames, n, HEAD), jnp.float32),
            pltpu.VMEM((half, wide, HEAD), jnp.bfloat16),
            pltpu.VMEM((half, HEAD, wide), jnp.float32),
            pltpu.VMEM((half, 1, wide), jnp.float32),
            pltpu.VMEM((half, 1, wide), jnp.float32),
            pltpu.VMEM((half, n * rows, HEAD), jnp.bfloat16),
            pltpu.VMEM((n * rows, HEAD), jnp.float32),
            pltpu.VMEM((half, rows, RATIO * HEAD), jnp.bfloat16),
            pltpu.SemaphoreType.DMA((2 * n,)),
            pltpu.SemaphoreType.DMA((2,)),
            pltpu.SemaphoreType.DMA((n,)),
            pltpu.SemaphoreType.DMA,
            pltpu.SemaphoreType.DMA((2,)),
            pltpu.SemaphoreType.DMA((2 * half,)),
            pltpu.SemaphoreType.DMA((8,)),
        ],
        compiler_params=pltpu.CompilerParams(vmem_limit_bytes=24 << 20, collective_id=1, has_side_effects=True),
    )(*(
        pltpu.with_memory_space_constraint(x, pltpu.HBM)
        for x in (
            query, keys, values, query_bias, key_bias, value_projection_bias, frame_order,
            jnp.asarray(line_tables()),
        )
    ))


def on_device(n, query, keys, values, query_bias, key_bias, value_projection_bias, frame_order):
    chips = n // 2
    B = 1
    while B * B * 4 <= chips:
        B *= 2
    A = chips // B
    rows = keys.shape[0]
    qper = query_bias.shape[0]
    wide = RATIO * rows
    keys_at_once = 4 * rows
    whole = pl.BlockSpec(memory_space=pltpu.VMEM)
    far = pl.BlockSpec(memory_space=pltpu.HBM)
    return pl.pallas_call(
        functools.partial(kernel, A, B, n, qper),
        out_shape=jax.ShapeDtypeStruct(query.shape, jnp.bfloat16),
        in_specs=[far] * 8,
        out_specs=whole,
        scratch_shapes=[
            pltpu.VMEM(query_bias.shape, jnp.bfloat16),
            pltpu.VMEM(key_bias.shape, jnp.bfloat16),
            pltpu.VMEM(key_bias.shape, jnp.bfloat16),
            pltpu.SMEM(frame_order.shape, jnp.int32),
            pltpu.VMEM((40, HEAD), jnp.float32),
            pltpu.VMEM(query.shape, jnp.bfloat16),
            pltpu.VMEM((8, HEAD), jnp.float32),
            pltpu.VMEM((n, rows, KVH * HEAD), jnp.bfloat16),
            pltpu.VMEM((n, rows, KVH * HEAD), jnp.bfloat16),
            pltpu.VMEM((n, 8, HEAD), jnp.float32),
            pltpu.VMEM((KVH, wide, HEAD), jnp.bfloat16),
            pltpu.VMEM((KVH, HEAD, wide), jnp.float32),
            pltpu.VMEM((KVH, 1, wide), jnp.float32),
            pltpu.VMEM((KVH, 1, wide), jnp.float32),
            pltpu.VMEM((KVH, keys_at_once, HEAD), jnp.bfloat16),
            pltpu.VMEM((KVH, keys_at_once, HEAD), jnp.bfloat16),
            pltpu.VMEM((keys_at_once, HEAD), jnp.float32),
            pltpu.SemaphoreType.DMA((PIECES, n)),
            pltpu.SemaphoreType.DMA((PIECES, 5, n)),
            pltpu.SemaphoreType.DMA((n,)),
            pltpu.SemaphoreType.DMA((n,)),
            pltpu.SemaphoreType.DMA((8,)),
        ],
        compiler_params=pltpu.CompilerParams(vmem_limit_bytes=(16 if n <= 32 else 48) << 20, collective_id=0, has_side_effects=True),
    )(*(
        pltpu.with_memory_space_constraint(x, pltpu.HBM)
        for x in (
            query, keys, values, query_bias, key_bias, value_projection_bias, frame_order,
            jnp.asarray(tables()),
        )
    ))


def solution(mesh):
    placed = (
        P(("groups", "seq"), None),
        P(("groups", "seq"), None),
        P(("groups", "seq"), None),
        P("seq"),
        P("seq"),
        P("seq"),
        P(("groups", "seq")),
    )
    n = mesh.shape["seq"]
    return jax.shard_map(
        functools.partial(on_line if n == 16 else on_device, n),
        mesh=mesh,
        in_specs=placed,
        out_specs=P(("groups", "seq"), None),
        check_vma=False,
    )
```

```python
import functools
import math

import jax
import jax.numpy as jnp
import numpy as np
from jax import lax
from jax.experimental import pallas as pl
from jax.experimental.pallas import tpu as pltpu
from jax.sharding import PartitionSpec as P

HEAD = 128
HALF = HEAD // 2
QH = 32
KVH = 4
RATIO = QH // KVH
GRID = 4
FRAME_TOK = 16
MESH = pl.DeviceIdType.MESH
NEG = -1e30
PIECES = 2
PAIRS_T = HALF // 4
PAIRS_R = HALF // 4 + 3 * HALF // 8


def tables():
    pair = np.arange(HEAD) % HALF
    freq = np.exp(-(2.0 * pair / HEAD) * math.log(1000000.0))
    tok = np.arange(FRAME_TOK)
    source = np.where(pair[None, :] < PAIRS_R, (tok // GRID)[:, None], (tok % GRID)[:, None])
    angle = source * freq[None, :]
    sign = np.where(np.arange(HEAD) < HALF, -1.0, 1.0)
    rows = np.zeros((40, HEAD), np.float32)
    rows[0:16] = np.cos(angle)
    rows[16:32] = np.sin(angle) * sign[None, :]
    rows[32] = 2.0 * freq
    return rows


def cos_sin(frames, spatial):
    angle = frames * spatial[32:33, :]
    turns = jnp.round(angle * (1.0 / (2.0 * math.pi)))
    angle = angle - turns * 6.28125
    angle = angle - turns * (2.0 * math.pi - 6.28125)
    lane = lax.broadcasted_iota(jnp.int32, (FRAME_TOK, HEAD), 1)
    temporal = lane % HALF < PAIRS_T
    sign = jnp.where(lane < HALF, -1.0, 1.0)
    cos_t, sin_t = jnp.cos(angle), jnp.sin(angle)
    cosines, sines = [], []
    for j in range(frames.shape[0]):
        cosines.append(jnp.where(temporal, cos_t[j : j + 1, :], spatial[0:16, :]))
        sines.append(jnp.where(temporal, sin_t[j : j + 1, :] * sign, spatial[16:32, :]))
    return jnp.concatenate(cosines, axis=0), jnp.concatenate(sines, axis=0)


def spin(x, cosine, sine):
    return x * cosine + pltpu.roll(x, HALF, 1) * sine


def kernel(
    A, B, n, qper,
    q_hbm, k_hbm, v_hbm, qb_hbm, kb_hbm, vb_hbm, order_hbm, tab_hbm,
    o_ref,
    qb_ref, kb_ref, vb_ref, order_ref, tab_ref,
    q_ref, pack_ref, kbuf, vbuf, pbuf, qs, acc, top, den, ksc, vsc, hide,
    recv, send, precv, psend, load,
):
    me = lax.axis_index("seq")
    rows = kbuf.shape[1]
    frames = rows // FRAME_TOK
    cut = rows // (PIECES // 2)
    core = me % 2
    b = (me // 2) % B
    a = me // (2 * B)

    def piece(p, s):
        return (kbuf, vbuf)[p % 2].at[s, pl.ds((p // 2) * cut, cut)]

    def slot(x, y, z):
        return (x * B + y) * 2 + z

    ways = (
        (a + 1 < A, slot(a + 1, b, core)),
        (a > 0, slot(a - 1, b, core)),
        (b + 1 < B, slot(a, b + 1, core)),
        (b > 0, slot(a, b - 1, core)),
        (None, slot(a, b, 1 - core)),
    )

    def copy(t, s, way):
        return pltpu.make_async_remote_copy(
            src_ref=piece(t, s),
            dst_ref=piece(t, s),
            send_sem=send.at[t, way, s],
            recv_sem=recv.at[t, s],
            device_id={"seq": ways[way][1]},
            device_id_type=MESH,
        )

    def when(cond, act):
        if cond is None:
            act()
        else:
            pl.when(cond)(act)

    def fan(t, s, dirs, start):
        for way in dirs:
            c = copy(t, s, way)
            when(ways[way][0], c.start if start else c.wait_send)

    def arrive(t, s):
        copy(t, s, 4).wait_recv()

    def inside(i, size):
        return jnp.logical_and(i >= 0, i < size)

    def along_a(d, start):
        for t in range(PIECES):
            for sg in (1, -1):
                x = a + sg * d

                @pl.when(jnp.logical_and(inside(x, A), d < A))
                def _(x=x, sg=sg, t=t):
                    s = slot(x, b, core)
                    if start:
                        arrive(t, s)
                    fan(t, s, (1 if sg > 0 else 0, 2, 3, 4), start)

    def along_b(d, start):
        for e in range(1, B):
            for t in range(PIECES):
                for sg in (1, -1):
                    x = a + sg * d
                    ok = inside(x, A) if sg > 0 else jnp.logical_and(inside(x, A), d > 0)
                    for sb in (1, -1):
                        y = b + sb * e

                        @pl.when(jnp.logical_and(ok, inside(y, B)))
                        def _(x=x, y=y, sb=sb, t=t):
                            s = slot(x, y, core)
                            if start:
                                arrive(t, s)
                            fan(t, s, (3 if sb > 0 else 2, 4), start)

    barrier = pltpu.get_barrier_semaphore()

    def greet(i, _):
        pl.semaphore_signal(barrier, inc=1, device_id={"seq": lax.rem(me + i, n)}, device_id_type=MESH)
        return 0

    lax.fori_loop(1, n, greet, 0)
    k_load = pltpu.make_async_copy(k_hbm, kbuf.at[me], load.at[0])
    v_load = pltpu.make_async_copy(v_hbm, vbuf.at[me], load.at[1])
    q_load = pltpu.make_async_copy(q_hbm, q_ref, load.at[2])
    small = [
        pltpu.make_async_copy(src, dst, load.at[3 + i])
        for i, (src, dst) in enumerate((
            (order_hbm, order_ref), (qb_hbm, qb_ref), (kb_hbm, kb_ref), (vb_hbm, vb_ref), (tab_hbm, tab_ref),
        ))
    ]
    for c in small + [k_load, v_load, q_load]:
        c.start()

    lane = lax.broadcasted_iota(jnp.int32, (1, HEAD), 1)

    def placed(values):
        size = values.shape[1]
        spots = HEAD // size
        return jnp.where(lane // size == me % spots, jnp.concatenate([values] * spots, axis=1), 0.0)

    def row(ref):
        return ref[...].astype(jnp.float32)[None, :]

    for c in small:
        c.wait()
    pack_ref[...] = jnp.zeros_like(pack_ref)
    q_row = row(qb_ref)
    if qper >= HEAD:
        for i in range(qper // HEAD):
            pack_ref[i : i + 1, :] = q_row[:, i * HEAD : (i + 1) * HEAD]
    else:
        pack_ref[0:1, :] = placed(q_row)
    pack_ref[2:3, :] = placed(row(kb_ref))
    pack_ref[3:4, :] = placed(row(vb_ref))
    qpos = (lane % FRAME_TOK).astype(jnp.float32)
    for f in range(frames):
        frame = order_ref[f].astype(jnp.float32)
        pack_ref[8 - frames + f : 9 - frames + f, :] = jnp.full((1, HEAD), 1.0, jnp.float32) * frame
        qpos = qpos + jnp.where((lane % rows) // FRAME_TOK == f, frame * FRAME_TOK, 0.0)
    pbuf[me] = pack_ref[...]
    tab = tab_ref[...]
    q_cos, q_sin = cos_sin(pack_ref[8 - frames :, :], tab)
    fold = math.log2(math.e) / math.sqrt(HEAD)
    q_cos, q_sin = q_cos * fold, q_sin * fold
    k_load.wait()
    v_load.wait()
    pl.semaphore_wait(barrier, n - 1)

    def pack_copy(i, s):
        return pltpu.make_async_remote_copy(
            src_ref=pack_ref,
            dst_ref=pbuf.at[s],
            send_sem=psend.at[i],
            recv_sem=precv.at[s],
            device_id={"seq": lax.rem(me + i, n)},
            device_id_type=MESH,
        )

    def push(i, _):
        pack_copy(i, me).start()
        return 0

    lax.fori_loop(1, n, push, 0)
    for t in range(PIECES):
        fan(t, me, (0, 1, 2, 3, 4), True)

    acc[...] = jnp.zeros_like(acc)
    den[...] = jnp.zeros_like(den)
    top[...] = jnp.full_like(top, NEG)

    def pulled(i, _):
        pack_copy(i, lax.rem(me + i, n)).wait_recv()
        return 0

    lax.fori_loop(1, n, pulled, 0)
    q_load.wait()

    for h in range(QH):
        if qper >= HEAD:
            per = qper // HEAD
            bias = pbuf[h // per, h % per : h % per + 1, :]
        else:
            parts = HEAD // qper
            bias = sum(pbuf[h * parts + i, 0:1, :] for i in range(parts))
        x = q_ref[:, h * HEAD : (h + 1) * HEAD].astype(jnp.float32) + bias
        at = (h % RATIO) * rows
        qs[h // RATIO, at : at + rows, :] = spin(x, q_cos, q_sin).astype(jnp.bfloat16)
    share = n // KVH
    k_bias = [sum(pbuf[g * share + i, 2:3, :] for i in range(share)) for g in range(KVH)]
    v_bias = [sum(pbuf[g * share + i, 3:4, :] for i in range(share)) for g in range(KVH)]
    within = lax.broadcasted_iota(jnp.int32, (FRAME_TOK, HEAD), 0).astype(jnp.float32)

    def chunk(first):
        for j in range(4):
            s = first + j
            order = pbuf[s][8 - frames :, :]
            cosine, sine = cos_sin(order, tab)
            for f in range(frames):
                kpos = order[f : f + 1, :] * FRAME_TOK + within
                at = j * rows + f * FRAME_TOK
                hide[at : at + FRAME_TOK, :] = jnp.where(kpos <= qpos, 0.0, NEG)
            for g in range(KVH):
                cols = slice(g * HEAD, (g + 1) * HEAD)
                x = kbuf[s, :, cols].astype(jnp.float32) + k_bias[g]
                ksc[g, j * rows : (j + 1) * rows, :] = spin(x, cosine, sine).astype(jnp.bfloat16)
                y = vbuf[s, :, cols].astype(jnp.float32) + v_bias[g]
                vsc[g, j * rows : (j + 1) * rows, :] = y.astype(jnp.bfloat16)
        for g in range(KVH):
            scores = lax.dot_general(
                ksc[g], qs[g], (((1,), (1,)), ((), ())), preferred_element_type=jnp.float32
            )
            mask = hide[...]
            scores = scores + jnp.concatenate([mask] * (scores.shape[1] // HEAD), axis=1)
            old = top[g]
            new = jnp.maximum(old, jnp.max(scores, axis=0, keepdims=True))
            expo = jnp.exp2(scores - new)
            factor = jnp.exp2(old - new)
            top[g] = new
            den[g] = den[g] * factor + jnp.sum(expo, axis=0, keepdims=True)
            acc[g] = acc[g] * factor + lax.dot_general(
                vsc[g], expo.astype(jnp.bfloat16), (((0,), (0,)), ((), ())),
                preferred_element_type=jnp.float32,
            )

    low = a < A // 2
    mirror = jnp.where(low, a, A - 1 - a)

    def step(d, _):
        along_a(d + 1, True)
        along_b(d, True)
        near = jnp.where(d % 2 == 1, -((d + 1) // 2), d // 2)
        plane = mirror + jnp.where(d <= 2 * mirror, near, d - mirror)
        plane = jnp.where(low, plane, A - 1 - plane)
        for y in range(B):
            for t in range(PIECES):
                arrive(t, slot(plane, y, 1 - core))
        if 2 * B == 4:
            chunk(plane * 4)
        else:
            def part(i, _):
                chunk(plane * 2 * B + i * 4)
                return 0

            lax.fori_loop(0, 2 * B // 4, part, 0)
        return 0

    lax.fori_loop(0, A, step, 0)

    for g in range(KVH):
        mixed = acc[g] * (1.0 / den[g])
        flat = mixed.T.astype(jnp.bfloat16)
        for r in range(RATIO):
            h = g * RATIO + r
            o_ref[:, h * HEAD : (h + 1) * HEAD] = flat[r * rows : (r + 1) * rows, :]

    for t in range(PIECES):
        fan(t, me, (0, 1, 2, 3, 4), False)

    def drain(d, _):
        along_a(d + 1, False)
        along_b(d, False)
        return 0

    lax.fori_loop(0, A, drain, 0)

    def pushed(i, _):
        pack_copy(i, me).wait_send()
        return 0

    lax.fori_loop(1, n, pushed, 0)


def line_tables():
    rows = tables()
    pair = np.arange(HEAD) % HALF
    temporal = pair < PAIRS_T
    rows[0:32, temporal] = 0.0
    rows[32] = np.where(temporal, rows[32], 0.0)
    rows[33] = np.where(temporal, 1.0, 0.0)
    rows[34] = np.where(temporal, np.where(np.arange(HEAD) < HALF, -1.0, 1.0), 0.0)
    return rows


def circle(x):
    k = jnp.round(x * (2.0 / math.pi))
    r = x - k * 1.5703125
    r = r - k * (math.pi / 2.0 - 1.5703125)
    w = r * r
    s = r + r * w * (-1.6666654611e-1 + w * (8.3321608736e-3 - w * 1.9515295891e-4))
    c = 1.0 - 0.5 * w + w * w * (4.166664568298827e-2 + w * (-1.388731625493765e-3 + w * 2.443315711809948e-5))
    turn = k - 4.0 * jnp.floor(k * 0.25)
    odd = jnp.logical_or(turn == 1.0, turn == 3.0)
    cosine = jnp.where(odd, s, c)
    sine = jnp.where(odd, c, s)
    cosine = jnp.where(jnp.logical_or(turn == 1.0, turn == 2.0), -cosine, cosine)
    sine = jnp.where(turn >= 2.0, -sine, sine)
    return cosine, sine


def line_kernel(
    n,
    q_hbm, k_hbm, v_hbm, qb_hbm, kb_hbm, vb_hbm, order_hbm, tab_hbm,
    o_ref,
    qb_ref, kb_ref, vb_ref, order_ref, tab_ref,
    q_ref, kv, pbuf, ctab, stab, ftab, qs, acc, top, den, ksc, hide, obuf,
    recv, send, precv, psend, qsem, osem, load,
):
    me = lax.axis_index("seq")
    rows = k_hbm.shape[0]
    frames = rows // FRAME_TOK
    half = KVH // 2
    wide = half * HEAD
    qwide = QH * HEAD // 2
    core = me % 2
    y = (me // 2) % 2
    z = me // 4
    sib = me + 1 - 2 * core
    low = z < 2
    end = jnp.logical_or(z == 0, z == 3)
    mid = jnp.logical_not(end)

    def slot(a, b, c):
        return (a * 2 + b) * 2 + c

    def up(i):
        return jnp.where(low, i, 3 - i)

    Z0, Z1, Z2, Z3 = up(0), up(1), up(2), up(3)
    beside = jnp.where(end, Z1, Z0)

    def to(s):
        return dict(device_id={"seq": s}, device_id_type=MESH)

    def part(c, size):
        return pl.ds(pl.multiple_of(c * size, size), size)

    barrier = pltpu.get_barrier_semaphore()

    def greet(i, _):
        pl.semaphore_signal(barrier, inc=1, **to(lax.rem(me + i, n)))
        return 0

    lax.fori_loop(1, n, greet, 0)
    small = [
        pltpu.make_async_copy(src, dst, load.at[i])
        for i, (src, dst) in enumerate((
            (order_hbm, order_ref), (qb_hbm, qb_ref), (kb_hbm, kb_ref), (vb_hbm, vb_ref), (tab_hbm, tab_ref),
        ))
    ]
    mine = [
        pltpu.make_async_copy(k_hbm.at[:, part(core, wide)], kv.at[me], load.at[5]),
        pltpu.make_async_copy(v_hbm.at[:, part(core, wide)], kv.at[n + me], load.at[6]),
        pltpu.make_async_copy(q_hbm.at[:, part(core, qwide)], q_ref.at[0], load.at[7]),
    ]
    for c in small + mine:
        c.start()

    lane = lax.broadcasted_iota(jnp.int32, (1, HEAD), 1)
    group = lane // (HEAD // KVH)

    def row(ref):
        return ref[...].astype(jnp.float32)[None, :]

    def placed(values, at):
        return jnp.where(group == at % KVH, jnp.concatenate([values] * KVH, axis=1), 0.0)

    for c in small:
        c.wait()
    q_row = row(qb_ref)
    pbuf[0, pl.ds(me, 1), :] = q_row[:, :HEAD]
    pbuf[1, pl.ds(me, 1), :] = q_row[:, HEAD:]
    third = placed(row(kb_ref), me) + placed(row(vb_ref), me + 1)
    for f in range(frames):
        third = third + jnp.where(lane == (me + 2) % KVH * (HEAD // KVH) + f, order_ref[f].astype(jnp.float32), 0.0)
    pbuf[2, pl.ds(me, 1), :] = third
    pl.semaphore_wait(barrier, n - 1)

    def own(t, dz, dy, dc):
        return pltpu.make_async_remote_copy(
            src_ref=(k_hbm, v_hbm)[t].at[:, part(dc, wide)],
            dst_ref=kv.at[t * n + me],
            send_sem=send.at[0],
            recv_sem=recv.at[t * n + me],
            **to(slot(dz, dy, dc)),
        )

    def passed(t, s, dz, dy):
        return pltpu.make_async_remote_copy(
            src_ref=kv.at[t * n + s],
            dst_ref=kv.at[t * n + s],
            send_sem=send.at[1],
            recv_sem=recv.at[t * n + s],
            **to(slot(dz, dy, core)),
        )

    sent = {"end": [0, 0], "mid": [0, 0]}

    def own_to(roles, t, dz, dy):
        for dc in (core, 1 - core):
            own(t, dz, dy, dc).start()
        for r in roles:
            sent[r][0] += 2

    def pass_on(role, t, s, dz, dy):
        passed(t, s, dz, dy).start()
        sent[role][1] += 1

    def arrive(t, s):
        passed(t, s, z, y).wait_recv()

    def pack_copy(i, s):
        return pltpu.make_async_remote_copy(
            src_ref=pbuf.at[:, pl.ds(s, 1)],
            dst_ref=pbuf.at[:, pl.ds(s, 1)],
            send_sem=psend,
            recv_sem=precv.at[s],
            **to(lax.rem(me + i, n)),
        )

    def push(i, _):
        pack_copy(i, me).start()
        return 0

    def ways(t):
        own_to(("end", "mid"), t, beside, y)
        own_to(("end", "mid"), t, z, 1 - y)
        pl.when(mid)(lambda: own_to(("mid",), t, Z2, y))

    lax.fori_loop(1, n, push, 0)
    ways(0)
    q_send = pltpu.make_async_remote_copy(
        src_ref=q_hbm.at[:, part(1 - core, qwide)], dst_ref=q_ref.at[1],
        send_sem=qsem.at[0], recv_sem=qsem.at[1], **to(sib),
    )
    q_send.start()
    ways(1)
    for t in (0, 1):
        own(t, z, y, 1 - core).start()
        for r in sent:
            sent[r][0] += 1

    def pulled(i, _):
        pack_copy(i, lax.rem(me + i, n)).wait_recv()
        return 0

    lax.fori_loop(1, n, pulled, 0)
    tab = tab_ref[...]
    third = pbuf[2]
    at = lax.broadcasted_iota(jnp.int32, (n, HEAD), 0)
    spot = lax.broadcasted_iota(jnp.int32, (n, HEAD), 1) - (at + 2) % KVH * (HEAD // KVH)
    for f in range(frames):
        frame = jnp.sum(jnp.where(spot == f, third, 0.0), axis=1, keepdims=True)
        frame = jnp.broadcast_to(frame, (n, HEAD))
        cosine, sine = circle(frame * tab[32:33, :])
        ctab[f] = cosine * tab[33:34, :]
        stab[f] = sine * tab[34:35, :]
        ftab[f] = frame * FRAME_TOK

    def bias_row(g, turn):
        got = jnp.zeros((1, HEAD), jnp.float32)
        for i in range(KVH):
            piece = pbuf[2, pl.ds((core * half + g) * KVH + i, 1), :]
            got = got + jnp.where(group == (i + turn) % KVH, piece, 0.0)
        return got if turn == 0 else pltpu.roll(got, HEAD - turn * (HEAD // KVH), 1)

    k_bias = [bias_row(g, 0) for g in range(half)]
    v_bias = [bias_row(g, 1) for g in range(half)]

    def angles(s):
        cosines = [ctab[f, pl.ds(s, 1), :] + tab[0:16, :] for f in range(frames)]
        sines = [stab[f, pl.ds(s, 1), :] + tab[16:32, :] for f in range(frames)]
        return jnp.concatenate(cosines, axis=0), jnp.concatenate(sines, axis=0)

    fold = math.log2(math.e) / math.sqrt(HEAD)
    qpos = (lane % FRAME_TOK).astype(jnp.float32)
    q_cos, q_sin = [], []
    for k, s in enumerate((me, sib)):
        cosine, sine = angles(s)
        q_cos.append(cosine * fold)
        q_sin.append(sine * fold)
        for f in range(frames):
            qpos = qpos + jnp.where(lane // FRAME_TOK == k * frames + f, ftab[f, pl.ds(s, 1), :], 0.0)
    mine[2].wait()
    q_send.wait_recv()
    for k in range(2):
        for h in range(QH // 2):
            bias = pbuf[h % 2, pl.ds(core * (n // 2) + h // 2, 1), :]
            x = q_ref[k, :, h * HEAD : (h + 1) * HEAD].astype(jnp.float32) + bias
            r = (h % RATIO) * 2 * rows + k * rows
            qs[h // RATIO, r : r + rows, :] = spin(x, q_cos[k], q_sin[k]).astype(jnp.bfloat16)

    within = lax.broadcasted_iota(jnp.int32, (FRAME_TOK, HEAD), 0).astype(jnp.float32)

    def turn_keys(first, count, at):
        for j in range(count):
            s = first + j
            cosine, sine = angles(s)
            for f in range(frames):
                kpos = ftab[f, pl.ds(s, 1), :] + within
                r = at + j * rows + f * FRAME_TOK
                hide[r : r + FRAME_TOK, :] = jnp.where(kpos <= qpos, 0.0, NEG)
            for g in range(half):
                x = kv[s, :, g * HEAD : (g + 1) * HEAD].astype(jnp.float32) + k_bias[g]
                r = at + j * rows
                ksc[g, r : r + rows, :] = spin(x, cosine, sine).astype(jnp.bfloat16)

    block = HEAD

    def attend(g, first, count, at, fresh):
        keys = slice(at, at + count * rows)
        vals = kv[pl.ds(n + first, count), :, g * HEAD : (g + 1) * HEAD].reshape(count * rows, HEAD)
        mask = hide[keys, :]
        mask = jnp.concatenate([mask] * (block // HEAD), axis=1)
        for b in range(RATIO * 2 * rows // block):
            cols = slice(b * block, (b + 1) * block)
            scores = lax.dot_general(
                ksc[g, keys, :], qs[g, cols, :], (((1,), (1,)), ((), ())), preferred_element_type=jnp.float32
            )
            scores = scores + mask
            new = jnp.max(scores, axis=0, keepdims=True)
            if not fresh:
                old = top[g, :, cols]
                new = jnp.maximum(old, new)
            expo = jnp.exp2(scores - new)
            total = jnp.sum(expo, axis=0, keepdims=True)
            mixed = lax.dot_general(
                vals, expo.astype(jnp.bfloat16), (((0,), (0,)), ((), ())), preferred_element_type=jnp.float32
            )
            top[g, :, cols] = new
            if fresh:
                den[g, :, cols] = total
                acc[g, :, cols] = mixed
            else:
                factor = jnp.exp2(old - new)
                den[g, :, cols] = den[g, :, cols] * factor + total
                acc[g, :, cols] = acc[g, :, cols] * factor + mixed

    def role(cond, name, steps):
        def act():
            for t, s, targets in steps:
                arrive(t, s)
                for dz, dy in targets:
                    pass_on(name, t, s, dz, dy)

        pl.when(cond)(act)

    def both(t, dz, dy, targets):
        return [(t, slot(dz, dy, k), targets) for k in range(2)]

    across = (z, 1 - y)

    def gather(t, dz, dy):
        for k in range(2):
            arrive(t, slot(dz, dy, k))

    role(end, "end", both(0, Z1, y, [across]))
    role(mid, "mid", both(0, Z0, y, [(Z2, y), across]) + both(0, Z2, y, [(Z0, y), across]))
    for c in mine[:2]:
        c.wait()
    for t in (0, 1):
        arrive(t, sib)
    gather(0, z, 1 - y)
    turn_keys(z * 4, 4, 0)
    role(end, "end", both(1, Z1, y, [across]) + both(1, Z0, 1 - y, [(Z1, y), (Z2, y)]))
    role(mid, "mid", both(1, Z0, y, [(Z2, y)]) + both(1, Z2, y, [(Z0, y), across]) + both(1, z, 1 - y, []))
    for g in range(half):
        attend(g, z * 4, 4, 0, True)
    role(end, "end", both(0, Z2, y, [across]))
    role(mid, "mid", both(0, Z3, y, [(Z0, y), across]))
    role(end, "end", both(0, Z1, 1 - y, []))
    role(mid, "mid", both(0, Z2, 1 - y, []))
    second = jnp.where(end, Z1, Z2)
    third_plane = jnp.where(end, Z2, Z0)
    turn_keys(second * 4, 4, 4 * rows)
    role(end, "end", both(1, Z2, y, [across]))
    role(mid, "mid", both(1, Z3, y, [(Z0, y)]))
    role(end, "end", both(1, Z1, 1 - y, []))
    role(mid, "mid", both(1, Z2, 1 - y, []))
    attend(0, second * 4, 4, 4 * rows, False)
    role(end, "end", both(0, Z3, y, [across]))
    attend(1, second * 4, 4, 4 * rows, False)
    role(end, "end", both(0, Z2, 1 - y, []))
    role(mid, "mid", both(0, Z0, 1 - y, []))
    role(mid, "mid", both(1, Z3, 1 - y, [(Z0, y)]))
    turn_keys(third_plane * 4, 4, 8 * rows)
    role(end, "end", both(1, Z2, 1 - y, []))
    role(mid, "mid", both(1, Z0, 1 - y, []))
    for g in range(half):
        attend(g, third_plane * 4, 4, 8 * rows, False)
    gather(0, Z3, 1 - y)
    turn_keys(Z3 * 4, 4, 12 * rows)
    role(end, "end", both(1, Z3, y, []) + both(1, Z3, 1 - y, []))

    out = []
    for g in range(half):
        attend(g, Z3 * 4, 4, 12 * rows, False)
        for r in range(RATIO):
            cols = slice(r * 2 * rows, (r + 1) * 2 * rows)
            mixed = acc[g, :, cols] * (1.0 / den[g, :, cols])
            flat = (mixed.T + v_bias[g]).astype(jnp.bfloat16)
            h = g * RATIO + r
            o_ref[:, pl.ds(pl.multiple_of(core * qwide + h * HEAD, HEAD), HEAD)] = flat[:rows, :]
            obuf[g, :, r * HEAD : (r + 1) * HEAD] = flat[rows:, :]
        c = pltpu.make_async_remote_copy(
            src_ref=obuf.at[g],
            dst_ref=o_ref.at[:, pl.ds(pl.multiple_of(core * qwide + g * RATIO * HEAD, HEAD), RATIO * HEAD)],
            send_sem=osem.at[g], recv_sem=osem.at[half + g], **to(sib),
        )
        c.start()
        out.append(c)

    def drain(name):
        def act():
            for i in range(2):
                size = kv.at[pl.ds(0, sent[name][i])]
                pltpu.make_async_copy(size, size, send.at[i]).wait()

        return act

    pl.when(end)(drain("end"))
    pl.when(mid)(drain("mid"))
    size = pbuf.at[:, pl.ds(0, n - 1)]
    pltpu.make_async_copy(size, size, psend).wait()
    q_send.wait_send()
    for c in out:
        c.wait()


def on_line(n, query, keys, values, query_bias, key_bias, value_projection_bias, frame_order):
    rows = keys.shape[0]
    half = KVH // 2
    frames = rows // FRAME_TOK
    wide = RATIO * 2 * rows
    return pl.pallas_call(
        functools.partial(line_kernel, n),
        out_shape=jax.ShapeDtypeStruct(query.shape, jnp.bfloat16),
        in_specs=[pl.BlockSpec(memory_space=pltpu.HBM)] * 8,
        out_specs=pl.BlockSpec(memory_space=pltpu.VMEM),
        scratch_shapes=[
            pltpu.VMEM(query_bias.shape, jnp.bfloat16),
            pltpu.VMEM(key_bias.shape, jnp.bfloat16),
            pltpu.VMEM(key_bias.shape, jnp.bfloat16),
            pltpu.SMEM(frame_order.shape, jnp.int32),
            pltpu.VMEM((40, HEAD), jnp.float32),
            pltpu.VMEM((2, rows, QH * HEAD // 2), jnp.bfloat16),
            pltpu.VMEM((2 * n, rows, half * HEAD), jnp.bfloat16),
            pltpu.VMEM((3, n, HEAD), jnp.float32),
            pltpu.VMEM((frames, n, HEAD), jnp.float32),
            pltpu.VMEM((frames, n, HEAD), jnp.float32),
            pltpu.VMEM((frames, n, HEAD), jnp.float32),
            pltpu.VMEM((half, wide, HEAD), jnp.bfloat16),
            pltpu.VMEM((half, HEAD, wide), jnp.float32),
            pltpu.VMEM((half, 1, wide), jnp.float32),
            pltpu.VMEM((half, 1, wide), jnp.float32),
            pltpu.VMEM((half, n * rows, HEAD), jnp.bfloat16),
            pltpu.VMEM((n * rows, HEAD), jnp.float32),
            pltpu.VMEM((half, rows, RATIO * HEAD), jnp.bfloat16),
            pltpu.SemaphoreType.DMA((2 * n,)),
            pltpu.SemaphoreType.DMA((2,)),
            pltpu.SemaphoreType.DMA((n,)),
            pltpu.SemaphoreType.DMA,
            pltpu.SemaphoreType.DMA((2,)),
            pltpu.SemaphoreType.DMA((2 * half,)),
            pltpu.SemaphoreType.DMA((8,)),
        ],
        compiler_params=pltpu.CompilerParams(vmem_limit_bytes=24 << 20, collective_id=1, has_side_effects=True),
    )(*(
        pltpu.with_memory_space_constraint(x, pltpu.HBM)
        for x in (
            query, keys, values, query_bias, key_bias, value_projection_bias, frame_order,
            jnp.asarray(line_tables()),
        )
    ))


def on_device(n, query, keys, values, query_bias, key_bias, value_projection_bias, frame_order):
    chips = n // 2
    B = 1
    while B * B * 4 <= chips:
        B *= 2
    A = chips // B
    rows = keys.shape[0]
    qper = query_bias.shape[0]
    wide = RATIO * rows
    keys_at_once = 4 * rows
    whole = pl.BlockSpec(memory_space=pltpu.VMEM)
    far = pl.BlockSpec(memory_space=pltpu.HBM)
    return pl.pallas_call(
        functools.partial(kernel, A, B, n, qper),
        out_shape=jax.ShapeDtypeStruct(query.shape, jnp.bfloat16),
        in_specs=[far] * 8,
        out_specs=whole,
        scratch_shapes=[
            pltpu.VMEM(query_bias.shape, jnp.bfloat16),
            pltpu.VMEM(key_bias.shape, jnp.bfloat16),
            pltpu.VMEM(key_bias.shape, jnp.bfloat16),
            pltpu.SMEM(frame_order.shape, jnp.int32),
            pltpu.VMEM((40, HEAD), jnp.float32),
            pltpu.VMEM(query.shape, jnp.bfloat16),
            pltpu.VMEM((8, HEAD), jnp.float32),
            pltpu.VMEM((n, rows, KVH * HEAD), jnp.bfloat16),
            pltpu.VMEM((n, rows, KVH * HEAD), jnp.bfloat16),
            pltpu.VMEM((n, 8, HEAD), jnp.float32),
            pltpu.VMEM((KVH, wide, HEAD), jnp.bfloat16),
            pltpu.VMEM((KVH, HEAD, wide), jnp.float32),
            pltpu.VMEM((KVH, 1, wide), jnp.float32),
            pltpu.VMEM((KVH, 1, wide), jnp.float32),
            pltpu.VMEM((KVH, keys_at_once, HEAD), jnp.bfloat16),
            pltpu.VMEM((KVH, keys_at_once, HEAD), jnp.bfloat16),
            pltpu.VMEM((keys_at_once, HEAD), jnp.float32),
            pltpu.SemaphoreType.DMA((PIECES, n)),
            pltpu.SemaphoreType.DMA((PIECES, 5, n)),
            pltpu.SemaphoreType.DMA((n,)),
            pltpu.SemaphoreType.DMA((n,)),
            pltpu.SemaphoreType.DMA((8,)),
        ],
        compiler_params=pltpu.CompilerParams(vmem_limit_bytes=(16 if n <= 32 else 48) << 20, collective_id=0, has_side_effects=True),
    )(*(
        pltpu.with_memory_space_constraint(x, pltpu.HBM)
        for x in (
            query, keys, values, query_bias, key_bias, value_projection_bias, frame_order,
            jnp.asarray(tables()),
        )
    ))


def solution(mesh):
    placed = (
        P(("groups", "seq"), None),
        P(("groups", "seq"), None),
        P(("groups", "seq"), None),
        P("seq"),
        P("seq"),
        P("seq"),
        P(("groups", "seq")),
    )
    n = mesh.shape["seq"]
    return jax.shard_map(
        functools.partial(on_line if n == 16 else on_device, n),
        mesh=mesh,
        in_specs=placed,
        out_specs=P(("groups", "seq"), None),
        check_vma=False,
    )
```

```python
import functools
import math

import jax
import jax.numpy as jnp
import numpy as np
from jax import lax
from jax.experimental import pallas as pl
from jax.experimental.pallas import tpu as pltpu
from jax.sharding import PartitionSpec as P

HEAD = 128
HALF = HEAD // 2
QH = 32
KVH = 4
RATIO = QH // KVH
GRID = 4
FRAME_TOK = 16
MESH = pl.DeviceIdType.MESH
NEG = -1e30
PIECES = 2
PAIRS_T = HALF // 4
PAIRS_R = HALF // 4 + 3 * HALF // 8


def tables():
    pair = np.arange(HEAD) % HALF
    freq = np.exp(-(2.0 * pair / HEAD) * math.log(1000000.0))
    tok = np.arange(FRAME_TOK)
    source = np.where(pair[None, :] < PAIRS_R, (tok // GRID)[:, None], (tok % GRID)[:, None])
    angle = source * freq[None, :]
    sign = np.where(np.arange(HEAD) < HALF, -1.0, 1.0)
    rows = np.zeros((40, HEAD), np.float32)
    rows[0:16] = np.cos(angle)
    rows[16:32] = np.sin(angle) * sign[None, :]
    rows[32] = 2.0 * freq
    return rows


def cos_sin(frames, spatial):
    angle = frames * spatial[32:33, :]
    turns = jnp.round(angle * (1.0 / (2.0 * math.pi)))
    angle = angle - turns * 6.28125
    angle = angle - turns * (2.0 * math.pi - 6.28125)
    lane = lax.broadcasted_iota(jnp.int32, (FRAME_TOK, HEAD), 1)
    temporal = lane % HALF < PAIRS_T
    sign = jnp.where(lane < HALF, -1.0, 1.0)
    cos_t, sin_t = jnp.cos(angle), jnp.sin(angle)
    cosines, sines = [], []
    for j in range(frames.shape[0]):
        cosines.append(jnp.where(temporal, cos_t[j : j + 1, :], spatial[0:16, :]))
        sines.append(jnp.where(temporal, sin_t[j : j + 1, :] * sign, spatial[16:32, :]))
    return jnp.concatenate(cosines, axis=0), jnp.concatenate(sines, axis=0)


def spin(x, cosine, sine):
    return x * cosine + pltpu.roll(x, HALF, 1) * sine


def kernel(
    A, B, n, qper,
    q_hbm, k_hbm, v_hbm, qb_hbm, kb_hbm, vb_hbm, order_hbm, tab_hbm,
    o_ref,
    qb_ref, kb_ref, vb_ref, order_ref, tab_ref,
    q_ref, pack_ref, kbuf, vbuf, pbuf, qs, acc, top, den, ksc, vsc, hide,
    recv, send, precv, psend, load,
):
    me = lax.axis_index("seq")
    rows = kbuf.shape[1]
    frames = rows // FRAME_TOK
    cut = rows // (PIECES // 2)
    core = me % 2
    b = (me // 2) % B
    a = me // (2 * B)

    def piece(p, s):
        return (kbuf, vbuf)[p % 2].at[s, pl.ds((p // 2) * cut, cut)]

    def slot(x, y, z):
        return (x * B + y) * 2 + z

    ways = (
        (a + 1 < A, slot(a + 1, b, core)),
        (a > 0, slot(a - 1, b, core)),
        (b + 1 < B, slot(a, b + 1, core)),
        (b > 0, slot(a, b - 1, core)),
        (None, slot(a, b, 1 - core)),
    )

    def copy(t, s, way):
        return pltpu.make_async_remote_copy(
            src_ref=piece(t, s),
            dst_ref=piece(t, s),
            send_sem=send.at[t, way, s],
            recv_sem=recv.at[t, s],
            device_id={"seq": ways[way][1]},
            device_id_type=MESH,
        )

    def when(cond, act):
        if cond is None:
            act()
        else:
            pl.when(cond)(act)

    def fan(t, s, dirs, start):
        for way in dirs:
            c = copy(t, s, way)
            when(ways[way][0], c.start if start else c.wait_send)

    def arrive(t, s):
        copy(t, s, 4).wait_recv()

    def inside(i, size):
        return jnp.logical_and(i >= 0, i < size)

    def along_a(d, start):
        for t in range(PIECES):
            for sg in (1, -1):
                x = a + sg * d

                @pl.when(jnp.logical_and(inside(x, A), d < A))
                def _(x=x, sg=sg, t=t):
                    s = slot(x, b, core)
                    if start:
                        arrive(t, s)
                    fan(t, s, (1 if sg > 0 else 0, 2, 3, 4), start)

    def along_b(d, start):
        for e in range(1, B):
            for t in range(PIECES):
                for sg in (1, -1):
                    x = a + sg * d
                    ok = inside(x, A) if sg > 0 else jnp.logical_and(inside(x, A), d > 0)
                    for sb in (1, -1):
                        y = b + sb * e

                        @pl.when(jnp.logical_and(ok, inside(y, B)))
                        def _(x=x, y=y, sb=sb, t=t):
                            s = slot(x, y, core)
                            if start:
                                arrive(t, s)
                            fan(t, s, (3 if sb > 0 else 2, 4), start)

    barrier = pltpu.get_barrier_semaphore()

    def greet(i, _):
        pl.semaphore_signal(barrier, inc=1, device_id={"seq": lax.rem(me + i, n)}, device_id_type=MESH)
        return 0

    lax.fori_loop(1, n, greet, 0)
    k_load = pltpu.make_async_copy(k_hbm, kbuf.at[me], load.at[0])
    v_load = pltpu.make_async_copy(v_hbm, vbuf.at[me], load.at[1])
    q_load = pltpu.make_async_copy(q_hbm, q_ref, load.at[2])
    small = [
        pltpu.make_async_copy(src, dst, load.at[3 + i])
        for i, (src, dst) in enumerate((
            (order_hbm, order_ref), (qb_hbm, qb_ref), (kb_hbm, kb_ref), (vb_hbm, vb_ref), (tab_hbm, tab_ref),
        ))
    ]
    for c in small + [k_load, v_load, q_load]:
        c.start()

    lane = lax.broadcasted_iota(jnp.int32, (1, HEAD), 1)

    def placed(values):
        size = values.shape[1]
        spots = HEAD // size
        return jnp.where(lane // size == me % spots, jnp.concatenate([values] * spots, axis=1), 0.0)

    def row(ref):
        return ref[...].astype(jnp.float32)[None, :]

    for c in small:
        c.wait()
    pack_ref[...] = jnp.zeros_like(pack_ref)
    q_row = row(qb_ref)
    if qper >= HEAD:
        for i in range(qper // HEAD):
            pack_ref[i : i + 1, :] = q_row[:, i * HEAD : (i + 1) * HEAD]
    else:
        pack_ref[0:1, :] = placed(q_row)
    pack_ref[2:3, :] = placed(row(kb_ref))
    pack_ref[3:4, :] = placed(row(vb_ref))
    qpos = (lane % FRAME_TOK).astype(jnp.float32)
    for f in range(frames):
        frame = order_ref[f].astype(jnp.float32)
        pack_ref[8 - frames + f : 9 - frames + f, :] = jnp.full((1, HEAD), 1.0, jnp.float32) * frame
        qpos = qpos + jnp.where((lane % rows) // FRAME_TOK == f, frame * FRAME_TOK, 0.0)
    pbuf[me] = pack_ref[...]
    tab = tab_ref[...]
    q_cos, q_sin = cos_sin(pack_ref[8 - frames :, :], tab)
    fold = math.log2(math.e) / math.sqrt(HEAD)
    q_cos, q_sin = q_cos * fold, q_sin * fold
    k_load.wait()
    v_load.wait()
    pl.semaphore_wait(barrier, n - 1)

    def pack_copy(i, s):
        return pltpu.make_async_remote_copy(
            src_ref=pack_ref,
            dst_ref=pbuf.at[s],
            send_sem=psend.at[i],
            recv_sem=precv.at[s],
            device_id={"seq": lax.rem(me + i, n)},
            device_id_type=MESH,
        )

    def push(i, _):
        pack_copy(i, me).start()
        return 0

    lax.fori_loop(1, n, push, 0)
    for t in range(PIECES):
        fan(t, me, (0, 1, 2, 3, 4), True)

    acc[...] = jnp.zeros_like(acc)
    den[...] = jnp.zeros_like(den)
    top[...] = jnp.full_like(top, NEG)

    def pulled(i, _):
        pack_copy(i, lax.rem(me + i, n)).wait_recv()
        return 0

    lax.fori_loop(1, n, pulled, 0)
    q_load.wait()

    for h in range(QH):
        if qper >= HEAD:
            per = qper // HEAD
            bias = pbuf[h // per, h % per : h % per + 1, :]
        else:
            parts = HEAD // qper
            bias = sum(pbuf[h * parts + i, 0:1, :] for i in range(parts))
        x = q_ref[:, h * HEAD : (h + 1) * HEAD].astype(jnp.float32) + bias
        at = (h % RATIO) * rows
        qs[h // RATIO, at : at + rows, :] = spin(x, q_cos, q_sin).astype(jnp.bfloat16)
    share = n // KVH
    k_bias = [sum(pbuf[g * share + i, 2:3, :] for i in range(share)) for g in range(KVH)]
    v_bias = [sum(pbuf[g * share + i, 3:4, :] for i in range(share)) for g in range(KVH)]
    within = lax.broadcasted_iota(jnp.int32, (FRAME_TOK, HEAD), 0).astype(jnp.float32)

    def chunk(first):
        for j in range(4):
            s = first + j
            order = pbuf[s][8 - frames :, :]
            cosine, sine = cos_sin(order, tab)
            for f in range(frames):
                kpos = order[f : f + 1, :] * FRAME_TOK + within
                at = j * rows + f * FRAME_TOK
                hide[at : at + FRAME_TOK, :] = jnp.where(kpos <= qpos, 0.0, NEG)
            for g in range(KVH):
                cols = slice(g * HEAD, (g + 1) * HEAD)
                x = kbuf[s, :, cols].astype(jnp.float32) + k_bias[g]
                ksc[g, j * rows : (j + 1) * rows, :] = spin(x, cosine, sine).astype(jnp.bfloat16)
                y = vbuf[s, :, cols].astype(jnp.float32) + v_bias[g]
                vsc[g, j * rows : (j + 1) * rows, :] = y.astype(jnp.bfloat16)
        for g in range(KVH):
            scores = lax.dot_general(
                ksc[g], qs[g], (((1,), (1,)), ((), ())), preferred_element_type=jnp.float32
            )
            mask = hide[...]
            scores = scores + jnp.concatenate([mask] * (scores.shape[1] // HEAD), axis=1)
            old = top[g]
            new = jnp.maximum(old, jnp.max(scores, axis=0, keepdims=True))
            expo = jnp.exp2(scores - new)
            factor = jnp.exp2(old - new)
            top[g] = new
            den[g] = den[g] * factor + jnp.sum(expo, axis=0, keepdims=True)
            acc[g] = acc[g] * factor + lax.dot_general(
                vsc[g], expo.astype(jnp.bfloat16), (((0,), (0,)), ((), ())),
                preferred_element_type=jnp.float32,
            )

    low = a < A // 2
    mirror = jnp.where(low, a, A - 1 - a)

    def step(d, _):
        along_a(d + 1, True)
        along_b(d, True)
        near = jnp.where(d % 2 == 1, -((d + 1) // 2), d // 2)
        plane = mirror + jnp.where(d <= 2 * mirror, near, d - mirror)
        plane = jnp.where(low, plane, A - 1 - plane)
        for y in range(B):
            for t in range(PIECES):
                arrive(t, slot(plane, y, 1 - core))
        if 2 * B == 4:
            chunk(plane * 4)
        else:
            def part(i, _):
                chunk(plane * 2 * B + i * 4)
                return 0

            lax.fori_loop(0, 2 * B // 4, part, 0)
        return 0

    lax.fori_loop(0, A, step, 0)

    for g in range(KVH):
        mixed = acc[g] * (1.0 / den[g])
        flat = mixed.T.astype(jnp.bfloat16)
        for r in range(RATIO):
            h = g * RATIO + r
            o_ref[:, h * HEAD : (h + 1) * HEAD] = flat[r * rows : (r + 1) * rows, :]

    for t in range(PIECES):
        fan(t, me, (0, 1, 2, 3, 4), False)

    def drain(d, _):
        along_a(d + 1, False)
        along_b(d, False)
        return 0

    lax.fori_loop(0, A, drain, 0)

    def pushed(i, _):
        pack_copy(i, me).wait_send()
        return 0

    lax.fori_loop(1, n, pushed, 0)


def line_tables():
    rows = tables()
    pair = np.arange(HEAD) % HALF
    temporal = pair < PAIRS_T
    rows[0:32, temporal] = 0.0
    rows[32] = np.where(temporal, rows[32], 0.0)
    rows[33] = np.where(temporal, 1.0, 0.0)
    rows[34] = np.where(temporal, np.where(np.arange(HEAD) < HALF, -1.0, 1.0), 0.0)
    return rows


def circle(x):
    k = jnp.round(x * (2.0 / math.pi))
    r = x - k * 1.5703125
    r = r - k * (math.pi / 2.0 - 1.5703125)
    w = r * r
    s = r + r * w * (-1.6666654611e-1 + w * (8.3321608736e-3 - w * 1.9515295891e-4))
    c = 1.0 - 0.5 * w + w * w * (4.166664568298827e-2 + w * (-1.388731625493765e-3 + w * 2.443315711809948e-5))
    turn = k - 4.0 * jnp.floor(k * 0.25)
    odd = jnp.logical_or(turn == 1.0, turn == 3.0)
    cosine = jnp.where(odd, s, c)
    sine = jnp.where(odd, c, s)
    cosine = jnp.where(jnp.logical_or(turn == 1.0, turn == 2.0), -cosine, cosine)
    sine = jnp.where(turn >= 2.0, -sine, sine)
    return cosine, sine


def line_kernel(
    n,
    q_hbm, k_hbm, v_hbm, qb_hbm, kb_hbm, vb_hbm, order_hbm, tab_hbm,
    o_ref,
    qb_ref, kb_ref, vb_ref, order_ref, tab_ref,
    q_ref, kv, pbuf, ctab, stab, ftab, qs, acc, top, den, ksc, hide, obuf,
    recv, send, precv, psend, qsem, osem, load,
):
    me = lax.axis_index("seq")
    rows = k_hbm.shape[0]
    frames = rows // FRAME_TOK
    half = KVH // 2
    wide = half * HEAD
    qwide = QH * HEAD // 2
    core = me % 2
    y = (me // 2) % 2
    z = me // 4
    sib = me + 1 - 2 * core
    low = z < 2
    end = jnp.logical_or(z == 0, z == 3)
    mid = jnp.logical_not(end)

    def slot(a, b, c):
        return (a * 2 + b) * 2 + c

    def up(i):
        return jnp.where(low, i, 3 - i)

    Z0, Z1, Z2, Z3 = up(0), up(1), up(2), up(3)
    beside = jnp.where(end, Z1, Z0)

    def to(s):
        return dict(device_id={"seq": s}, device_id_type=MESH)

    def part(c, size):
        return pl.ds(pl.multiple_of(c * size, size), size)

    barrier = pltpu.get_barrier_semaphore()

    def greet(i, _):
        pl.semaphore_signal(barrier, inc=1, **to(lax.rem(me + i, n)))
        return 0

    lax.fori_loop(1, n, greet, 0)
    small = [
        pltpu.make_async_copy(src, dst, load.at[i])
        for i, (src, dst) in enumerate((
            (order_hbm, order_ref), (qb_hbm, qb_ref), (kb_hbm, kb_ref), (vb_hbm, vb_ref), (tab_hbm, tab_ref),
        ))
    ]
    mine = [
        pltpu.make_async_copy(k_hbm.at[:, part(core, wide)], kv.at[me], load.at[5]),
        pltpu.make_async_copy(v_hbm.at[:, part(core, wide)], kv.at[n + me], load.at[6]),
        pltpu.make_async_copy(q_hbm.at[:, part(core, qwide)], q_ref.at[0], load.at[7]),
    ]
    for c in small + mine:
        c.start()

    lane = lax.broadcasted_iota(jnp.int32, (1, HEAD), 1)
    group = lane // (HEAD // KVH)

    def row(ref):
        return ref[...].astype(jnp.float32)[None, :]

    def placed(values, at):
        return jnp.where(group == at % KVH, jnp.concatenate([values] * KVH, axis=1), 0.0)

    pl.semaphore_wait(barrier, n - 1)

    def own(t, dz, dy, dc):
        return pltpu.make_async_remote_copy(
            src_ref=(k_hbm, v_hbm)[t].at[:, part(dc, wide)],
            dst_ref=kv.at[t * n + me],
            send_sem=send.at[0],
            recv_sem=recv.at[t * n + me],
            **to(slot(dz, dy, dc)),
        )

    def passed(t, s, dz, dy):
        return pltpu.make_async_remote_copy(
            src_ref=kv.at[t * n + s],
            dst_ref=kv.at[t * n + s],
            send_sem=send.at[1],
            recv_sem=recv.at[t * n + s],
            **to(slot(dz, dy, core)),
        )

    sent = {"end": [0, 0], "mid": [0, 0]}

    def own_to(roles, t, dz, dy):
        for dc in (0, 1):
            own(t, dz, dy, dc).start()
        for r in roles:
            sent[r][0] += 2

    def pass_on(role, t, s, dz, dy):
        passed(t, s, dz, dy).start()
        sent[role][1] += 1

    def arrive(t, s):
        passed(t, s, z, y).wait_recv()

    def pack_copy(i, s):
        return pltpu.make_async_remote_copy(
            src_ref=pbuf.at[:, pl.ds(s, 1)],
            dst_ref=pbuf.at[:, pl.ds(s, 1)],
            send_sem=psend,
            recv_sem=precv.at[s],
            **to(lax.rem(me + i, n)),
        )

    def push(i, _):
        pack_copy(i, me).start()
        return 0

    def ways(t):
        own_to(("end", "mid"), t, beside, y)
        own_to(("end", "mid"), t, z, 1 - y)
        pl.when(mid)(lambda: own_to(("mid",), t, Z2, y))

    ways(0)
    for c in small:
        c.wait()
    q_row = row(qb_ref)
    pbuf[0, pl.ds(me, 1), :] = q_row[:, :HEAD]
    pbuf[1, pl.ds(me, 1), :] = q_row[:, HEAD:]
    third = placed(row(kb_ref), me) + placed(row(vb_ref), me + 1)
    for f in range(frames):
        third = third + jnp.where(lane == (me + 2) % KVH * (HEAD // KVH) + f, order_ref[f].astype(jnp.float32), 0.0)
    pbuf[2, pl.ds(me, 1), :] = third
    lax.fori_loop(1, n, push, 0)
    ways(1)
    q_send = pltpu.make_async_remote_copy(
        src_ref=q_hbm.at[:, part(1 - core, qwide)], dst_ref=q_ref.at[1],
        send_sem=qsem.at[0], recv_sem=qsem.at[1], **to(sib),
    )
    q_send.start()
    for t in (0, 1):
        own(t, z, y, 1 - core).start()
        for r in sent:
            sent[r][0] += 1

    ORDER = (1, 0)
    def role(cond, name, steps):
        def act():
            for t, s, targets in steps:
                arrive(t, s)
                for dz, dy in targets:
                    pass_on(name, t, s, dz, dy)

        pl.when(cond)(act)

    def both(t, dz, dy, targets):
        return [(t, slot(dz, dy, k), targets) for k in ORDER]

    across = (z, 1 - y)

    def gather(t, dz, dy):
        for k in ORDER:
            arrive(t, slot(dz, dy, k))

    def pairs(t, ahead, behind):
        steps = []
        for k in ORDER:
            steps += [(t, slot(Z0, y, k), ahead), (t, slot(Z2, y, k), behind)]
        return steps

    role(end, "end", both(0, Z1, y, [across]))
    role(mid, "mid", pairs(0, [(Z2, y), across], [(Z0, y), across]))

    def pulled(i, _):
        pack_copy(i, lax.rem(me + i, n)).wait_recv()
        return 0

    lax.fori_loop(1, n, pulled, 0)
    tab = tab_ref[...]
    third = pbuf[2]
    at = lax.broadcasted_iota(jnp.int32, (n, HEAD), 0)
    spot = lax.broadcasted_iota(jnp.int32, (n, HEAD), 1) - (at + 2) % KVH * (HEAD // KVH)
    for f in range(frames):
        frame = jnp.sum(jnp.where(spot == f, third, 0.0), axis=1, keepdims=True)
        frame = jnp.broadcast_to(frame, (n, HEAD))
        cosine, sine = circle(frame * tab[32:33, :])
        ctab[f] = cosine * tab[33:34, :]
        stab[f] = sine * tab[34:35, :]
        ftab[f] = frame * FRAME_TOK

    def bias_row(g, turn):
        got = jnp.zeros((1, HEAD), jnp.float32)
        for i in range(KVH):
            piece = pbuf[2, pl.ds((core * half + g) * KVH + i, 1), :]
            got = got + jnp.where(group == (i + turn) % KVH, piece, 0.0)
        return got if turn == 0 else pltpu.roll(got, HEAD - turn * (HEAD // KVH), 1)

    k_bias = [bias_row(g, 0) for g in range(half)]
    v_bias = [bias_row(g, 1) for g in range(half)]

    def angles(s):
        cosines = [ctab[f, pl.ds(s, 1), :] + tab[0:16, :] for f in range(frames)]
        sines = [stab[f, pl.ds(s, 1), :] + tab[16:32, :] for f in range(frames)]
        return jnp.concatenate(cosines, axis=0), jnp.concatenate(sines, axis=0)

    fold = math.log2(math.e) / math.sqrt(HEAD)
    q_cos, q_sin, q_pos = [], [], []
    for s in (sib, me):
        cosine, sine = angles(s)
        q_cos.append(cosine * fold)
        q_sin.append(sine * fold)
        qpos = (lane % FRAME_TOK).astype(jnp.float32)
        for f in range(frames):
            qpos = qpos + jnp.where(lane % rows // FRAME_TOK == f, ftab[f, pl.ds(s, 1), :], 0.0)
        q_pos.append(qpos)
    blocks = RATIO * rows // HEAD
    within = lax.broadcasted_iota(jnp.int32, (FRAME_TOK, HEAD), 0).astype(jnp.float32)

    def turn_keys(first, count, at):
        for j in range(count):
            s = first + j
            cosine, sine = angles(s)
            for f in range(frames):
                kpos = ftab[f, pl.ds(s, 1), :] + within
                r = at + j * rows + f * FRAME_TOK
                for k in range(2):
                    hide[k, r : r + FRAME_TOK, :] = jnp.where(kpos <= q_pos[k], 0.0, NEG)
            for g in range(half):
                x = kv[s, :, g * HEAD : (g + 1) * HEAD].astype(jnp.float32) + k_bias[g]
                r = at + j * rows
                ksc[g, r : r + rows, :] = spin(x, cosine, sine).astype(jnp.bfloat16)

    def attend(g, k, first, count, at, fresh):
        keys = slice(at, at + count * rows)
        vals = kv[pl.ds(n + first, count), :, g * HEAD : (g + 1) * HEAD].reshape(count * rows, HEAD)
        mask = hide[k, keys, :]
        for b in range(k * blocks, (k + 1) * blocks):
            cols = slice(b * HEAD, (b + 1) * HEAD)
            scores = lax.dot_general(
                ksc[g, keys, :], qs[g, cols, :], (((1,), (1,)), ((), ())), preferred_element_type=jnp.float32
            )
            scores = scores + mask
            new = jnp.max(scores, axis=0, keepdims=True)
            if not fresh:
                old = top[g, :, cols]
                new = jnp.maximum(old, new)
            expo = jnp.exp2(scores - new)
            total = jnp.sum(expo, axis=0, keepdims=True)
            mixed = lax.dot_general(
                vals, expo.astype(jnp.bfloat16), (((0,), (0,)), ((), ())), preferred_element_type=jnp.float32
            )
            top[g, :, cols] = new
            if fresh:
                den[g, :, cols] = total
                acc[g, :, cols] = mixed
            else:
                factor = jnp.exp2(old - new)
                den[g, :, cols] = den[g, :, cols] * factor + total
                acc[g, :, cols] = acc[g, :, cols] * factor + mixed

    def plane(p, at, fresh):
        for g in range(half):
            for k in range(2):
                attend(g, k, p * 4, 4, at, fresh)

    role(end, "end", both(1, Z0, 1 - y, [(Z1, y), (Z2, y)]) + both(1, Z1, y, [across]))
    role(mid, "mid", pairs(1, [(Z2, y)], [(Z0, y), across]) + both(1, z, 1 - y, []))
    mine[2].wait()
    q_send.wait_recv()
    for k in range(2):
        for h in range(QH // 2):
            bias = pbuf[h % 2, pl.ds(core * (n // 2) + h // 2, 1), :]
            x = q_ref[1 - k, :, h * HEAD : (h + 1) * HEAD].astype(jnp.float32) + bias
            r = (k * RATIO + h % RATIO) * rows
            qs[h // RATIO, r : r + rows, :] = spin(x, q_cos[k], q_sin[k]).astype(jnp.bfloat16)

    for c in mine[:2]:
        c.wait()
    arrive(0, sib)
    gather(0, z, 1 - y)
    turn_keys(z * 4, 4, 0)
    arrive(1, sib)
    near = jnp.where(end, Z1, Z0)
    role(end, "end", both(0, Z2, y, [across]))
    role(mid, "mid", both(0, Z3, y, [(Z0, y), across]))
    plane(z, 0, True)
    gather(0, near, 1 - y)
    turn_keys(near * 4, 4, 4 * rows)
    role(end, "end", both(1, Z2, y, [across]))
    role(mid, "mid", both(1, Z3, y, [(Z0, y)]))
    gather(1, near, 1 - y)
    plane(near, 4 * rows, False)
    role(end, "end", both(0, Z3, y, [across]))
    role(mid, "mid", both(1, Z3, 1 - y, [(Z0, y)]))
    gather(0, Z2, 1 - y)
    turn_keys(Z2 * 4, 4, 8 * rows)
    gather(1, Z2, 1 - y)
    plane(Z2, 8 * rows, False)
    gather(0, Z3, 1 - y)
    turn_keys(Z3 * 4, 4, 12 * rows)
    role(end, "end", both(1, Z3, y, []) + both(1, Z3, 1 - y, []))

    out = []
    for k in range(2):
        for g in range(half):
            attend(g, k, Z3 * 4, 4, 12 * rows, False)
            for b in range(blocks):
                cols = slice((k * blocks + b) * HEAD, (k * blocks + b + 1) * HEAD)
                mixed = acc[g, :, cols] * (1.0 / den[g, :, cols])
                flat = (mixed.T + v_bias[g]).astype(jnp.bfloat16)
                for i in range(HEAD // rows):
                    h = b * (HEAD // rows) + i
                    piece = flat[i * rows : (i + 1) * rows, :]
                    if k == 0:
                        obuf[g, :, h * HEAD : (h + 1) * HEAD] = piece
                    else:
                        at = core * qwide + (g * RATIO + h) * HEAD
                        o_ref[:, pl.ds(pl.multiple_of(at, HEAD), HEAD)] = piece
            if k == 0:
                at = core * qwide + g * RATIO * HEAD
                c = pltpu.make_async_remote_copy(
                    src_ref=obuf.at[g],
                    dst_ref=o_ref.at[:, pl.ds(pl.multiple_of(at, HEAD), RATIO * HEAD)],
                    send_sem=osem.at[g], recv_sem=osem.at[half + g], **to(sib),
                )
                c.start()
                out.append(c)

    def drain(name):
        def act():
            for i in range(2):
                size = kv.at[pl.ds(0, sent[name][i])]
                pltpu.make_async_copy(size, size, send.at[i]).wait()

        return act

    pl.when(end)(drain("end"))
    pl.when(mid)(drain("mid"))
    size = pbuf.at[:, pl.ds(0, n - 1)]
    pltpu.make_async_copy(size, size, psend).wait()
    q_send.wait_send()
    for c in out:
        c.wait()


def on_line(n, query, keys, values, query_bias, key_bias, value_projection_bias, frame_order):
    rows = keys.shape[0]
    half = KVH // 2
    frames = rows // FRAME_TOK
    wide = RATIO * 2 * rows
    return pl.pallas_call(
        functools.partial(line_kernel, n),
        out_shape=jax.ShapeDtypeStruct(query.shape, jnp.bfloat16),
        in_specs=[pl.BlockSpec(memory_space=pltpu.HBM)] * 8,
        out_specs=pl.BlockSpec(memory_space=pltpu.VMEM),
        scratch_shapes=[
            pltpu.VMEM(query_bias.shape, jnp.bfloat16),
            pltpu.VMEM(key_bias.shape, jnp.bfloat16),
            pltpu.VMEM(key_bias.shape, jnp.bfloat16),
            pltpu.SMEM(frame_order.shape, jnp.int32),
            pltpu.VMEM((40, HEAD), jnp.float32),
            pltpu.VMEM((2, rows, QH * HEAD // 2), jnp.bfloat16),
            pltpu.VMEM((2 * n, rows, half * HEAD), jnp.bfloat16),
            pltpu.VMEM((3, n, HEAD), jnp.float32),
            pltpu.VMEM((frames, n, HEAD), jnp.float32),
            pltpu.VMEM((frames, n, HEAD), jnp.float32),
            pltpu.VMEM((frames, n, HEAD), jnp.float32),
            pltpu.VMEM((half, wide, HEAD), jnp.bfloat16),
            pltpu.VMEM((half, HEAD, wide), jnp.float32),
            pltpu.VMEM((half, 1, wide), jnp.float32),
            pltpu.VMEM((half, 1, wide), jnp.float32),
            pltpu.VMEM((half, n * rows, HEAD), jnp.bfloat16),
            pltpu.VMEM((2, n * rows, HEAD), jnp.float32),
            pltpu.VMEM((half, rows, RATIO * HEAD), jnp.bfloat16),
            pltpu.SemaphoreType.DMA((2 * n,)),
            pltpu.SemaphoreType.DMA((2,)),
            pltpu.SemaphoreType.DMA((n,)),
            pltpu.SemaphoreType.DMA,
            pltpu.SemaphoreType.DMA((2,)),
            pltpu.SemaphoreType.DMA((2 * half,)),
            pltpu.SemaphoreType.DMA((8,)),
        ],
        compiler_params=pltpu.CompilerParams(vmem_limit_bytes=24 << 20, collective_id=1, has_side_effects=True),
    )(*(
        pltpu.with_memory_space_constraint(x, pltpu.HBM)
        for x in (
            query, keys, values, query_bias, key_bias, value_projection_bias, frame_order,
            jnp.asarray(line_tables()),
        )
    ))


def on_device(n, query, keys, values, query_bias, key_bias, value_projection_bias, frame_order):
    chips = n // 2
    B = 1
    while B * B * 4 <= chips:
        B *= 2
    A = chips // B
    rows = keys.shape[0]
    qper = query_bias.shape[0]
    wide = RATIO * rows
    keys_at_once = 4 * rows
    whole = pl.BlockSpec(memory_space=pltpu.VMEM)
    far = pl.BlockSpec(memory_space=pltpu.HBM)
    return pl.pallas_call(
        functools.partial(kernel, A, B, n, qper),
        out_shape=jax.ShapeDtypeStruct(query.shape, jnp.bfloat16),
        in_specs=[far] * 8,
        out_specs=whole,
        scratch_shapes=[
            pltpu.VMEM(query_bias.shape, jnp.bfloat16),
            pltpu.VMEM(key_bias.shape, jnp.bfloat16),
            pltpu.VMEM(key_bias.shape, jnp.bfloat16),
            pltpu.SMEM(frame_order.shape, jnp.int32),
            pltpu.VMEM((40, HEAD), jnp.float32),
            pltpu.VMEM(query.shape, jnp.bfloat16),
            pltpu.VMEM((8, HEAD), jnp.float32),
            pltpu.VMEM((n, rows, KVH * HEAD), jnp.bfloat16),
            pltpu.VMEM((n, rows, KVH * HEAD), jnp.bfloat16),
            pltpu.VMEM((n, 8, HEAD), jnp.float32),
            pltpu.VMEM((KVH, wide, HEAD), jnp.bfloat16),
            pltpu.VMEM((KVH, HEAD, wide), jnp.float32),
            pltpu.VMEM((KVH, 1, wide), jnp.float32),
            pltpu.VMEM((KVH, 1, wide), jnp.float32),
            pltpu.VMEM((KVH, keys_at_once, HEAD), jnp.bfloat16),
            pltpu.VMEM((KVH, keys_at_once, HEAD), jnp.bfloat16),
            pltpu.VMEM((keys_at_once, HEAD), jnp.float32),
            pltpu.SemaphoreType.DMA((PIECES, n)),
            pltpu.SemaphoreType.DMA((PIECES, 5, n)),
            pltpu.SemaphoreType.DMA((n,)),
            pltpu.SemaphoreType.DMA((n,)),
            pltpu.SemaphoreType.DMA((8,)),
        ],
        compiler_params=pltpu.CompilerParams(vmem_limit_bytes=(16 if n <= 32 else 48) << 20, collective_id=0, has_side_effects=True),
    )(*(
        pltpu.with_memory_space_constraint(x, pltpu.HBM)
        for x in (
            query, keys, values, query_bias, key_bias, value_projection_bias, frame_order,
            jnp.asarray(tables()),
        )
    ))


def solution(mesh):
    placed = (
        P(("groups", "seq"), None),
        P(("groups", "seq"), None),
        P(("groups", "seq"), None),
        P("seq"),
        P("seq"),
        P("seq"),
        P(("groups", "seq")),
    )
    n = mesh.shape["seq"]
    return jax.shard_map(
        functools.partial(on_line if n == 16 else on_device, n),
        mesh=mesh,
        in_specs=placed,
        out_specs=P(("groups", "seq"), None),
        check_vma=False,
    )
```

```python
import functools
import math

import jax
import jax.numpy as jnp
import numpy as np
from jax import lax
from jax.experimental import pallas as pl
from jax.experimental.pallas import tpu as pltpu
from jax.sharding import PartitionSpec as P

HEAD = 128
HALF = HEAD // 2
QH = 32
KVH = 4
RATIO = QH // KVH
GRID = 4
FRAME_TOK = 16
MESH = pl.DeviceIdType.MESH
NEG = -1e30
PIECES = 2
PAIRS_T = HALF // 4
PAIRS_R = HALF // 4 + 3 * HALF // 8


def tables():
    pair = np.arange(HEAD) % HALF
    freq = np.exp(-(2.0 * pair / HEAD) * math.log(1000000.0))
    tok = np.arange(FRAME_TOK)
    source = np.where(pair[None, :] < PAIRS_R, (tok // GRID)[:, None], (tok % GRID)[:, None])
    angle = source * freq[None, :]
    sign = np.where(np.arange(HEAD) < HALF, -1.0, 1.0)
    rows = np.zeros((40, HEAD), np.float32)
    rows[0:16] = np.cos(angle)
    rows[16:32] = np.sin(angle) * sign[None, :]
    rows[32] = 2.0 * freq
    return rows


def cos_sin(frames, spatial):
    angle = frames * spatial[32:33, :]
    turns = jnp.round(angle * (1.0 / (2.0 * math.pi)))
    angle = angle - turns * 6.28125
    angle = angle - turns * (2.0 * math.pi - 6.28125)
    lane = lax.broadcasted_iota(jnp.int32, (FRAME_TOK, HEAD), 1)
    temporal = lane % HALF < PAIRS_T
    sign = jnp.where(lane < HALF, -1.0, 1.0)
    cos_t, sin_t = jnp.cos(angle), jnp.sin(angle)
    cosines, sines = [], []
    for j in range(frames.shape[0]):
        cosines.append(jnp.where(temporal, cos_t[j : j + 1, :], spatial[0:16, :]))
        sines.append(jnp.where(temporal, sin_t[j : j + 1, :] * sign, spatial[16:32, :]))
    return jnp.concatenate(cosines, axis=0), jnp.concatenate(sines, axis=0)


def spin(x, cosine, sine):
    return x * cosine + pltpu.roll(x, HALF, 1) * sine


def kernel(
    A, B, n, qper,
    q_hbm, k_hbm, v_hbm, qb_hbm, kb_hbm, vb_hbm, order_hbm, tab_hbm,
    o_ref,
    qb_ref, kb_ref, vb_ref, order_ref, tab_ref,
    q_ref, pack_ref, kbuf, vbuf, pbuf, qs, acc, top, den, ksc, vsc, hide,
    recv, send, precv, psend, load,
):
    me = lax.axis_index("seq")
    rows = kbuf.shape[1]
    frames = rows // FRAME_TOK
    cut = rows // (PIECES // 2)
    core = me % 2
    b = (me // 2) % B
    a = me // (2 * B)

    def piece(p, s):
        return (kbuf, vbuf)[p % 2].at[s, pl.ds((p // 2) * cut, cut)]

    def slot(x, y, z):
        return (x * B + y) * 2 + z

    ways = (
        (a + 1 < A, slot(a + 1, b, core)),
        (a > 0, slot(a - 1, b, core)),
        (b + 1 < B, slot(a, b + 1, core)),
        (b > 0, slot(a, b - 1, core)),
        (None, slot(a, b, 1 - core)),
    )

    def copy(t, s, way):
        return pltpu.make_async_remote_copy(
            src_ref=piece(t, s),
            dst_ref=piece(t, s),
            send_sem=send.at[t, way, s],
            recv_sem=recv.at[t, s],
            device_id={"seq": ways[way][1]},
            device_id_type=MESH,
        )

    def when(cond, act):
        if cond is None:
            act()
        else:
            pl.when(cond)(act)

    def fan(t, s, dirs, start):
        for way in dirs:
            c = copy(t, s, way)
            when(ways[way][0], c.start if start else c.wait_send)

    def arrive(t, s):
        copy(t, s, 4).wait_recv()

    def inside(i, size):
        return jnp.logical_and(i >= 0, i < size)

    def along_a(d, start):
        for t in range(PIECES):
            for sg in (1, -1):
                x = a + sg * d

                @pl.when(jnp.logical_and(inside(x, A), d < A))
                def _(x=x, sg=sg, t=t):
                    s = slot(x, b, core)
                    if start:
                        arrive(t, s)
                    fan(t, s, (1 if sg > 0 else 0, 2, 3, 4), start)

    def along_b(d, start):
        for e in range(1, B):
            for t in range(PIECES):
                for sg in (1, -1):
                    x = a + sg * d
                    ok = inside(x, A) if sg > 0 else jnp.logical_and(inside(x, A), d > 0)
                    for sb in (1, -1):
                        y = b + sb * e

                        @pl.when(jnp.logical_and(ok, inside(y, B)))
                        def _(x=x, y=y, sb=sb, t=t):
                            s = slot(x, y, core)
                            if start:
                                arrive(t, s)
                            fan(t, s, (3 if sb > 0 else 2, 4), start)

    barrier = pltpu.get_barrier_semaphore()

    def greet(i, _):
        pl.semaphore_signal(barrier, inc=1, device_id={"seq": lax.rem(me + i, n)}, device_id_type=MESH)
        return 0

    lax.fori_loop(1, n, greet, 0)
    k_load = pltpu.make_async_copy(k_hbm, kbuf.at[me], load.at[0])
    v_load = pltpu.make_async_copy(v_hbm, vbuf.at[me], load.at[1])
    q_load = pltpu.make_async_copy(q_hbm, q_ref, load.at[2])
    small = [
        pltpu.make_async_copy(src, dst, load.at[3 + i])
        for i, (src, dst) in enumerate((
            (order_hbm, order_ref), (qb_hbm, qb_ref), (kb_hbm, kb_ref), (vb_hbm, vb_ref), (tab_hbm, tab_ref),
        ))
    ]
    for c in small + [k_load, v_load, q_load]:
        c.start()

    lane = lax.broadcasted_iota(jnp.int32, (1, HEAD), 1)

    def placed(values):
        size = values.shape[1]
        spots = HEAD // size
        return jnp.where(lane // size == me % spots, jnp.concatenate([values] * spots, axis=1), 0.0)

    def row(ref):
        return ref[...].astype(jnp.float32)[None, :]

    for c in small:
        c.wait()
    pack_ref[...] = jnp.zeros_like(pack_ref)
    q_row = row(qb_ref)
    if qper >= HEAD:
        for i in range(qper // HEAD):
            pack_ref[i : i + 1, :] = q_row[:, i * HEAD : (i + 1) * HEAD]
    else:
        pack_ref[0:1, :] = placed(q_row)
    pack_ref[2:3, :] = placed(row(kb_ref))
    pack_ref[3:4, :] = placed(row(vb_ref))
    qpos = (lane % FRAME_TOK).astype(jnp.float32)
    for f in range(frames):
        frame = order_ref[f].astype(jnp.float32)
        pack_ref[8 - frames + f : 9 - frames + f, :] = jnp.full((1, HEAD), 1.0, jnp.float32) * frame
        qpos = qpos + jnp.where((lane % rows) // FRAME_TOK == f, frame * FRAME_TOK, 0.0)
    pbuf[me] = pack_ref[...]
    tab = tab_ref[...]
    q_cos, q_sin = cos_sin(pack_ref[8 - frames :, :], tab)
    fold = math.log2(math.e) / math.sqrt(HEAD)
    q_cos, q_sin = q_cos * fold, q_sin * fold
    k_load.wait()
    v_load.wait()
    pl.semaphore_wait(barrier, n - 1)

    def pack_copy(i, s):
        return pltpu.make_async_remote_copy(
            src_ref=pack_ref,
            dst_ref=pbuf.at[s],
            send_sem=psend.at[i],
            recv_sem=precv.at[s],
            device_id={"seq": lax.rem(me + i, n)},
            device_id_type=MESH,
        )

    def push(i, _):
        pack_copy(i, me).start()
        return 0

    lax.fori_loop(1, n, push, 0)
    for t in range(PIECES):
        fan(t, me, (0, 1, 2, 3, 4), True)

    acc[...] = jnp.zeros_like(acc)
    den[...] = jnp.zeros_like(den)
    top[...] = jnp.full_like(top, NEG)

    def pulled(i, _):
        pack_copy(i, lax.rem(me + i, n)).wait_recv()
        return 0

    lax.fori_loop(1, n, pulled, 0)
    q_load.wait()

    for h in range(QH):
        if qper >= HEAD:
            per = qper // HEAD
            bias = pbuf[h // per, h % per : h % per + 1, :]
        else:
            parts = HEAD // qper
            bias = sum(pbuf[h * parts + i, 0:1, :] for i in range(parts))
        x = q_ref[:, h * HEAD : (h + 1) * HEAD].astype(jnp.float32) + bias
        at = (h % RATIO) * rows
        qs[h // RATIO, at : at + rows, :] = spin(x, q_cos, q_sin).astype(jnp.bfloat16)
    share = n // KVH
    k_bias = [sum(pbuf[g * share + i, 2:3, :] for i in range(share)) for g in range(KVH)]
    v_bias = [sum(pbuf[g * share + i, 3:4, :] for i in range(share)) for g in range(KVH)]
    within = lax.broadcasted_iota(jnp.int32, (FRAME_TOK, HEAD), 0).astype(jnp.float32)

    def chunk(first):
        for j in range(4):
            s = first + j
            order = pbuf[s][8 - frames :, :]
            cosine, sine = cos_sin(order, tab)
            for f in range(frames):
                kpos = order[f : f + 1, :] * FRAME_TOK + within
                at = j * rows + f * FRAME_TOK
                hide[at : at + FRAME_TOK, :] = jnp.where(kpos <= qpos, 0.0, NEG)
            for g in range(KVH):
                cols = slice(g * HEAD, (g + 1) * HEAD)
                x = kbuf[s, :, cols].astype(jnp.float32) + k_bias[g]
                ksc[g, j * rows : (j + 1) * rows, :] = spin(x, cosine, sine).astype(jnp.bfloat16)
                y = vbuf[s, :, cols].astype(jnp.float32) + v_bias[g]
                vsc[g, j * rows : (j + 1) * rows, :] = y.astype(jnp.bfloat16)
        for g in range(KVH):
            scores = lax.dot_general(
                ksc[g], qs[g], (((1,), (1,)), ((), ())), preferred_element_type=jnp.float32
            )
            mask = hide[...]
            scores = scores + jnp.concatenate([mask] * (scores.shape[1] // HEAD), axis=1)
            old = top[g]
            new = jnp.maximum(old, jnp.max(scores, axis=0, keepdims=True))
            expo = jnp.exp2(scores - new)
            factor = jnp.exp2(old - new)
            top[g] = new
            den[g] = den[g] * factor + jnp.sum(expo, axis=0, keepdims=True)
            acc[g] = acc[g] * factor + lax.dot_general(
                vsc[g], expo.astype(jnp.bfloat16), (((0,), (0,)), ((), ())),
                preferred_element_type=jnp.float32,
            )

    low = a < A // 2
    mirror = jnp.where(low, a, A - 1 - a)

    def step(d, _):
        along_a(d + 1, True)
        along_b(d, True)
        near = jnp.where(d % 2 == 1, -((d + 1) // 2), d // 2)
        plane = mirror + jnp.where(d <= 2 * mirror, near, d - mirror)
        plane = jnp.where(low, plane, A - 1 - plane)
        for y in range(B):
            for t in range(PIECES):
                arrive(t, slot(plane, y, 1 - core))
        if 2 * B == 4:
            chunk(plane * 4)
        else:
            def part(i, _):
                chunk(plane * 2 * B + i * 4)
                return 0

            lax.fori_loop(0, 2 * B // 4, part, 0)
        return 0

    lax.fori_loop(0, A, step, 0)

    for g in range(KVH):
        mixed = acc[g] * (1.0 / den[g])
        flat = mixed.T.astype(jnp.bfloat16)
        for r in range(RATIO):
            h = g * RATIO + r
            o_ref[:, h * HEAD : (h + 1) * HEAD] = flat[r * rows : (r + 1) * rows, :]

    for t in range(PIECES):
        fan(t, me, (0, 1, 2, 3, 4), False)

    def drain(d, _):
        along_a(d + 1, False)
        along_b(d, False)
        return 0

    lax.fori_loop(0, A, drain, 0)

    def pushed(i, _):
        pack_copy(i, me).wait_send()
        return 0

    lax.fori_loop(1, n, pushed, 0)


def line_tables():
    rows = tables()
    pair = np.arange(HEAD) % HALF
    temporal = pair < PAIRS_T
    rows[0:32, temporal] = 0.0
    rows[32] = np.where(temporal, rows[32], 0.0)
    rows[33] = np.where(temporal, 1.0, 0.0)
    rows[34] = np.where(temporal, np.where(np.arange(HEAD) < HALF, -1.0, 1.0), 0.0)
    return rows


def circle(x):
    k = jnp.round(x * (2.0 / math.pi))
    r = x - k * 1.5703125
    r = r - k * (math.pi / 2.0 - 1.5703125)
    w = r * r
    s = r + r * w * (-1.6666654611e-1 + w * (8.3321608736e-3 - w * 1.9515295891e-4))
    c = 1.0 - 0.5 * w + w * w * (4.166664568298827e-2 + w * (-1.388731625493765e-3 + w * 2.443315711809948e-5))
    turn = k - 4.0 * jnp.floor(k * 0.25)
    odd = jnp.logical_or(turn == 1.0, turn == 3.0)
    cosine = jnp.where(odd, s, c)
    sine = jnp.where(odd, c, s)
    cosine = jnp.where(jnp.logical_or(turn == 1.0, turn == 2.0), -cosine, cosine)
    sine = jnp.where(turn >= 2.0, -sine, sine)
    return cosine, sine


def line_kernel(
    n,
    q_hbm, k_hbm, v_hbm, qb_hbm, kb_hbm, vb_hbm, order_hbm, tab_hbm,
    o_ref,
    qb_ref, kb_ref, vb_ref, order_ref, tab_ref,
    q_ref, kv, pbuf, ctab, stab, ftab, qs, acc, top, den, ksc, hide, obuf,
    recv, send, precv, psend, qsem, osem, load, entered,
):
    me = lax.axis_index("seq")
    rows = k_hbm.shape[0]
    frames = rows // FRAME_TOK
    half = KVH // 2
    wide = half * HEAD
    qwide = QH * HEAD // 2
    core = me % 2
    y = (me // 2) % 2
    z = me // 4
    sib = me + 1 - 2 * core
    low = z < 2
    end = jnp.logical_or(z == 0, z == 3)
    mid = jnp.logical_not(end)

    def slot(a, b, c):
        return (a * 2 + b) * 2 + c

    def up(i):
        return jnp.where(low, i, 3 - i)

    Z0, Z1, Z2, Z3 = up(0), up(1), up(2), up(3)

    def to(s):
        return dict(device_id={"seq": s}, device_id_type=MESH)

    def part(c, size):
        return pl.ds(pl.multiple_of(c * size, size), size)

    barrier = pltpu.get_barrier_semaphore()

    def greet(i, _):
        other = lax.rem(me + i, n)

        @pl.when(other // 4 >= z)
        def _():
            pl.semaphore_signal(barrier, inc=1, **to(other))

        return 0

    def tell(i, _):
        other = lax.rem(me + i, n)

        @pl.when(other // 4 < z)
        def _():
            pl.semaphore_signal(entered.at[z], inc=1, **to(other))

        return 0

    def above(i):
        @pl.when(z + i < 4)
        def _():
            pl.semaphore_wait(entered.at[jnp.minimum(z + i, 3)], 4)

    lax.fori_loop(1, n, greet, 0)
    small = [
        pltpu.make_async_copy(src, dst, load.at[i])
        for i, (src, dst) in enumerate((
            (order_hbm, order_ref), (qb_hbm, qb_ref), (kb_hbm, kb_ref), (vb_hbm, vb_ref), (tab_hbm, tab_ref),
        ))
    ]
    mine = [
        pltpu.make_async_copy(k_hbm.at[:, part(core, wide)], kv.at[me], load.at[5]),
        pltpu.make_async_copy(v_hbm.at[:, part(core, wide)], kv.at[n + me], load.at[6]),
        pltpu.make_async_copy(q_hbm.at[:, part(core, qwide)], q_ref.at[0], load.at[7]),
    ]
    for c in small + mine:
        c.start()

    lane = lax.broadcasted_iota(jnp.int32, (1, HEAD), 1)
    group = lane // (HEAD // KVH)

    def row(ref):
        return ref[...].astype(jnp.float32)[None, :]

    def placed(values, at):
        return jnp.where(group == at % KVH, jnp.concatenate([values] * KVH, axis=1), 0.0)

    pl.semaphore_wait(barrier, 4 * z + 3)
    lax.fori_loop(1, n, tell, 0)

    def own(t, dz, dy, dc):
        return pltpu.make_async_remote_copy(
            src_ref=(k_hbm, v_hbm)[t].at[:, part(dc, wide)],
            dst_ref=kv.at[t * n + me],
            send_sem=send.at[0],
            recv_sem=recv.at[t * n + me],
            **to(slot(dz, dy, dc)),
        )

    def passed(t, s, dz, dy):
        return pltpu.make_async_remote_copy(
            src_ref=kv.at[t * n + s],
            dst_ref=kv.at[t * n + s],
            send_sem=send.at[1],
            recv_sem=recv.at[t * n + s],
            **to(slot(dz, dy, core)),
        )

    sent = [[0, 0] for _ in range(4)]

    def own_to(roles, t, dz, dy):
        for dc in (0, 1):
            own(t, dz, dy, dc).start()
        for r in roles:
            sent[r][0] += 2

    def pass_on(at, t, s, dz, dy):
        passed(t, s, dz, dy).start()
        sent[at][1] += 1

    def arrive(t, s):
        passed(t, s, z, y).wait_recv()

    def pack_copy(i, s):
        return pltpu.make_async_remote_copy(
            src_ref=pbuf.at[:, pl.ds(s, 1)],
            dst_ref=pbuf.at[:, pl.ds(s, 1)],
            send_sem=psend,
            recv_sem=precv.at[s],
            **to(lax.rem(me + i, n)),
        )

    def push(upward):
        def act(i, _):
            other = lax.rem(me + i, n)

            @pl.when(other // 4 > z if upward else other // 4 <= z)
            def _():
                pack_copy(i, me).start()

            return 0

        lax.fori_loop(1, n, act, 0)

    def ways(t):
        pl.when(z > 0)(lambda: own_to((1, 2, 3), t, z - 1, y))
        own_to((0, 1, 2, 3), t, z, 1 - y)

    ways(0)
    for c in small:
        c.wait()
    q_row = row(qb_ref)
    pbuf[0, pl.ds(me, 1), :] = q_row[:, :HEAD]
    pbuf[1, pl.ds(me, 1), :] = q_row[:, HEAD:]
    third = placed(row(kb_ref), me) + placed(row(vb_ref), me + 1)
    for f in range(frames):
        third = third + jnp.where(lane == (me + 2) % KVH * (HEAD // KVH) + f, order_ref[f].astype(jnp.float32), 0.0)
    pbuf[2, pl.ds(me, 1), :] = third
    ways(1)
    push(False)
    q_send = pltpu.make_async_remote_copy(
        src_ref=q_hbm.at[:, part(1 - core, qwide)], dst_ref=q_ref.at[1],
        send_sem=qsem.at[0], recv_sem=qsem.at[1], **to(sib),
    )
    q_send.start()
    for t in (0, 1):
        own(t, z, y, 1 - core).start()
        for r in sent:
            r[0] += 1

    ORDER = (1, 0)
    def role(plane, steps):
        def act():
            for t, s, targets in steps:
                arrive(t, s)
                for dz, dy in targets:
                    pass_on(plane, t, s, dz, dy)

        pl.when(z == plane)(act)

    def both(t, dz, dy, targets):
        return [(t, slot(dz, dy, k), targets) for k in ORDER]

    across = (z, 1 - y)

    def gather(t, dz, dy):
        for k in ORDER:
            arrive(t, slot(dz, dy, k))

    above(1)
    for t in (0, 1):
        pl.when(z < 3)(lambda: own_to((0, 1, 2), t, z + 1, y))
    near_y = (0, y), (1, y), (2, y), (3, y)
    role(0, both(0, 1, y, [across]))
    role(1, both(0, 2, y, [near_y[0], across]))
    role(2, both(0, 3, y, [near_y[1], across]))
    role(3, both(1, 3, 1 - y, [near_y[1], near_y[2]]))
    above(2)
    above(3)
    push(True)
    role(0, both(1, 0, 1 - y, [near_y[2], near_y[1]]) + both(1, 1, y, [across]))
    role(1, both(1, 2, y, [near_y[0], across]) + both(0, 0, y, [near_y[2], across]))
    role(2, both(1, 3, y, [near_y[1]]) + both(0, 1, y, [near_y[3], across]))
    role(3, both(0, 2, y, [across]) + both(1, 2, y, [across]))

    def pulled(i, _):
        pack_copy(i, lax.rem(me + i, n)).wait_recv()
        return 0

    lax.fori_loop(1, n, pulled, 0)
    tab = tab_ref[...]
    third = pbuf[2]
    at = lax.broadcasted_iota(jnp.int32, (n, HEAD), 0)
    spot = lax.broadcasted_iota(jnp.int32, (n, HEAD), 1) - (at + 2) % KVH * (HEAD // KVH)
    for f in range(frames):
        frame = jnp.sum(jnp.where(spot == f, third, 0.0), axis=1, keepdims=True)
        frame = jnp.broadcast_to(frame, (n, HEAD))
        cosine, sine = circle(frame * tab[32:33, :])
        ctab[f] = cosine * tab[33:34, :]
        stab[f] = sine * tab[34:35, :]
        ftab[f] = frame * FRAME_TOK

    def bias_row(g, turn):
        got = jnp.zeros((1, HEAD), jnp.float32)
        for i in range(KVH):
            piece = pbuf[2, pl.ds((core * half + g) * KVH + i, 1), :]
            got = got + jnp.where(group == (i + turn) % KVH, piece, 0.0)
        return got if turn == 0 else pltpu.roll(got, HEAD - turn * (HEAD // KVH), 1)

    k_bias = [bias_row(g, 0) for g in range(half)]
    v_bias = [bias_row(g, 1) for g in range(half)]

    def angles(s):
        cosines = [ctab[f, pl.ds(s, 1), :] + tab[0:16, :] for f in range(frames)]
        sines = [stab[f, pl.ds(s, 1), :] + tab[16:32, :] for f in range(frames)]
        return jnp.concatenate(cosines, axis=0), jnp.concatenate(sines, axis=0)

    fold = math.log2(math.e) / math.sqrt(HEAD)
    q_cos, q_sin, q_pos = [], [], []
    for s in (sib, me):
        cosine, sine = angles(s)
        q_cos.append(cosine * fold)
        q_sin.append(sine * fold)
        qpos = (lane % FRAME_TOK).astype(jnp.float32)
        for f in range(frames):
            qpos = qpos + jnp.where(lane % rows // FRAME_TOK == f, ftab[f, pl.ds(s, 1), :], 0.0)
        q_pos.append(qpos)
    blocks = RATIO * rows // HEAD
    within = lax.broadcasted_iota(jnp.int32, (FRAME_TOK, HEAD), 0).astype(jnp.float32)

    def turn_keys(first, count, at):
        for j in range(count):
            s = first + j
            cosine, sine = angles(s)
            for f in range(frames):
                kpos = ftab[f, pl.ds(s, 1), :] + within
                r = at + j * rows + f * FRAME_TOK
                for k in range(2):
                    hide[k, r : r + FRAME_TOK, :] = jnp.where(kpos <= q_pos[k], 0.0, NEG)
            for g in range(half):
                x = kv[s, :, g * HEAD : (g + 1) * HEAD].astype(jnp.float32) + k_bias[g]
                r = at + j * rows
                ksc[g, r : r + rows, :] = spin(x, cosine, sine).astype(jnp.bfloat16)

    def attend(g, k, first, count, at, fresh):
        keys = slice(at, at + count * rows)
        vals = kv[pl.ds(n + first, count), :, g * HEAD : (g + 1) * HEAD].reshape(count * rows, HEAD)
        mask = hide[k, keys, :]
        for b in range(k * blocks, (k + 1) * blocks):
            cols = slice(b * HEAD, (b + 1) * HEAD)
            scores = lax.dot_general(
                ksc[g, keys, :], qs[g, cols, :], (((1,), (1,)), ((), ())), preferred_element_type=jnp.float32
            )
            scores = scores + mask
            new = jnp.max(scores, axis=0, keepdims=True)
            if not fresh:
                old = top[g, :, cols]
                new = jnp.maximum(old, new)
            expo = jnp.exp2(scores - new)
            total = jnp.sum(expo, axis=0, keepdims=True)
            mixed = lax.dot_general(
                vals, expo.astype(jnp.bfloat16), (((0,), (0,)), ((), ())), preferred_element_type=jnp.float32
            )
            top[g, :, cols] = new
            if fresh:
                den[g, :, cols] = total
                acc[g, :, cols] = mixed
            else:
                factor = jnp.exp2(old - new)
                den[g, :, cols] = den[g, :, cols] * factor + total
                acc[g, :, cols] = acc[g, :, cols] * factor + mixed

    def plane(p, at, fresh):
        for g in range(half):
            for k in range(2):
                attend(g, k, p * 4, 4, at, fresh)

    mine[2].wait()
    q_send.wait_recv()
    for k in range(2):
        for h in range(QH // 2):
            bias = pbuf[h % 2, pl.ds(core * (n // 2) + h // 2, 1), :]
            x = q_ref[1 - k, :, h * HEAD : (h + 1) * HEAD].astype(jnp.float32) + bias
            r = (k * RATIO + h % RATIO) * rows
            qs[h // RATIO, r : r + rows, :] = spin(x, q_cos[k], q_sin[k]).astype(jnp.bfloat16)

    for c in mine[:2]:
        c.wait()
    arrive(0, sib)
    gather(0, z, 1 - y)
    turn_keys(z * 4, 4, 0)
    arrive(1, sib)
    near = jnp.where(end, Z1, Z0)
    role(0, both(0, 2, y, [across]))
    role(1, both(0, 3, y, [near_y[0], across]) + both(1, 0, y, [near_y[2]]))
    role(2, both(1, 1, y, [near_y[3], across]) + both(0, 0, y, [near_y[3], across]))
    role(3, both(0, 1, y, [across]))
    pl.when(mid)(lambda: gather(1, z, 1 - y))
    plane(z, 0, True)
    gather(0, near, 1 - y)
    turn_keys(near * 4, 4, 4 * rows)
    role(0, both(1, 2, y, [across]))
    role(1, both(1, 3, y, [near_y[0]]))
    role(2, both(1, 0, y, [near_y[3]]))
    role(3, both(1, 1, y, [across]))
    gather(1, near, 1 - y)
    plane(near, 4 * rows, False)
    role(0, both(0, 3, y, [across]))
    role(1, both(1, 3, 1 - y, [near_y[0]]))
    role(2, both(1, 0, 1 - y, [near_y[3]]))
    role(3, both(0, 0, y, [across]))
    gather(0, Z2, 1 - y)
    turn_keys(Z2 * 4, 4, 8 * rows)
    gather(1, Z2, 1 - y)
    plane(Z2, 8 * rows, False)
    gather(0, Z3, 1 - y)
    turn_keys(Z3 * 4, 4, 12 * rows)
    role(0, both(1, 3, y, []) + both(1, 3, 1 - y, []))
    role(3, both(1, 0, y, []) + both(1, 0, 1 - y, []))

    out = []
    for k in range(2):
        for g in range(half):
            attend(g, k, Z3 * 4, 4, 12 * rows, False)
            for b in range(blocks):
                cols = slice((k * blocks + b) * HEAD, (k * blocks + b + 1) * HEAD)
                mixed = acc[g, :, cols] * (1.0 / den[g, :, cols])
                flat = (mixed.T + v_bias[g]).astype(jnp.bfloat16)
                for i in range(HEAD // rows):
                    h = b * (HEAD // rows) + i
                    piece = flat[i * rows : (i + 1) * rows, :]
                    if k == 0:
                        obuf[g, :, h * HEAD : (h + 1) * HEAD] = piece
                    else:
                        at = core * qwide + (g * RATIO + h) * HEAD
                        o_ref[:, pl.ds(pl.multiple_of(at, HEAD), HEAD)] = piece
            if k == 0:
                at = core * qwide + g * RATIO * HEAD
                c = pltpu.make_async_remote_copy(
                    src_ref=obuf.at[g],
                    dst_ref=o_ref.at[:, pl.ds(pl.multiple_of(at, HEAD), RATIO * HEAD)],
                    send_sem=osem.at[g], recv_sem=osem.at[half + g], **to(sib),
                )
                c.start()
                out.append(c)

    def drain(at):
        def act():
            for i in range(2):
                size = kv.at[pl.ds(0, sent[at][i])]
                pltpu.make_async_copy(size, size, send.at[i]).wait()

        return act

    for plane_at in range(4):
        pl.when(z == plane_at)(drain(plane_at))
    size = pbuf.at[:, pl.ds(0, n - 1)]
    pltpu.make_async_copy(size, size, psend).wait()
    q_send.wait_send()
    for c in out:
        c.wait()


def on_line(n, query, keys, values, query_bias, key_bias, value_projection_bias, frame_order):
    rows = keys.shape[0]
    half = KVH // 2
    frames = rows // FRAME_TOK
    wide = RATIO * 2 * rows
    return pl.pallas_call(
        functools.partial(line_kernel, n),
        out_shape=jax.ShapeDtypeStruct(query.shape, jnp.bfloat16),
        in_specs=[pl.BlockSpec(memory_space=pltpu.HBM)] * 8,
        out_specs=pl.BlockSpec(memory_space=pltpu.VMEM),
        scratch_shapes=[
            pltpu.VMEM(query_bias.shape, jnp.bfloat16),
            pltpu.VMEM(key_bias.shape, jnp.bfloat16),
            pltpu.VMEM(key_bias.shape, jnp.bfloat16),
            pltpu.SMEM(frame_order.shape, jnp.int32),
            pltpu.VMEM((40, HEAD), jnp.float32),
            pltpu.VMEM((2, rows, QH * HEAD // 2), jnp.bfloat16),
            pltpu.VMEM((2 * n, rows, half * HEAD), jnp.bfloat16),
            pltpu.VMEM((3, n, HEAD), jnp.float32),
            pltpu.VMEM((frames, n, HEAD), jnp.float32),
            pltpu.VMEM((frames, n, HEAD), jnp.float32),
            pltpu.VMEM((frames, n, HEAD), jnp.float32),
            pltpu.VMEM((half, wide, HEAD), jnp.bfloat16),
            pltpu.VMEM((half, HEAD, wide), jnp.float32),
            pltpu.VMEM((half, 1, wide), jnp.float32),
            pltpu.VMEM((half, 1, wide), jnp.float32),
            pltpu.VMEM((half, n * rows, HEAD), jnp.bfloat16),
            pltpu.VMEM((2, n * rows, HEAD), jnp.float32),
            pltpu.VMEM((half, rows, RATIO * HEAD), jnp.bfloat16),
            pltpu.SemaphoreType.DMA((2 * n,)),
            pltpu.SemaphoreType.DMA((2,)),
            pltpu.SemaphoreType.DMA((n,)),
            pltpu.SemaphoreType.DMA,
            pltpu.SemaphoreType.DMA((2,)),
            pltpu.SemaphoreType.DMA((2 * half,)),
            pltpu.SemaphoreType.DMA((8,)),
            pltpu.SemaphoreType.REGULAR((4,)),
        ],
        compiler_params=pltpu.CompilerParams(vmem_limit_bytes=24 << 20, collective_id=1, has_side_effects=True),
    )(*(
        pltpu.with_memory_space_constraint(x, pltpu.HBM)
        for x in (
            query, keys, values, query_bias, key_bias, value_projection_bias, frame_order,
            jnp.asarray(line_tables()),
        )
    ))


def on_device(n, query, keys, values, query_bias, key_bias, value_projection_bias, frame_order):
    chips = n // 2
    B = 1
    while B * B * 4 <= chips:
        B *= 2
    A = chips // B
    rows = keys.shape[0]
    qper = query_bias.shape[0]
    wide = RATIO * rows
    keys_at_once = 4 * rows
    whole = pl.BlockSpec(memory_space=pltpu.VMEM)
    far = pl.BlockSpec(memory_space=pltpu.HBM)
    return pl.pallas_call(
        functools.partial(kernel, A, B, n, qper),
        out_shape=jax.ShapeDtypeStruct(query.shape, jnp.bfloat16),
        in_specs=[far] * 8,
        out_specs=whole,
        scratch_shapes=[
            pltpu.VMEM(query_bias.shape, jnp.bfloat16),
            pltpu.VMEM(key_bias.shape, jnp.bfloat16),
            pltpu.VMEM(key_bias.shape, jnp.bfloat16),
            pltpu.SMEM(frame_order.shape, jnp.int32),
            pltpu.VMEM((40, HEAD), jnp.float32),
            pltpu.VMEM(query.shape, jnp.bfloat16),
            pltpu.VMEM((8, HEAD), jnp.float32),
            pltpu.VMEM((n, rows, KVH * HEAD), jnp.bfloat16),
            pltpu.VMEM((n, rows, KVH * HEAD), jnp.bfloat16),
            pltpu.VMEM((n, 8, HEAD), jnp.float32),
            pltpu.VMEM((KVH, wide, HEAD), jnp.bfloat16),
            pltpu.VMEM((KVH, HEAD, wide), jnp.float32),
            pltpu.VMEM((KVH, 1, wide), jnp.float32),
            pltpu.VMEM((KVH, 1, wide), jnp.float32),
            pltpu.VMEM((KVH, keys_at_once, HEAD), jnp.bfloat16),
            pltpu.VMEM((KVH, keys_at_once, HEAD), jnp.bfloat16),
            pltpu.VMEM((keys_at_once, HEAD), jnp.float32),
            pltpu.SemaphoreType.DMA((PIECES, n)),
            pltpu.SemaphoreType.DMA((PIECES, 5, n)),
            pltpu.SemaphoreType.DMA((n,)),
            pltpu.SemaphoreType.DMA((n,)),
            pltpu.SemaphoreType.DMA((8,)),
        ],
        compiler_params=pltpu.CompilerParams(vmem_limit_bytes=(16 if n <= 32 else 48) << 20, collective_id=0, has_side_effects=True),
    )(*(
        pltpu.with_memory_space_constraint(x, pltpu.HBM)
        for x in (
            query, keys, values, query_bias, key_bias, value_projection_bias, frame_order,
            jnp.asarray(tables()),
        )
    ))


def solution(mesh):
    placed = (
        P(("groups", "seq"), None),
        P(("groups", "seq"), None),
        P(("groups", "seq"), None),
        P("seq"),
        P("seq"),
        P("seq"),
        P(("groups", "seq")),
    )
    n = mesh.shape["seq"]
    return jax.shard_map(
        functools.partial(on_line if n == 16 else on_device, n),
        mesh=mesh,
        in_specs=placed,
        out_specs=P(("groups", "seq"), None),
        check_vma=False,
    )
```

```python
import functools
import math

import jax
import jax.numpy as jnp
import numpy as np
from jax import lax
from jax.experimental import pallas as pl
from jax.experimental.pallas import tpu as pltpu
from jax.sharding import PartitionSpec as P

HEAD = 128
HALF = HEAD // 2
QH = 32
KVH = 4
RATIO = QH // KVH
GRID = 4
FRAME_TOK = 16
MESH = pl.DeviceIdType.MESH
NEG = -1e30
PIECES = 2
PAIRS_T = HALF // 4
PAIRS_R = HALF // 4 + 3 * HALF // 8


def tables():
    pair = np.arange(HEAD) % HALF
    freq = np.exp(-(2.0 * pair / HEAD) * math.log(1000000.0))
    tok = np.arange(FRAME_TOK)
    source = np.where(pair[None, :] < PAIRS_R, (tok // GRID)[:, None], (tok % GRID)[:, None])
    angle = source * freq[None, :]
    sign = np.where(np.arange(HEAD) < HALF, -1.0, 1.0)
    rows = np.zeros((40, HEAD), np.float32)
    rows[0:16] = np.cos(angle)
    rows[16:32] = np.sin(angle) * sign[None, :]
    rows[32] = 2.0 * freq
    return rows


def cos_sin(frames, spatial):
    angle = frames * spatial[32:33, :]
    turns = jnp.round(angle * (1.0 / (2.0 * math.pi)))
    angle = angle - turns * 6.28125
    angle = angle - turns * (2.0 * math.pi - 6.28125)
    lane = lax.broadcasted_iota(jnp.int32, (FRAME_TOK, HEAD), 1)
    temporal = lane % HALF < PAIRS_T
    sign = jnp.where(lane < HALF, -1.0, 1.0)
    cos_t, sin_t = jnp.cos(angle), jnp.sin(angle)
    cosines, sines = [], []
    for j in range(frames.shape[0]):
        cosines.append(jnp.where(temporal, cos_t[j : j + 1, :], spatial[0:16, :]))
        sines.append(jnp.where(temporal, sin_t[j : j + 1, :] * sign, spatial[16:32, :]))
    return jnp.concatenate(cosines, axis=0), jnp.concatenate(sines, axis=0)


def spin(x, cosine, sine):
    return x * cosine + pltpu.roll(x, HALF, 1) * sine


def kernel(
    A, B, n, qper,
    q_hbm, k_hbm, v_hbm, qb_hbm, kb_hbm, vb_hbm, order_hbm, tab_hbm,
    o_ref,
    qb_ref, kb_ref, vb_ref, order_ref, tab_ref,
    q_ref, pack_ref, kbuf, vbuf, pbuf, qs, acc, top, den, ksc, vsc, hide,
    recv, send, precv, psend, load,
):
    me = lax.axis_index("seq")
    rows = kbuf.shape[1]
    frames = rows // FRAME_TOK
    cut = rows // (PIECES // 2)
    core = me % 2
    b = (me // 2) % B
    a = me // (2 * B)

    def piece(p, s):
        return (kbuf, vbuf)[p % 2].at[s, pl.ds((p // 2) * cut, cut)]

    def slot(x, y, z):
        return (x * B + y) * 2 + z

    ways = (
        (a + 1 < A, slot(a + 1, b, core)),
        (a > 0, slot(a - 1, b, core)),
        (b + 1 < B, slot(a, b + 1, core)),
        (b > 0, slot(a, b - 1, core)),
        (None, slot(a, b, 1 - core)),
    )

    def copy(t, s, way):
        return pltpu.make_async_remote_copy(
            src_ref=piece(t, s),
            dst_ref=piece(t, s),
            send_sem=send.at[t, way, s],
            recv_sem=recv.at[t, s],
            device_id={"seq": ways[way][1]},
            device_id_type=MESH,
        )

    def when(cond, act):
        if cond is None:
            act()
        else:
            pl.when(cond)(act)

    def fan(t, s, dirs, start):
        for way in dirs:
            c = copy(t, s, way)
            when(ways[way][0], c.start if start else c.wait_send)

    def arrive(t, s):
        copy(t, s, 4).wait_recv()

    def inside(i, size):
        return jnp.logical_and(i >= 0, i < size)

    def along_a(d, start):
        for t in range(PIECES):
            for sg in (1, -1):
                x = a + sg * d

                @pl.when(jnp.logical_and(inside(x, A), d < A))
                def _(x=x, sg=sg, t=t):
                    s = slot(x, b, core)
                    if start:
                        arrive(t, s)
                    fan(t, s, (1 if sg > 0 else 0, 2, 3, 4), start)

    def along_b(d, start):
        for e in range(1, B):
            for t in range(PIECES):
                for sg in (1, -1):
                    x = a + sg * d
                    ok = inside(x, A) if sg > 0 else jnp.logical_and(inside(x, A), d > 0)
                    for sb in (1, -1):
                        y = b + sb * e

                        @pl.when(jnp.logical_and(ok, inside(y, B)))
                        def _(x=x, y=y, sb=sb, t=t):
                            s = slot(x, y, core)
                            if start:
                                arrive(t, s)
                            fan(t, s, (3 if sb > 0 else 2, 4), start)

    barrier = pltpu.get_barrier_semaphore()

    def greet(i, _):
        pl.semaphore_signal(barrier, inc=1, device_id={"seq": lax.rem(me + i, n)}, device_id_type=MESH)
        return 0

    lax.fori_loop(1, n, greet, 0)
    k_load = pltpu.make_async_copy(k_hbm, kbuf.at[me], load.at[0])
    v_load = pltpu.make_async_copy(v_hbm, vbuf.at[me], load.at[1])
    q_load = pltpu.make_async_copy(q_hbm, q_ref, load.at[2])
    small = [
        pltpu.make_async_copy(src, dst, load.at[3 + i])
        for i, (src, dst) in enumerate((
            (order_hbm, order_ref), (qb_hbm, qb_ref), (kb_hbm, kb_ref), (vb_hbm, vb_ref), (tab_hbm, tab_ref),
        ))
    ]
    for c in small + [k_load, v_load, q_load]:
        c.start()

    lane = lax.broadcasted_iota(jnp.int32, (1, HEAD), 1)

    def placed(values):
        size = values.shape[1]
        spots = HEAD // size
        return jnp.where(lane // size == me % spots, jnp.concatenate([values] * spots, axis=1), 0.0)

    def row(ref):
        return ref[...].astype(jnp.float32)[None, :]

    for c in small:
        c.wait()
    pack_ref[...] = jnp.zeros_like(pack_ref)
    q_row = row(qb_ref)
    if qper >= HEAD:
        for i in range(qper // HEAD):
            pack_ref[i : i + 1, :] = q_row[:, i * HEAD : (i + 1) * HEAD]
    else:
        pack_ref[0:1, :] = placed(q_row)
    pack_ref[2:3, :] = placed(row(kb_ref))
    pack_ref[3:4, :] = placed(row(vb_ref))
    qpos = (lane % FRAME_TOK).astype(jnp.float32)
    for f in range(frames):
        frame = order_ref[f].astype(jnp.float32)
        pack_ref[8 - frames + f : 9 - frames + f, :] = jnp.full((1, HEAD), 1.0, jnp.float32) * frame
        qpos = qpos + jnp.where((lane % rows) // FRAME_TOK == f, frame * FRAME_TOK, 0.0)
    pbuf[me] = pack_ref[...]
    tab = tab_ref[...]
    q_cos, q_sin = cos_sin(pack_ref[8 - frames :, :], tab)
    fold = math.log2(math.e) / math.sqrt(HEAD)
    q_cos, q_sin = q_cos * fold, q_sin * fold
    k_load.wait()
    v_load.wait()
    pl.semaphore_wait(barrier, n - 1)

    def pack_copy(i, s):
        return pltpu.make_async_remote_copy(
            src_ref=pack_ref,
            dst_ref=pbuf.at[s],
            send_sem=psend.at[i],
            recv_sem=precv.at[s],
            device_id={"seq": lax.rem(me + i, n)},
            device_id_type=MESH,
        )

    def push(i, _):
        pack_copy(i, me).start()
        return 0

    lax.fori_loop(1, n, push, 0)
    for t in range(PIECES):
        fan(t, me, (0, 1, 2, 3, 4), True)

    acc[...] = jnp.zeros_like(acc)
    den[...] = jnp.zeros_like(den)
    top[...] = jnp.full_like(top, NEG)

    def pulled(i, _):
        pack_copy(i, lax.rem(me + i, n)).wait_recv()
        return 0

    lax.fori_loop(1, n, pulled, 0)
    q_load.wait()

    for h in range(QH):
        if qper >= HEAD:
            per = qper // HEAD
            bias = pbuf[h // per, h % per : h % per + 1, :]
        else:
            parts = HEAD // qper
            bias = sum(pbuf[h * parts + i, 0:1, :] for i in range(parts))
        x = q_ref[:, h * HEAD : (h + 1) * HEAD].astype(jnp.float32) + bias
        at = (h % RATIO) * rows
        qs[h // RATIO, at : at + rows, :] = spin(x, q_cos, q_sin).astype(jnp.bfloat16)
    share = n // KVH
    k_bias = [sum(pbuf[g * share + i, 2:3, :] for i in range(share)) for g in range(KVH)]
    v_bias = [sum(pbuf[g * share + i, 3:4, :] for i in range(share)) for g in range(KVH)]
    within = lax.broadcasted_iota(jnp.int32, (FRAME_TOK, HEAD), 0).astype(jnp.float32)

    def chunk(first):
        for j in range(4):
            s = first + j
            order = pbuf[s][8 - frames :, :]
            cosine, sine = cos_sin(order, tab)
            for f in range(frames):
                kpos = order[f : f + 1, :] * FRAME_TOK + within
                at = j * rows + f * FRAME_TOK
                hide[at : at + FRAME_TOK, :] = jnp.where(kpos <= qpos, 0.0, NEG)
            for g in range(KVH):
                cols = slice(g * HEAD, (g + 1) * HEAD)
                x = kbuf[s, :, cols].astype(jnp.float32) + k_bias[g]
                ksc[g, j * rows : (j + 1) * rows, :] = spin(x, cosine, sine).astype(jnp.bfloat16)
                y = vbuf[s, :, cols].astype(jnp.float32) + v_bias[g]
                vsc[g, j * rows : (j + 1) * rows, :] = y.astype(jnp.bfloat16)
        for g in range(KVH):
            scores = lax.dot_general(
                ksc[g], qs[g], (((1,), (1,)), ((), ())), preferred_element_type=jnp.float32
            )
            mask = hide[...]
            scores = scores + jnp.concatenate([mask] * (scores.shape[1] // HEAD), axis=1)
            old = top[g]
            new = jnp.maximum(old, jnp.max(scores, axis=0, keepdims=True))
            expo = jnp.exp2(scores - new)
            factor = jnp.exp2(old - new)
            top[g] = new
            den[g] = den[g] * factor + jnp.sum(expo, axis=0, keepdims=True)
            acc[g] = acc[g] * factor + lax.dot_general(
                vsc[g], expo.astype(jnp.bfloat16), (((0,), (0,)), ((), ())),
                preferred_element_type=jnp.float32,
            )

    low = a < A // 2
    mirror = jnp.where(low, a, A - 1 - a)

    def step(d, _):
        along_a(d + 1, True)
        along_b(d, True)
        near = jnp.where(d % 2 == 1, -((d + 1) // 2), d // 2)
        plane = mirror + jnp.where(d <= 2 * mirror, near, d - mirror)
        plane = jnp.where(low, plane, A - 1 - plane)
        for y in range(B):
            for t in range(PIECES):
                arrive(t, slot(plane, y, 1 - core))
        if 2 * B == 4:
            chunk(plane * 4)
        else:
            def part(i, _):
                chunk(plane * 2 * B + i * 4)
                return 0

            lax.fori_loop(0, 2 * B // 4, part, 0)
        return 0

    lax.fori_loop(0, A, step, 0)

    for g in range(KVH):
        mixed = acc[g] * (1.0 / den[g])
        flat = mixed.T.astype(jnp.bfloat16)
        for r in range(RATIO):
            h = g * RATIO + r
            o_ref[:, h * HEAD : (h + 1) * HEAD] = flat[r * rows : (r + 1) * rows, :]

    for t in range(PIECES):
        fan(t, me, (0, 1, 2, 3, 4), False)

    def drain(d, _):
        along_a(d + 1, False)
        along_b(d, False)
        return 0

    lax.fori_loop(0, A, drain, 0)

    def pushed(i, _):
        pack_copy(i, me).wait_send()
        return 0

    lax.fori_loop(1, n, pushed, 0)


def line_tables():
    rows = tables()
    pair = np.arange(HEAD) % HALF
    temporal = pair < PAIRS_T
    rows[0:32, temporal] = 0.0
    rows[32] = np.where(temporal, rows[32], 0.0)
    rows[33] = np.where(temporal, 1.0, 0.0)
    rows[34] = np.where(temporal, np.where(np.arange(HEAD) < HALF, -1.0, 1.0), 0.0)
    return rows


def circle(x):
    k = jnp.round(x * (2.0 / math.pi))
    r = x - k * 1.5703125
    r = r - k * (math.pi / 2.0 - 1.5703125)
    w = r * r
    s = r + r * w * (-1.6666654611e-1 + w * (8.3321608736e-3 - w * 1.9515295891e-4))
    c = 1.0 - 0.5 * w + w * w * (4.166664568298827e-2 + w * (-1.388731625493765e-3 + w * 2.443315711809948e-5))
    turn = k - 4.0 * jnp.floor(k * 0.25)
    odd = jnp.logical_or(turn == 1.0, turn == 3.0)
    cosine = jnp.where(odd, s, c)
    sine = jnp.where(odd, c, s)
    cosine = jnp.where(jnp.logical_or(turn == 1.0, turn == 2.0), -cosine, cosine)
    sine = jnp.where(turn >= 2.0, -sine, sine)
    return cosine, sine


def line_kernel(
    n,
    q_hbm, k_hbm, v_hbm, qb_hbm, kb_hbm, vb_hbm, order_hbm, tab_hbm,
    o_ref,
    qb_ref, kb_ref, vb_ref, order_ref, tab_ref,
    q_ref, kv, pbuf, ctab, stab, ftab, qs, acc, top, den, ksc, hide, obuf,
    recv, send, precv, psend, qsem, osem, load, entered,
):
    me = lax.axis_index("seq")
    rows = k_hbm.shape[0]
    frames = rows // FRAME_TOK
    half = KVH // 2
    wide = half * HEAD
    qwide = QH * HEAD // 2
    core = me % 2
    y = (me // 2) % 2
    z = me // 4
    sib = me + 1 - 2 * core
    low = z < 2
    end = jnp.logical_or(z == 0, z == 3)
    mid = jnp.logical_not(end)

    def slot(a, b, c):
        return (a * 2 + b) * 2 + c

    def up(i):
        return jnp.where(low, i, 3 - i)

    Z0, Z1, Z2, Z3 = up(0), up(1), up(2), up(3)

    def to(s):
        return dict(device_id={"seq": s}, device_id_type=MESH)

    def part(c, size):
        return pl.ds(pl.multiple_of(c * size, size), size)

    barrier = pltpu.get_barrier_semaphore()

    def greet(other, _):
        @pl.when(other != me)
        def _():
            pl.semaphore_signal(barrier, inc=1, **to(other))

        return 0

    def tell(other, _):
        pl.semaphore_signal(entered.at[z], inc=1, **to(other))
        return 0

    def above(i):
        @pl.when(z + i < 4)
        def _():
            pl.semaphore_wait(entered.at[jnp.minimum(z + i, 3)], 4)

    lax.fori_loop(4 * z, n, greet, 0)
    small = [
        pltpu.make_async_copy(src, dst, load.at[i])
        for i, (src, dst) in enumerate((
            (order_hbm, order_ref), (qb_hbm, qb_ref), (kb_hbm, kb_ref), (vb_hbm, vb_ref), (tab_hbm, tab_ref),
        ))
    ]
    mine = [
        pltpu.make_async_copy(k_hbm.at[:, part(core, wide)], kv.at[me], load.at[5]),
        pltpu.make_async_copy(v_hbm.at[:, part(core, wide)], kv.at[n + me], load.at[6]),
        pltpu.make_async_copy(q_hbm.at[:, part(core, qwide)], q_ref.at[0], load.at[7]),
    ]
    for c in small + mine:
        c.start()

    lane = lax.broadcasted_iota(jnp.int32, (1, HEAD), 1)
    group = lane // (HEAD // KVH)

    def row(ref):
        return ref[...].astype(jnp.float32)[None, :]

    def placed(values, at):
        return jnp.where(group == at % KVH, jnp.concatenate([values] * KVH, axis=1), 0.0)

    pl.semaphore_wait(barrier, 4 * z + 3)

    def own(t, dz, dy, dc, relay=False):
        at = (2 + t if relay else t) * n + me
        return pltpu.make_async_remote_copy(
            src_ref=(k_hbm, v_hbm)[t].at[:, part(dc, wide)],
            dst_ref=kv.at[at],
            send_sem=send.at[0],
            recv_sem=recv.at[at],
            **to(slot(dz, dy, 1 if relay else dc)),
        )

    def passed(source, target, s):
        return pltpu.make_async_remote_copy(
            src_ref=kv.at[source],
            dst_ref=kv.at[target],
            send_sem=send.at[1],
            recv_sem=recv.at[target],
            **to(s),
        )

    sent = [[0, 0] for _ in range(4)]

    def own_to(planes, t, dz, dy, relay):
        for dc in (0, 1):
            own(t, dz, dy, dc, relay and dc == 0).start()
        for p in planes:
            sent[p][0] += 2

    def arrive(t, s):
        passed(t * n + s, t * n + s, sib).wait_recv()

    def pack_copy(i, s):
        return pltpu.make_async_remote_copy(
            src_ref=pbuf.at[:, pl.ds(s, 1)],
            dst_ref=pbuf.at[:, pl.ds(s, 1)],
            send_sem=psend,
            recv_sem=precv.at[s],
            **to(lax.rem(me + i, n)),
        )

    def push(upward):
        def act(other, _):
            @pl.when(other != me)
            def _():
                pack_copy(other - me + n, me).start()

            return 0

        lax.fori_loop(*((4 * z + 4, n) if upward else (0, 4 * z + 4)), act, 0)

    def ways(t):
        pl.when(z > 0)(lambda: own_to((1, 2, 3), t, z - 1, y, True))
        if t == 0:
            own_to((0, 1, 2, 3), t, z, 1 - y, False)
        else:
            pl.when(end)(lambda: own_to((0, 3), t, z, 1 - y, True))
            pl.when(mid)(lambda: own_to((1, 2), t, z, 1 - y, False))

    ways(0)
    lax.fori_loop(0, 4 * z, tell, 0)
    for c in small:
        c.wait()
    q_row = row(qb_ref)
    pbuf[0, pl.ds(me, 1), :] = q_row[:, :HEAD]
    pbuf[1, pl.ds(me, 1), :] = q_row[:, HEAD:]
    third = placed(row(kb_ref), me) + placed(row(vb_ref), me + 1)
    for f in range(frames):
        third = third + jnp.where(lane == (me + 2) % KVH * (HEAD // KVH) + f, order_ref[f].astype(jnp.float32), 0.0)
    pbuf[2, pl.ds(me, 1), :] = third
    ways(1)
    push(False)
    q_send = pltpu.make_async_remote_copy(
        src_ref=q_hbm.at[:, part(1 - core, qwide)], dst_ref=q_ref.at[1],
        send_sem=qsem.at[0], recv_sem=qsem.at[1], **to(sib),
    )
    q_send.start()
    for t in (0, 1):
        own(t, z, y, 1 - core).start()
        for r in sent:
            r[0] += 1

    ORDER = (1, 0)
    def role(plane, steps):
        def forward():
            for t, s, targets in steps:
                for kind in (2 + t, t):
                    source = kind * n + s
                    passed(source, source, sib).wait_recv()
                    for dz, dy, relay in targets:
                        if kind == t or relay:
                            passed(source, source, slot(dz, dy, 1)).start()
                        else:
                            passed(source, t * n + s, slot(dz, dy, 0)).start()
                        sent[plane][1] += 1
                    if kind != t:
                        passed(source, t * n + s, sib).start()
                        sent[plane][1] += 1

        def take():
            for t, s, _ in steps:
                arrive(t, s)

        pl.when(jnp.logical_and(z == plane, core == 1))(forward)
        pl.when(jnp.logical_and(z == plane, core == 0))(take)

    def both(t, dz, dy, targets):
        return [(t, slot(dz, dy, k), targets) for k in ORDER]

    across = (z, 1 - y, False)

    def gather(t, dz, dy):
        for k in ORDER:
            arrive(t, slot(dz, dy, k))

    above(1)
    for t in (0, 1):
        pl.when(z < 3)(lambda: own_to((0, 1, 2), t, z + 1, y, True))
    relay = [(p, y, True) for p in range(4)]
    last = [(p, y, False) for p in range(4)]
    role(0, both(0, 1, y, [across]))
    role(1, both(0, 2, y, [relay[0], across]))
    role(2, both(0, 3, y, [relay[1], across]))
    role(3, both(1, 3, 1 - y, [relay[1], last[2]]))
    above(2)
    above(3)
    push(True)
    role(0, both(1, 0, 1 - y, [relay[2], last[1]]) + both(1, 1, y, [across]))
    role(1, both(1, 2, y, [relay[0], across]) + both(0, 0, y, [relay[2], across]))
    role(2, both(1, 3, y, [relay[1]]) + both(0, 1, y, [relay[3], across]))
    role(3, both(0, 2, y, [across]) + both(1, 2, y, [across]))

    def pulled(i, _):
        pack_copy(i, lax.rem(me + i, n)).wait_recv()
        return 0

    lax.fori_loop(1, n, pulled, 0)
    tab = tab_ref[...]
    third = pbuf[2]
    at = lax.broadcasted_iota(jnp.int32, (n, HEAD), 0)
    spot = lax.broadcasted_iota(jnp.int32, (n, HEAD), 1) - (at + 2) % KVH * (HEAD // KVH)
    for f in range(frames):
        frame = jnp.sum(jnp.where(spot == f, third, 0.0), axis=1, keepdims=True)
        frame = jnp.broadcast_to(frame, (n, HEAD))
        cosine, sine = circle(frame * tab[32:33, :])
        ctab[f] = cosine * tab[33:34, :]
        stab[f] = sine * tab[34:35, :]
        ftab[f] = frame * FRAME_TOK

    def bias_row(g, turn):
        got = jnp.zeros((1, HEAD), jnp.float32)
        for i in range(KVH):
            piece = pbuf[2, pl.ds((core * half + g) * KVH + i, 1), :]
            got = got + jnp.where(group == (i + turn) % KVH, piece, 0.0)
        return got if turn == 0 else pltpu.roll(got, HEAD - turn * (HEAD // KVH), 1)

    k_bias = [bias_row(g, 0) for g in range(half)]
    v_bias = [bias_row(g, 1) for g in range(half)]

    def angles(s):
        cosines = [ctab[f, pl.ds(s, 1), :] + tab[0:16, :] for f in range(frames)]
        sines = [stab[f, pl.ds(s, 1), :] + tab[16:32, :] for f in range(frames)]
        return jnp.concatenate(cosines, axis=0), jnp.concatenate(sines, axis=0)

    fold = math.log2(math.e) / math.sqrt(HEAD)
    q_cos, q_sin, q_pos = [], [], []
    for s in (sib, me):
        cosine, sine = angles(s)
        q_cos.append(cosine * fold)
        q_sin.append(sine * fold)
        qpos = (lane % FRAME_TOK).astype(jnp.float32)
        for f in range(frames):
            qpos = qpos + jnp.where(lane % rows // FRAME_TOK == f, ftab[f, pl.ds(s, 1), :], 0.0)
        q_pos.append(qpos)
    blocks = RATIO * rows // HEAD
    within = lax.broadcasted_iota(jnp.int32, (FRAME_TOK, HEAD), 0).astype(jnp.float32)

    def turn_keys(first, count, at):
        for j in range(count):
            s = first + j
            cosine, sine = angles(s)
            for f in range(frames):
                kpos = ftab[f, pl.ds(s, 1), :] + within
                r = at + j * rows + f * FRAME_TOK
                for k in range(2):
                    hide[k, r : r + FRAME_TOK, :] = jnp.where(kpos <= q_pos[k], 0.0, NEG)
            for g in range(half):
                x = kv[s, :, g * HEAD : (g + 1) * HEAD].astype(jnp.float32) + k_bias[g]
                r = at + j * rows
                ksc[g, r : r + rows, :] = spin(x, cosine, sine).astype(jnp.bfloat16)

    def attend(g, k, spans, at, fresh, finish=None):
        vals = jnp.concatenate([
            kv[pl.ds(n + first, count), :, g * HEAD : (g + 1) * HEAD].reshape(count * rows, HEAD)
            for first, count in spans
        ], axis=0)
        keys = slice(at, at + vals.shape[0])
        mask = hide[k, keys, :]
        for b in range(k * blocks, (k + 1) * blocks):
            cols = slice(b * HEAD, (b + 1) * HEAD)
            scores = lax.dot_general(
                ksc[g, keys, :], qs[g, cols, :], (((1,), (1,)), ((), ())), preferred_element_type=jnp.float32
            )
            scores = scores + mask
            new = jnp.max(scores, axis=0, keepdims=True)
            if not fresh:
                old = top[g, :, cols]
                new = jnp.maximum(old, new)
            expo = jnp.exp2(scores - new)
            total = jnp.sum(expo, axis=0, keepdims=True)
            mixed = lax.dot_general(
                vals, expo.astype(jnp.bfloat16), (((0,), (0,)), ((), ())), preferred_element_type=jnp.float32
            )
            if finish is not None:
                factor = jnp.exp2(old - new)
                scale = 1.0 / (den[g, :, cols] * factor + total)
                finish(b - k * blocks, (acc[g, :, cols] * factor + mixed) * scale)
                continue
            top[g, :, cols] = new
            if fresh:
                den[g, :, cols] = total
                acc[g, :, cols] = mixed
            else:
                factor = jnp.exp2(old - new)
                den[g, :, cols] = den[g, :, cols] * factor + total
                acc[g, :, cols] = acc[g, :, cols] * factor + mixed

    def chunk(spans, at, fresh):
        for g in range(half):
            for k in range(2):
                attend(g, k, spans, at, fresh)

    mine[2].wait()
    q_send.wait_recv()
    for k in range(2):
        for h in range(QH // 2):
            bias = pbuf[h % 2, pl.ds(core * (n // 2) + h // 2, 1), :]
            x = q_ref[1 - k, :, h * HEAD : (h + 1) * HEAD].astype(jnp.float32) + bias
            r = (k * RATIO + h % RATIO) * rows
            qs[h // RATIO, r : r + rows, :] = spin(x, q_cos[k], q_sin[k]).astype(jnp.bfloat16)

    for c in mine[:2]:
        c.wait()
    arrive(0, sib)
    gather(0, z, 1 - y)
    turn_keys(z * 4, 4, 0)
    arrive(1, sib)
    near = jnp.where(end, Z1, Z0)
    role(0, both(0, 2, y, [across]))
    role(1, both(0, 3, y, [relay[0], across]) + both(1, 0, y, [relay[2]]))
    role(2, both(1, 1, y, [relay[3], across]) + both(0, 0, y, [relay[3], across]))
    role(3, both(0, 1, y, [across]))
    pl.when(mid)(lambda: gather(1, z, 1 - y))
    chunk([(z * 4, 4)], 0, True)
    gather(0, near, 1 - y)
    turn_keys(near * 4, 4, 4 * rows)
    role(0, both(1, 2, y, [across]))
    role(1, both(1, 3, y, [last[0]]))
    role(2, both(1, 0, y, [last[3]]))
    role(3, both(1, 1, y, [across]))
    gather(1, near, 1 - y)
    chunk([(near * 4, 4)], 4 * rows, False)
    role(0, both(0, 3, y, [across]))
    role(1, both(1, 3, 1 - y, [last[0]]))
    role(2, both(1, 0, 1 - y, [last[3]]))
    role(3, both(0, 0, y, [across]))
    here = [(slot(p, y, 0), 2) for p in (Z2, Z3)]
    over = [(slot(p, 1 - y, 0), 2) for p in (Z2, Z3)]
    for i, (first, count) in enumerate(here):
        turn_keys(first, count, (8 + 2 * i) * rows)
    pl.when(end)(lambda: gather(1, Z3, y))
    chunk(here, 8 * rows, False)
    for i, (first, count) in enumerate(over):
        gather(0, (Z2, Z3)[i], 1 - y)
        turn_keys(first, count, (12 + 2 * i) * rows)
    gather(1, Z2, 1 - y)
    pl.when(end)(lambda: gather(1, Z3, 1 - y))

    out = []
    for k in range(2):
        for g in range(half):
            def finish(b, mixed, g=g, k=k):
                flat = (mixed.T + v_bias[g]).astype(jnp.bfloat16)
                for i in range(HEAD // rows):
                    h = b * (HEAD // rows) + i
                    piece = flat[i * rows : (i + 1) * rows, :]
                    if k == 0:
                        obuf[g, :, h * HEAD : (h + 1) * HEAD] = piece
                    else:
                        at = core * qwide + (g * RATIO + h) * HEAD
                        o_ref[:, pl.ds(pl.multiple_of(at, HEAD), HEAD)] = piece

            attend(g, k, over, 12 * rows, False, finish)
            if k == 0:
                at = core * qwide + g * RATIO * HEAD
                c = pltpu.make_async_remote_copy(
                    src_ref=obuf.at[g],
                    dst_ref=o_ref.at[:, pl.ds(pl.multiple_of(at, HEAD), RATIO * HEAD)],
                    send_sem=osem.at[g], recv_sem=osem.at[half + g], **to(sib),
                )
                c.start()
                out.append(c)

    def drain(plane_at, i):
        size = kv.at[pl.ds(0, sent[plane_at][i])]
        pltpu.make_async_copy(size, size, send.at[i]).wait()

    for plane_at in range(4):
        pl.when(z == plane_at)(functools.partial(drain, plane_at, 0))
        pl.when(jnp.logical_and(z == plane_at, core == 1))(functools.partial(drain, plane_at, 1))
    size = pbuf.at[:, pl.ds(0, n - 1)]
    pltpu.make_async_copy(size, size, psend).wait()
    q_send.wait_send()
    for c in out:
        c.wait()


def on_line(n, query, keys, values, query_bias, key_bias, value_projection_bias, frame_order):
    rows = keys.shape[0]
    half = KVH // 2
    frames = rows // FRAME_TOK
    wide = RATIO * 2 * rows
    return pl.pallas_call(
        functools.partial(line_kernel, n),
        out_shape=jax.ShapeDtypeStruct(query.shape, jnp.bfloat16),
        in_specs=[pl.BlockSpec(memory_space=pltpu.HBM)] * 8,
        out_specs=pl.BlockSpec(memory_space=pltpu.VMEM),
        scratch_shapes=[
            pltpu.VMEM(query_bias.shape, jnp.bfloat16),
            pltpu.VMEM(key_bias.shape, jnp.bfloat16),
            pltpu.VMEM(key_bias.shape, jnp.bfloat16),
            pltpu.SMEM(frame_order.shape, jnp.int32),
            pltpu.VMEM((40, HEAD), jnp.float32),
            pltpu.VMEM((2, rows, QH * HEAD // 2), jnp.bfloat16),
            pltpu.VMEM((4 * n, rows, half * HEAD), jnp.bfloat16),
            pltpu.VMEM((3, n, HEAD), jnp.float32),
            pltpu.VMEM((frames, n, HEAD), jnp.float32),
            pltpu.VMEM((frames, n, HEAD), jnp.float32),
            pltpu.VMEM((frames, n, HEAD), jnp.float32),
            pltpu.VMEM((half, wide, HEAD), jnp.bfloat16),
            pltpu.VMEM((half, HEAD, wide), jnp.float32),
            pltpu.VMEM((half, 1, wide), jnp.float32),
            pltpu.VMEM((half, 1, wide), jnp.float32),
            pltpu.VMEM((half, n * rows, HEAD), jnp.bfloat16),
            pltpu.VMEM((2, n * rows, HEAD), jnp.float32),
            pltpu.VMEM((half, rows, RATIO * HEAD), jnp.bfloat16),
            pltpu.SemaphoreType.DMA((4 * n,)),
            pltpu.SemaphoreType.DMA((2,)),
            pltpu.SemaphoreType.DMA((n,)),
            pltpu.SemaphoreType.DMA,
            pltpu.SemaphoreType.DMA((2,)),
            pltpu.SemaphoreType.DMA((2 * half,)),
            pltpu.SemaphoreType.DMA((8,)),
            pltpu.SemaphoreType.REGULAR((4,)),
        ],
        compiler_params=pltpu.CompilerParams(vmem_limit_bytes=24 << 20, collective_id=1, has_side_effects=True),
    )(*(
        pltpu.with_memory_space_constraint(x, pltpu.HBM)
        for x in (
            query, keys, values, query_bias, key_bias, value_projection_bias, frame_order,
            jnp.asarray(line_tables()),
        )
    ))


def on_device(n, query, keys, values, query_bias, key_bias, value_projection_bias, frame_order):
    chips = n // 2
    B = 1
    while B * B * 4 <= chips:
        B *= 2
    A = chips // B
    rows = keys.shape[0]
    qper = query_bias.shape[0]
    wide = RATIO * rows
    keys_at_once = 4 * rows
    whole = pl.BlockSpec(memory_space=pltpu.VMEM)
    far = pl.BlockSpec(memory_space=pltpu.HBM)
    return pl.pallas_call(
        functools.partial(kernel, A, B, n, qper),
        out_shape=jax.ShapeDtypeStruct(query.shape, jnp.bfloat16),
        in_specs=[far] * 8,
        out_specs=whole,
        scratch_shapes=[
            pltpu.VMEM(query_bias.shape, jnp.bfloat16),
            pltpu.VMEM(key_bias.shape, jnp.bfloat16),
            pltpu.VMEM(key_bias.shape, jnp.bfloat16),
            pltpu.SMEM(frame_order.shape, jnp.int32),
            pltpu.VMEM((40, HEAD), jnp.float32),
            pltpu.VMEM(query.shape, jnp.bfloat16),
            pltpu.VMEM((8, HEAD), jnp.float32),
            pltpu.VMEM((n, rows, KVH * HEAD), jnp.bfloat16),
            pltpu.VMEM((n, rows, KVH * HEAD), jnp.bfloat16),
            pltpu.VMEM((n, 8, HEAD), jnp.float32),
            pltpu.VMEM((KVH, wide, HEAD), jnp.bfloat16),
            pltpu.VMEM((KVH, HEAD, wide), jnp.float32),
            pltpu.VMEM((KVH, 1, wide), jnp.float32),
            pltpu.VMEM((KVH, 1, wide), jnp.float32),
            pltpu.VMEM((KVH, keys_at_once, HEAD), jnp.bfloat16),
            pltpu.VMEM((KVH, keys_at_once, HEAD), jnp.bfloat16),
            pltpu.VMEM((keys_at_once, HEAD), jnp.float32),
            pltpu.SemaphoreType.DMA((PIECES, n)),
            pltpu.SemaphoreType.DMA((PIECES, 5, n)),
            pltpu.SemaphoreType.DMA((n,)),
            pltpu.SemaphoreType.DMA((n,)),
            pltpu.SemaphoreType.DMA((8,)),
        ],
        compiler_params=pltpu.CompilerParams(vmem_limit_bytes=(16 if n <= 32 else 48) << 20, collective_id=0, has_side_effects=True),
    )(*(
        pltpu.with_memory_space_constraint(x, pltpu.HBM)
        for x in (
            query, keys, values, query_bias, key_bias, value_projection_bias, frame_order,
            jnp.asarray(tables()),
        )
    ))


def solution(mesh):
    placed = (
        P(("groups", "seq"), None),
        P(("groups", "seq"), None),
        P(("groups", "seq"), None),
        P("seq"),
        P("seq"),
        P("seq"),
        P(("groups", "seq")),
    )
    n = mesh.shape["seq"]
    return jax.shard_map(
        functools.partial(on_line if n == 16 else on_device, n),
        mesh=mesh,
        in_specs=placed,
        out_specs=P(("groups", "seq"), None),
        check_vma=False,
    )
```

```python
import functools
import math

import jax
import jax.numpy as jnp
import numpy as np
from jax import lax
from jax.experimental import pallas as pl
from jax.experimental.pallas import tpu as pltpu
from jax.sharding import PartitionSpec as P

HEAD = 128
HALF = HEAD // 2
QH = 32
KVH = 4
RATIO = QH // KVH
GRID = 4
FRAME_TOK = 16
MESH = pl.DeviceIdType.MESH
NEG = -1e30
PIECES = 2
PAIRS_T = HALF // 4
PAIRS_R = HALF // 4 + 3 * HALF // 8


def tables():
    pair = np.arange(HEAD) % HALF
    freq = np.exp(-(2.0 * pair / HEAD) * math.log(1000000.0))
    tok = np.arange(FRAME_TOK)
    source = np.where(pair[None, :] < PAIRS_R, (tok // GRID)[:, None], (tok % GRID)[:, None])
    angle = source * freq[None, :]
    sign = np.where(np.arange(HEAD) < HALF, -1.0, 1.0)
    rows = np.zeros((40, HEAD), np.float32)
    rows[0:16] = np.cos(angle)
    rows[16:32] = np.sin(angle) * sign[None, :]
    rows[32] = 2.0 * freq
    return rows


def cos_sin(frames, spatial):
    angle = frames * spatial[32:33, :]
    turns = jnp.round(angle * (1.0 / (2.0 * math.pi)))
    angle = angle - turns * 6.28125
    angle = angle - turns * (2.0 * math.pi - 6.28125)
    lane = lax.broadcasted_iota(jnp.int32, (FRAME_TOK, HEAD), 1)
    temporal = lane % HALF < PAIRS_T
    sign = jnp.where(lane < HALF, -1.0, 1.0)
    cos_t, sin_t = jnp.cos(angle), jnp.sin(angle)
    cosines, sines = [], []
    for j in range(frames.shape[0]):
        cosines.append(jnp.where(temporal, cos_t[j : j + 1, :], spatial[0:16, :]))
        sines.append(jnp.where(temporal, sin_t[j : j + 1, :] * sign, spatial[16:32, :]))
    return jnp.concatenate(cosines, axis=0), jnp.concatenate(sines, axis=0)


def spin(x, cosine, sine):
    return x * cosine + pltpu.roll(x, HALF, 1) * sine


def kernel(
    A, B, n, qper,
    q_hbm, k_hbm, v_hbm, qb_hbm, kb_hbm, vb_hbm, order_hbm, tab_hbm,
    o_ref,
    qb_ref, kb_ref, vb_ref, order_ref, tab_ref,
    q_ref, pack_ref, kbuf, vbuf, pbuf, qs, acc, top, den, ksc, vsc, hide,
    recv, send, precv, psend, load,
):
    me = lax.axis_index("seq")
    rows = kbuf.shape[1]
    frames = rows // FRAME_TOK
    cut = rows // (PIECES // 2)
    core = me % 2
    b = (me // 2) % B
    a = me // (2 * B)

    def piece(p, s):
        return (kbuf, vbuf)[p % 2].at[s, pl.ds((p // 2) * cut, cut)]

    def slot(x, y, z):
        return (x * B + y) * 2 + z

    ways = (
        (a + 1 < A, slot(a + 1, b, core)),
        (a > 0, slot(a - 1, b, core)),
        (b + 1 < B, slot(a, b + 1, core)),
        (b > 0, slot(a, b - 1, core)),
        (None, slot(a, b, 1 - core)),
    )

    def copy(t, s, way):
        return pltpu.make_async_remote_copy(
            src_ref=piece(t, s),
            dst_ref=piece(t, s),
            send_sem=send.at[t, way, s],
            recv_sem=recv.at[t, s],
            device_id={"seq": ways[way][1]},
            device_id_type=MESH,
        )

    def when(cond, act):
        if cond is None:
            act()
        else:
            pl.when(cond)(act)

    def fan(t, s, dirs, start):
        for way in dirs:
            c = copy(t, s, way)
            when(ways[way][0], c.start if start else c.wait_send)

    def arrive(t, s):
        copy(t, s, 4).wait_recv()

    def inside(i, size):
        return jnp.logical_and(i >= 0, i < size)

    def along_a(d, start):
        for t in range(PIECES):
            for sg in (1, -1):
                x = a + sg * d

                @pl.when(jnp.logical_and(inside(x, A), d < A))
                def _(x=x, sg=sg, t=t):
                    s = slot(x, b, core)
                    if start:
                        arrive(t, s)
                    fan(t, s, (1 if sg > 0 else 0, 2, 3, 4), start)

    def along_b(d, start):
        for e in range(1, B):
            for t in range(PIECES):
                for sg in (1, -1):
                    x = a + sg * d
                    ok = inside(x, A) if sg > 0 else jnp.logical_and(inside(x, A), d > 0)
                    for sb in (1, -1):
                        y = b + sb * e

                        @pl.when(jnp.logical_and(ok, inside(y, B)))
                        def _(x=x, y=y, sb=sb, t=t):
                            s = slot(x, y, core)
                            if start:
                                arrive(t, s)
                            fan(t, s, (3 if sb > 0 else 2, 4), start)

    barrier = pltpu.get_barrier_semaphore()

    def greet(i, _):
        pl.semaphore_signal(barrier, inc=1, device_id={"seq": lax.rem(me + i, n)}, device_id_type=MESH)
        return 0

    lax.fori_loop(1, n, greet, 0)
    k_load = pltpu.make_async_copy(k_hbm, kbuf.at[me], load.at[0])
    v_load = pltpu.make_async_copy(v_hbm, vbuf.at[me], load.at[1])
    q_load = pltpu.make_async_copy(q_hbm, q_ref, load.at[2])
    small = [
        pltpu.make_async_copy(src, dst, load.at[3 + i])
        for i, (src, dst) in enumerate((
            (order_hbm, order_ref), (qb_hbm, qb_ref), (kb_hbm, kb_ref), (vb_hbm, vb_ref), (tab_hbm, tab_ref),
        ))
    ]
    for c in small + [k_load, v_load, q_load]:
        c.start()

    lane = lax.broadcasted_iota(jnp.int32, (1, HEAD), 1)

    def placed(values):
        size = values.shape[1]
        spots = HEAD // size
        return jnp.where(lane // size == me % spots, jnp.concatenate([values] * spots, axis=1), 0.0)

    def row(ref):
        return ref[...].astype(jnp.float32)[None, :]

    for c in small:
        c.wait()
    pack_ref[...] = jnp.zeros_like(pack_ref)
    q_row = row(qb_ref)
    if qper >= HEAD:
        for i in range(qper // HEAD):
            pack_ref[i : i + 1, :] = q_row[:, i * HEAD : (i + 1) * HEAD]
    else:
        pack_ref[0:1, :] = placed(q_row)
    pack_ref[2:3, :] = placed(row(kb_ref))
    pack_ref[3:4, :] = placed(row(vb_ref))
    qpos = (lane % FRAME_TOK).astype(jnp.float32)
    for f in range(frames):
        frame = order_ref[f].astype(jnp.float32)
        pack_ref[8 - frames + f : 9 - frames + f, :] = jnp.full((1, HEAD), 1.0, jnp.float32) * frame
        qpos = qpos + jnp.where((lane % rows) // FRAME_TOK == f, frame * FRAME_TOK, 0.0)
    pbuf[me] = pack_ref[...]
    tab = tab_ref[...]
    q_cos, q_sin = cos_sin(pack_ref[8 - frames :, :], tab)
    fold = math.log2(math.e) / math.sqrt(HEAD)
    q_cos, q_sin = q_cos * fold, q_sin * fold
    k_load.wait()
    v_load.wait()
    pl.semaphore_wait(barrier, n - 1)

    def pack_copy(i, s):
        return pltpu.make_async_remote_copy(
            src_ref=pack_ref,
            dst_ref=pbuf.at[s],
            send_sem=psend.at[i],
            recv_sem=precv.at[s],
            device_id={"seq": lax.rem(me + i, n)},
            device_id_type=MESH,
        )

    def push(i, _):
        pack_copy(i, me).start()
        return 0

    lax.fori_loop(1, n, push, 0)
    for t in range(PIECES):
        fan(t, me, (0, 1, 2, 3, 4), True)

    acc[...] = jnp.zeros_like(acc)
    den[...] = jnp.zeros_like(den)
    top[...] = jnp.full_like(top, NEG)

    def pulled(i, _):
        pack_copy(i, lax.rem(me + i, n)).wait_recv()
        return 0

    lax.fori_loop(1, n, pulled, 0)
    q_load.wait()

    for h in range(QH):
        if qper >= HEAD:
            per = qper // HEAD
            bias = pbuf[h // per, h % per : h % per + 1, :]
        else:
            parts = HEAD // qper
            bias = sum(pbuf[h * parts + i, 0:1, :] for i in range(parts))
        x = q_ref[:, h * HEAD : (h + 1) * HEAD].astype(jnp.float32) + bias
        at = (h % RATIO) * rows
        qs[h // RATIO, at : at + rows, :] = spin(x, q_cos, q_sin).astype(jnp.bfloat16)
    share = n // KVH
    k_bias = [sum(pbuf[g * share + i, 2:3, :] for i in range(share)) for g in range(KVH)]
    v_bias = [sum(pbuf[g * share + i, 3:4, :] for i in range(share)) for g in range(KVH)]
    within = lax.broadcasted_iota(jnp.int32, (FRAME_TOK, HEAD), 0).astype(jnp.float32)

    def chunk(first):
        for j in range(4):
            s = first + j
            order = pbuf[s][8 - frames :, :]
            cosine, sine = cos_sin(order, tab)
            for f in range(frames):
                kpos = order[f : f + 1, :] * FRAME_TOK + within
                at = j * rows + f * FRAME_TOK
                hide[at : at + FRAME_TOK, :] = jnp.where(kpos <= qpos, 0.0, NEG)
            for g in range(KVH):
                cols = slice(g * HEAD, (g + 1) * HEAD)
                x = kbuf[s, :, cols].astype(jnp.float32) + k_bias[g]
                ksc[g, j * rows : (j + 1) * rows, :] = spin(x, cosine, sine).astype(jnp.bfloat16)
                y = vbuf[s, :, cols].astype(jnp.float32) + v_bias[g]
                vsc[g, j * rows : (j + 1) * rows, :] = y.astype(jnp.bfloat16)
        for g in range(KVH):
            scores = lax.dot_general(
                ksc[g], qs[g], (((1,), (1,)), ((), ())), preferred_element_type=jnp.float32
            )
            mask = hide[...]
            scores = scores + jnp.concatenate([mask] * (scores.shape[1] // HEAD), axis=1)
            old = top[g]
            new = jnp.maximum(old, jnp.max(scores, axis=0, keepdims=True))
            expo = jnp.exp2(scores - new)
            factor = jnp.exp2(old - new)
            top[g] = new
            den[g] = den[g] * factor + jnp.sum(expo, axis=0, keepdims=True)
            acc[g] = acc[g] * factor + lax.dot_general(
                vsc[g], expo.astype(jnp.bfloat16), (((0,), (0,)), ((), ())),
                preferred_element_type=jnp.float32,
            )

    low = a < A // 2
    mirror = jnp.where(low, a, A - 1 - a)

    def step(d, _):
        along_a(d + 1, True)
        along_b(d, True)
        near = jnp.where(d % 2 == 1, -((d + 1) // 2), d // 2)
        plane = mirror + jnp.where(d <= 2 * mirror, near, d - mirror)
        plane = jnp.where(low, plane, A - 1 - plane)
        for y in range(B):
            for t in range(PIECES):
                arrive(t, slot(plane, y, 1 - core))
        if 2 * B == 4:
            chunk(plane * 4)
        else:
            def part(i, _):
                chunk(plane * 2 * B + i * 4)
                return 0

            lax.fori_loop(0, 2 * B // 4, part, 0)
        return 0

    lax.fori_loop(0, A, step, 0)

    for g in range(KVH):
        mixed = acc[g] * (1.0 / den[g])
        flat = mixed.T.astype(jnp.bfloat16)
        for r in range(RATIO):
            h = g * RATIO + r
            o_ref[:, h * HEAD : (h + 1) * HEAD] = flat[r * rows : (r + 1) * rows, :]

    for t in range(PIECES):
        fan(t, me, (0, 1, 2, 3, 4), False)

    def drain(d, _):
        along_a(d + 1, False)
        along_b(d, False)
        return 0

    lax.fori_loop(0, A, drain, 0)

    def pushed(i, _):
        pack_copy(i, me).wait_send()
        return 0

    lax.fori_loop(1, n, pushed, 0)


def line_tables():
    rows = tables()
    pair = np.arange(HEAD) % HALF
    temporal = pair < PAIRS_T
    rows[0:32, temporal] = 0.0
    rows[32] = np.where(temporal, rows[32], 0.0)
    rows[33] = np.where(temporal, 1.0, 0.0)
    rows[34] = np.where(temporal, np.where(np.arange(HEAD) < HALF, -1.0, 1.0), 0.0)
    return rows


def circle(x):
    k = jnp.round(x * (2.0 / math.pi))
    r = x - k * 1.5703125
    r = r - k * (math.pi / 2.0 - 1.5703125)
    w = r * r
    s = r + r * w * (-1.6666654611e-1 + w * (8.3321608736e-3 - w * 1.9515295891e-4))
    c = 1.0 - 0.5 * w + w * w * (4.166664568298827e-2 + w * (-1.388731625493765e-3 + w * 2.443315711809948e-5))
    turn = k - 4.0 * jnp.floor(k * 0.25)
    odd = jnp.logical_or(turn == 1.0, turn == 3.0)
    cosine = jnp.where(odd, s, c)
    sine = jnp.where(odd, c, s)
    cosine = jnp.where(jnp.logical_or(turn == 1.0, turn == 2.0), -cosine, cosine)
    sine = jnp.where(turn >= 2.0, -sine, sine)
    return cosine, sine


def line_kernel(
    n,
    q_hbm, k_hbm, v_hbm, qb_hbm, kb_hbm, vb_hbm, order_hbm, tab_hbm,
    o_ref,
    qb_ref, kb_ref, vb_ref, order_ref, tab_ref,
    q_ref, kv, pbuf, ctab, stab, ftab, qs, acc, top, den, ksc, hide, obuf,
    recv, send, precv, psend, qsem, osem, load, entered,
):
    me = lax.axis_index("seq")
    rows = k_hbm.shape[0]
    frames = rows // FRAME_TOK
    half = KVH // 2
    wide = half * HEAD
    qwide = QH * HEAD // 2
    core = me % 2
    y = (me // 2) % 2
    z = me // 4
    sib = me + 1 - 2 * core
    low = z < 2
    end = jnp.logical_or(z == 0, z == 3)
    mid = jnp.logical_not(end)

    def slot(a, b, c):
        return (a * 2 + b) * 2 + c

    def up(i):
        return jnp.where(low, i, 3 - i)

    Z0, Z1, Z2, Z3 = up(0), up(1), up(2), up(3)

    def to(s):
        return dict(device_id={"seq": s}, device_id_type=MESH)

    def part(c, size):
        return pl.ds(pl.multiple_of(c * size, size), size)

    barrier = pltpu.get_barrier_semaphore()

    def greet(other, _):
        @pl.when(other != me)
        def _():
            pl.semaphore_signal(barrier, inc=1, **to(other))

        return 0

    def tell(other, _):
        pl.semaphore_signal(entered.at[z], inc=1, **to(other))
        return 0

    def above(i):
        @pl.when(z + i < 4)
        def _():
            pl.semaphore_wait(entered.at[jnp.minimum(z + i, 3)], 4)

    lax.fori_loop(4 * z, n, greet, 0)
    small = [
        pltpu.make_async_copy(src, dst, load.at[i])
        for i, (src, dst) in enumerate((
            (order_hbm, order_ref), (qb_hbm, qb_ref), (kb_hbm, kb_ref), (vb_hbm, vb_ref), (tab_hbm, tab_ref),
        ))
    ]
    mine = [
        pltpu.make_async_copy(k_hbm.at[:, part(core, wide)], kv.at[me], load.at[5]),
        pltpu.make_async_copy(v_hbm.at[:, part(core, wide)], kv.at[n + me], load.at[6]),
        pltpu.make_async_copy(q_hbm.at[:, part(core, qwide)], q_ref.at[0], load.at[7]),
    ]
    for c in small + mine:
        c.start()

    lane = lax.broadcasted_iota(jnp.int32, (1, HEAD), 1)
    group = lane // (HEAD // KVH)

    def row(ref):
        return ref[...].astype(jnp.float32)[None, :]

    def placed(values, at):
        return jnp.where(group == at % KVH, jnp.concatenate([values] * KVH, axis=1), 0.0)

    pl.semaphore_wait(barrier, 4 * z + 3)

    def own(t, dz, dy, dc, relay=False):
        at = (2 + t if relay else t) * n + me
        return pltpu.make_async_remote_copy(
            src_ref=(k_hbm, v_hbm)[t].at[:, part(dc, wide)],
            dst_ref=kv.at[at],
            send_sem=send.at[0],
            recv_sem=recv.at[at],
            **to(slot(dz, dy, 1 if relay else dc)),
        )

    def passed(source, target, s):
        return pltpu.make_async_remote_copy(
            src_ref=kv.at[source],
            dst_ref=kv.at[target],
            send_sem=send.at[1],
            recv_sem=recv.at[target],
            **to(s),
        )

    sent = [[0, 0] for _ in range(4)]

    def own_to(planes, t, dz, dy, relay):
        for dc in (0, 1):
            own(t, dz, dy, dc, relay and dc == 0).start()
        for p in planes:
            sent[p][0] += 2

    def arrive(t, s):
        passed(t * n + s, t * n + s, sib).wait_recv()

    def pack_copy(i, s):
        return pltpu.make_async_remote_copy(
            src_ref=pbuf.at[:, pl.ds(s, 1)],
            dst_ref=pbuf.at[:, pl.ds(s, 1)],
            send_sem=psend,
            recv_sem=precv.at[s],
            **to(lax.rem(me + i, n)),
        )

    def push(upward):
        def act(other, _):
            @pl.when(other != me)
            def _():
                pack_copy(other - me + n, me).start()

            return 0

        lax.fori_loop(*((4 * z + 4, n) if upward else (0, 4 * z + 4)), act, 0)

    def ways(t):
        pl.when(z > 0)(lambda: own_to((1, 2, 3), t, z - 1, y, True))
        if t == 0:
            own_to((0, 1, 2, 3), t, z, 1 - y, False)
        else:
            pl.when(end)(lambda: own_to((0, 3), t, z, 1 - y, True))
            pl.when(mid)(lambda: own_to((1, 2), t, z, 1 - y, False))

    ways(0)
    lax.fori_loop(0, 4 * z, tell, 0)
    for c in small:
        c.wait()
    q_row = row(qb_ref)
    pbuf[0, pl.ds(me, 1), :] = q_row[:, :HEAD]
    pbuf[1, pl.ds(me, 1), :] = q_row[:, HEAD:]
    third = placed(row(kb_ref), me) + placed(row(vb_ref), me + 1)
    for f in range(frames):
        third = third + jnp.where(lane == (me + 2) % KVH * (HEAD // KVH) + f, order_ref[f].astype(jnp.float32), 0.0)
    pbuf[2, pl.ds(me, 1), :] = third
    push(False)
    ways(1)
    q_send = pltpu.make_async_remote_copy(
        src_ref=q_hbm.at[:, part(1 - core, qwide)], dst_ref=q_ref.at[1],
        send_sem=qsem.at[0], recv_sem=qsem.at[1], **to(sib),
    )
    q_send.start()
    for t in (0, 1):
        own(t, z, y, 1 - core).start()
        for r in sent:
            r[0] += 1

    ORDER = (1, 0)
    def role(plane, steps):
        def forward():
            for t, s, targets in steps:
                for kind in (2 + t, t):
                    source = kind * n + s
                    passed(source, source, sib).wait_recv()
                    for dz, dy, relay in targets:
                        if kind == t or relay:
                            passed(source, source, slot(dz, dy, 1)).start()
                        else:
                            passed(source, t * n + s, slot(dz, dy, 0)).start()
                        sent[plane][1] += 1
                    if kind != t:
                        passed(source, t * n + s, sib).start()
                        sent[plane][1] += 1

        def take():
            for t, s, _ in steps:
                arrive(t, s)

        pl.when(jnp.logical_and(z == plane, core == 1))(forward)
        pl.when(jnp.logical_and(z == plane, core == 0))(take)

    def both(t, dz, dy, targets):
        return [(t, slot(dz, dy, k), targets) for k in ORDER]

    across = (z, 1 - y, False)

    def gather(t, dz, dy):
        for k in ORDER:
            arrive(t, slot(dz, dy, k))

    above(1)
    for t in (0, 1):
        pl.when(z < 3)(lambda: own_to((0, 1, 2), t, z + 1, y, True))
    relay = [(p, y, True) for p in range(4)]
    last = [(p, y, False) for p in range(4)]
    role(0, both(0, 1, y, [across]))
    role(1, both(0, 2, y, [relay[0], across]))
    role(2, both(0, 3, y, [relay[1], across]))
    role(3, both(1, 3, 1 - y, [relay[1], last[2]]))
    above(2)
    above(3)
    push(True)
    role(0, both(1, 0, 1 - y, [relay[2], last[1]]) + both(1, 1, y, [across]))
    role(1, both(1, 2, y, [relay[0], across]) + both(0, 0, y, [relay[2], across]))
    role(2, both(1, 3, y, [relay[1]]) + both(0, 1, y, [relay[3], across]))
    role(3, both(0, 2, y, [across]) + both(1, 2, y, [across]))

    def pulled(i, _):
        pack_copy(i, lax.rem(me + i, n)).wait_recv()
        return 0

    lax.fori_loop(1, n, pulled, 0)
    tab = tab_ref[...]
    third = pbuf[2]
    at = lax.broadcasted_iota(jnp.int32, (n, HEAD), 0)
    spot = lax.broadcasted_iota(jnp.int32, (n, HEAD), 1) - (at + 2) % KVH * (HEAD // KVH)
    for f in range(frames):
        frame = jnp.sum(jnp.where(spot == f, third, 0.0), axis=1, keepdims=True)
        frame = jnp.broadcast_to(frame, (n, HEAD))
        cosine, sine = circle(frame * tab[32:33, :])
        ctab[f] = cosine * tab[33:34, :]
        stab[f] = sine * tab[34:35, :]
        ftab[f] = frame * FRAME_TOK

    def bias_row(g, turn):
        got = jnp.zeros((1, HEAD), jnp.float32)
        for i in range(KVH):
            piece = pbuf[2, pl.ds((core * half + g) * KVH + i, 1), :]
            got = got + jnp.where(group == (i + turn) % KVH, piece, 0.0)
        return got if turn == 0 else pltpu.roll(got, HEAD - turn * (HEAD // KVH), 1)

    k_bias = [bias_row(g, 0) for g in range(half)]
    v_bias = [bias_row(g, 1) for g in range(half)]

    def angles(s):
        cosines = [ctab[f, pl.ds(s, 1), :] + tab[0:16, :] for f in range(frames)]
        sines = [stab[f, pl.ds(s, 1), :] + tab[16:32, :] for f in range(frames)]
        return jnp.concatenate(cosines, axis=0), jnp.concatenate(sines, axis=0)

    fold = math.log2(math.e) / math.sqrt(HEAD)
    q_cos, q_sin, q_pos = [], [], []
    for s in (sib, me):
        cosine, sine = angles(s)
        q_cos.append(cosine * fold)
        q_sin.append(sine * fold)
        qpos = (lane % FRAME_TOK).astype(jnp.float32)
        for f in range(frames):
            qpos = qpos + jnp.where(lane % rows // FRAME_TOK == f, ftab[f, pl.ds(s, 1), :], 0.0)
        q_pos.append(qpos)
    blocks = RATIO * rows // HEAD
    within = lax.broadcasted_iota(jnp.int32, (FRAME_TOK, HEAD), 0).astype(jnp.float32)

    def turn_keys(first, count, at):
        for j in range(count):
            s = first + j
            cosine, sine = angles(s)
            for f in range(frames):
                kpos = ftab[f, pl.ds(s, 1), :] + within
                r = at + j * rows + f * FRAME_TOK
                for k in range(2):
                    hide[k, r : r + FRAME_TOK, :] = jnp.where(kpos <= q_pos[k], 0.0, NEG)
            for g in range(half):
                x = kv[s, :, g * HEAD : (g + 1) * HEAD].astype(jnp.float32) + k_bias[g]
                r = at + j * rows
                ksc[g, r : r + rows, :] = spin(x, cosine, sine).astype(jnp.bfloat16)

    def attend(g, k, spans, at, fresh, finish=None):
        vals = jnp.concatenate([
            kv[pl.ds(n + first, count), :, g * HEAD : (g + 1) * HEAD].reshape(count * rows, HEAD)
            for first, count in spans
        ], axis=0)
        keys = slice(at, at + vals.shape[0])
        mask = hide[k, keys, :]
        for b in range(k * blocks, (k + 1) * blocks):
            cols = slice(b * HEAD, (b + 1) * HEAD)
            scores = lax.dot_general(
                ksc[g, keys, :], qs[g, cols, :], (((1,), (1,)), ((), ())), preferred_element_type=jnp.float32
            )
            scores = scores + mask
            new = jnp.max(scores, axis=0, keepdims=True)
            if not fresh:
                old = top[g, :, cols]
                new = jnp.maximum(old, new)
            expo = jnp.exp2(scores - new)
            total = jnp.sum(expo, axis=0, keepdims=True)
            mixed = lax.dot_general(
                vals, expo.astype(jnp.bfloat16), (((0,), (0,)), ((), ())), preferred_element_type=jnp.float32
            )
            if finish is not None:
                factor = jnp.exp2(old - new)
                scale = 1.0 / (den[g, :, cols] * factor + total)
                finish(b - k * blocks, (acc[g, :, cols] * factor + mixed) * scale)
                continue
            top[g, :, cols] = new
            if fresh:
                den[g, :, cols] = total
                acc[g, :, cols] = mixed
            else:
                factor = jnp.exp2(old - new)
                den[g, :, cols] = den[g, :, cols] * factor + total
                acc[g, :, cols] = acc[g, :, cols] * factor + mixed

    def chunk(spans, at, fresh):
        for g in range(half):
            for k in range(2):
                attend(g, k, spans, at, fresh)

    mine[2].wait()
    q_send.wait_recv()
    for k in range(2):
        for h in range(QH // 2):
            bias = pbuf[h % 2, pl.ds(core * (n // 2) + h // 2, 1), :]
            x = q_ref[1 - k, :, h * HEAD : (h + 1) * HEAD].astype(jnp.float32) + bias
            r = (k * RATIO + h % RATIO) * rows
            qs[h // RATIO, r : r + rows, :] = spin(x, q_cos[k], q_sin[k]).astype(jnp.bfloat16)

    for c in mine[:2]:
        c.wait()
    arrive(0, sib)
    gather(0, z, 1 - y)
    turn_keys(z * 4, 4, 0)
    arrive(1, sib)
    near = jnp.where(end, Z1, Z0)
    role(0, both(0, 2, y, [across]))
    role(1, both(0, 3, y, [relay[0], across]) + both(1, 0, y, [relay[2]]))
    role(2, both(1, 1, y, [relay[3], across]) + both(0, 0, y, [relay[3], across]))
    role(3, both(0, 1, y, [across]))
    pl.when(mid)(lambda: gather(1, z, 1 - y))
    chunk([(z * 4, 4)], 0, True)
    gather(0, near, 1 - y)
    turn_keys(near * 4, 4, 4 * rows)
    role(0, both(1, 2, y, [across]))
    role(1, both(1, 3, y, [last[0]]))
    role(2, both(1, 0, y, [last[3]]))
    role(3, both(1, 1, y, [across]))
    gather(1, near, 1 - y)
    role(0, both(0, 3, y, [across]))
    role(1, both(1, 3, 1 - y, [last[0]]))
    role(2, both(1, 0, 1 - y, [last[3]]))
    role(3, both(0, 0, y, [across]))
    chunk([(near * 4, 4)], 4 * rows, False)
    here = [(slot(p, y, 0), 2) for p in (Z2, Z3)]
    over = [(slot(p, 1 - y, 0), 2) for p in (Z2, Z3)]
    for i, (first, count) in enumerate(here):
        turn_keys(first, count, (8 + 2 * i) * rows)
    pl.when(end)(lambda: gather(1, Z3, y))
    chunk(here, 8 * rows, False)
    for i, (first, count) in enumerate(over):
        gather(0, (Z2, Z3)[i], 1 - y)
        turn_keys(first, count, (12 + 2 * i) * rows)
    gather(1, Z2, 1 - y)
    pl.when(end)(lambda: gather(1, Z3, 1 - y))

    out = []
    for k in range(2):
        for g in range(half):
            def finish(b, mixed, g=g, k=k):
                flat = (mixed.T + v_bias[g]).astype(jnp.bfloat16)
                for i in range(HEAD // rows):
                    h = b * (HEAD // rows) + i
                    piece = flat[i * rows : (i + 1) * rows, :]
                    if k == 0:
                        obuf[g, :, h * HEAD : (h + 1) * HEAD] = piece
                    else:
                        at = core * qwide + (g * RATIO + h) * HEAD
                        o_ref[:, pl.ds(pl.multiple_of(at, HEAD), HEAD)] = piece

            attend(g, k, over, 12 * rows, False, finish)
            if k == 0:
                at = core * qwide + g * RATIO * HEAD
                c = pltpu.make_async_remote_copy(
                    src_ref=obuf.at[g],
                    dst_ref=o_ref.at[:, pl.ds(pl.multiple_of(at, HEAD), RATIO * HEAD)],
                    send_sem=osem.at[g], recv_sem=osem.at[half + g], **to(sib),
                )
                c.start()
                out.append(c)

    def drain(plane_at, i):
        size = kv.at[pl.ds(0, sent[plane_at][i])]
        pltpu.make_async_copy(size, size, send.at[i]).wait()

    for plane_at in range(4):
        pl.when(z == plane_at)(functools.partial(drain, plane_at, 0))
        pl.when(jnp.logical_and(z == plane_at, core == 1))(functools.partial(drain, plane_at, 1))
    size = pbuf.at[:, pl.ds(0, n - 1)]
    pltpu.make_async_copy(size, size, psend).wait()
    q_send.wait_send()
    for c in out:
        c.wait()


def on_line(n, query, keys, values, query_bias, key_bias, value_projection_bias, frame_order):
    rows = keys.shape[0]
    half = KVH // 2
    frames = rows // FRAME_TOK
    wide = RATIO * 2 * rows
    return pl.pallas_call(
        functools.partial(line_kernel, n),
        out_shape=jax.ShapeDtypeStruct(query.shape, jnp.bfloat16),
        in_specs=[pl.BlockSpec(memory_space=pltpu.HBM)] * 8,
        out_specs=pl.BlockSpec(memory_space=pltpu.VMEM),
        scratch_shapes=[
            pltpu.VMEM(query_bias.shape, jnp.bfloat16),
            pltpu.VMEM(key_bias.shape, jnp.bfloat16),
            pltpu.VMEM(key_bias.shape, jnp.bfloat16),
            pltpu.SMEM(frame_order.shape, jnp.int32),
            pltpu.VMEM((40, HEAD), jnp.float32),
            pltpu.VMEM((2, rows, QH * HEAD // 2), jnp.bfloat16),
            pltpu.VMEM((4 * n, rows, half * HEAD), jnp.bfloat16),
            pltpu.VMEM((3, n, HEAD), jnp.float32),
            pltpu.VMEM((frames, n, HEAD), jnp.float32),
            pltpu.VMEM((frames, n, HEAD), jnp.float32),
            pltpu.VMEM((frames, n, HEAD), jnp.float32),
            pltpu.VMEM((half, wide, HEAD), jnp.bfloat16),
            pltpu.VMEM((half, HEAD, wide), jnp.float32),
            pltpu.VMEM((half, 1, wide), jnp.float32),
            pltpu.VMEM((half, 1, wide), jnp.float32),
            pltpu.VMEM((half, n * rows, HEAD), jnp.bfloat16),
            pltpu.VMEM((2, n * rows, HEAD), jnp.float32),
            pltpu.VMEM((half, rows, RATIO * HEAD), jnp.bfloat16),
            pltpu.SemaphoreType.DMA((4 * n,)),
            pltpu.SemaphoreType.DMA((2,)),
            pltpu.SemaphoreType.DMA((n,)),
            pltpu.SemaphoreType.DMA,
            pltpu.SemaphoreType.DMA((2,)),
            pltpu.SemaphoreType.DMA((2 * half,)),
            pltpu.SemaphoreType.DMA((8,)),
            pltpu.SemaphoreType.REGULAR((4,)),
        ],
        compiler_params=pltpu.CompilerParams(vmem_limit_bytes=24 << 20, collective_id=1, has_side_effects=True),
    )(*(
        pltpu.with_memory_space_constraint(x, pltpu.HBM)
        for x in (
            query, keys, values, query_bias, key_bias, value_projection_bias, frame_order,
            jnp.asarray(line_tables()),
        )
    ))


def on_device(n, query, keys, values, query_bias, key_bias, value_projection_bias, frame_order):
    chips = n // 2
    B = 1
    while B * B * 4 <= chips:
        B *= 2
    A = chips // B
    rows = keys.shape[0]
    qper = query_bias.shape[0]
    wide = RATIO * rows
    keys_at_once = 4 * rows
    whole = pl.BlockSpec(memory_space=pltpu.VMEM)
    far = pl.BlockSpec(memory_space=pltpu.HBM)
    return pl.pallas_call(
        functools.partial(kernel, A, B, n, qper),
        out_shape=jax.ShapeDtypeStruct(query.shape, jnp.bfloat16),
        in_specs=[far] * 8,
        out_specs=whole,
        scratch_shapes=[
            pltpu.VMEM(query_bias.shape, jnp.bfloat16),
            pltpu.VMEM(key_bias.shape, jnp.bfloat16),
            pltpu.VMEM(key_bias.shape, jnp.bfloat16),
            pltpu.SMEM(frame_order.shape, jnp.int32),
            pltpu.VMEM((40, HEAD), jnp.float32),
            pltpu.VMEM(query.shape, jnp.bfloat16),
            pltpu.VMEM((8, HEAD), jnp.float32),
            pltpu.VMEM((n, rows, KVH * HEAD), jnp.bfloat16),
            pltpu.VMEM((n, rows, KVH * HEAD), jnp.bfloat16),
            pltpu.VMEM((n, 8, HEAD), jnp.float32),
            pltpu.VMEM((KVH, wide, HEAD), jnp.bfloat16),
            pltpu.VMEM((KVH, HEAD, wide), jnp.float32),
            pltpu.VMEM((KVH, 1, wide), jnp.float32),
            pltpu.VMEM((KVH, 1, wide), jnp.float32),
            pltpu.VMEM((KVH, keys_at_once, HEAD), jnp.bfloat16),
            pltpu.VMEM((KVH, keys_at_once, HEAD), jnp.bfloat16),
            pltpu.VMEM((keys_at_once, HEAD), jnp.float32),
            pltpu.SemaphoreType.DMA((PIECES, n)),
            pltpu.SemaphoreType.DMA((PIECES, 5, n)),
            pltpu.SemaphoreType.DMA((n,)),
            pltpu.SemaphoreType.DMA((n,)),
            pltpu.SemaphoreType.DMA((8,)),
        ],
        compiler_params=pltpu.CompilerParams(vmem_limit_bytes=(16 if n <= 32 else 48) << 20, collective_id=0, has_side_effects=True),
    )(*(
        pltpu.with_memory_space_constraint(x, pltpu.HBM)
        for x in (
            query, keys, values, query_bias, key_bias, value_projection_bias, frame_order,
            jnp.asarray(tables()),
        )
    ))


def solution(mesh):
    placed = (
        P(("groups", "seq"), None),
        P(("groups", "seq"), None),
        P(("groups", "seq"), None),
        P("seq"),
        P("seq"),
        P("seq"),
        P(("groups", "seq")),
    )
    n = mesh.shape["seq"]
    return jax.shard_map(
        functools.partial(on_line if n == 16 else on_device, n),
        mesh=mesh,
        in_specs=placed,
        out_specs=P(("groups", "seq"), None),
        check_vma=False,
    )
```

```python
import functools
import math

import jax
import jax.numpy as jnp
import numpy as np
from jax import lax
from jax.experimental import pallas as pl
from jax.experimental.pallas import tpu as pltpu
from jax.sharding import PartitionSpec as P

HEAD = 128
HALF = HEAD // 2
QH = 32
KVH = 4
RATIO = QH // KVH
GRID = 4
FRAME_TOK = 16
MESH = pl.DeviceIdType.MESH
NEG = -1e30
PIECES = 2
PAIRS_T = HALF // 4
PAIRS_R = HALF // 4 + 3 * HALF // 8


def tables():
    pair = np.arange(HEAD) % HALF
    freq = np.exp(-(2.0 * pair / HEAD) * math.log(1000000.0))
    tok = np.arange(FRAME_TOK)
    source = np.where(pair[None, :] < PAIRS_R, (tok // GRID)[:, None], (tok % GRID)[:, None])
    angle = source * freq[None, :]
    sign = np.where(np.arange(HEAD) < HALF, -1.0, 1.0)
    rows = np.zeros((40, HEAD), np.float32)
    rows[0:16] = np.cos(angle)
    rows[16:32] = np.sin(angle) * sign[None, :]
    rows[32] = 2.0 * freq
    return rows


def cos_sin(frames, spatial):
    angle = frames * spatial[32:33, :]
    turns = jnp.round(angle * (1.0 / (2.0 * math.pi)))
    angle = angle - turns * 6.28125
    angle = angle - turns * (2.0 * math.pi - 6.28125)
    lane = lax.broadcasted_iota(jnp.int32, (FRAME_TOK, HEAD), 1)
    temporal = lane % HALF < PAIRS_T
    sign = jnp.where(lane < HALF, -1.0, 1.0)
    cos_t, sin_t = jnp.cos(angle), jnp.sin(angle)
    cosines, sines = [], []
    for j in range(frames.shape[0]):
        cosines.append(jnp.where(temporal, cos_t[j : j + 1, :], spatial[0:16, :]))
        sines.append(jnp.where(temporal, sin_t[j : j + 1, :] * sign, spatial[16:32, :]))
    return jnp.concatenate(cosines, axis=0), jnp.concatenate(sines, axis=0)


def spin(x, cosine, sine):
    return x * cosine + pltpu.roll(x, HALF, 1) * sine


def kernel(
    A, B, n, qper,
    q_hbm, k_hbm, v_hbm, qb_hbm, kb_hbm, vb_hbm, order_hbm, tab_hbm,
    o_ref,
    qb_ref, kb_ref, vb_ref, order_ref, tab_ref,
    q_ref, pack_ref, kbuf, vbuf, pbuf, qs, acc, top, den, ksc, vsc, hide,
    recv, send, precv, psend, load,
):
    me = lax.axis_index("seq")
    rows = kbuf.shape[1]
    frames = rows // FRAME_TOK
    cut = rows // (PIECES // 2)
    core = me % 2
    b = (me // 2) % B
    a = me // (2 * B)

    def piece(p, s):
        return (kbuf, vbuf)[p % 2].at[s, pl.ds((p // 2) * cut, cut)]

    def slot(x, y, z):
        return (x * B + y) * 2 + z

    ways = (
        (a + 1 < A, slot(a + 1, b, core)),
        (a > 0, slot(a - 1, b, core)),
        (b + 1 < B, slot(a, b + 1, core)),
        (b > 0, slot(a, b - 1, core)),
        (None, slot(a, b, 1 - core)),
    )

    def copy(t, s, way):
        return pltpu.make_async_remote_copy(
            src_ref=piece(t, s),
            dst_ref=piece(t, s),
            send_sem=send.at[t, way, s],
            recv_sem=recv.at[t, s],
            device_id={"seq": ways[way][1]},
            device_id_type=MESH,
        )

    def when(cond, act):
        if cond is None:
            act()
        else:
            pl.when(cond)(act)

    def fan(t, s, dirs, start):
        for way in dirs:
            c = copy(t, s, way)
            when(ways[way][0], c.start if start else c.wait_send)

    def arrive(t, s):
        copy(t, s, 4).wait_recv()

    def inside(i, size):
        return jnp.logical_and(i >= 0, i < size)

    def along_a(d, start):
        for t in range(PIECES):
            for sg in (1, -1):
                x = a + sg * d

                @pl.when(jnp.logical_and(inside(x, A), d < A))
                def _(x=x, sg=sg, t=t):
                    s = slot(x, b, core)
                    if start:
                        arrive(t, s)
                    fan(t, s, (1 if sg > 0 else 0, 2, 3, 4), start)

    def along_b(d, start):
        for e in range(1, B):
            for t in range(PIECES):
                for sg in (1, -1):
                    x = a + sg * d
                    ok = inside(x, A) if sg > 0 else jnp.logical_and(inside(x, A), d > 0)
                    for sb in (1, -1):
                        y = b + sb * e

                        @pl.when(jnp.logical_and(ok, inside(y, B)))
                        def _(x=x, y=y, sb=sb, t=t):
                            s = slot(x, y, core)
                            if start:
                                arrive(t, s)
                            fan(t, s, (3 if sb > 0 else 2, 4), start)

    barrier = pltpu.get_barrier_semaphore()

    def greet(i, _):
        pl.semaphore_signal(barrier, inc=1, device_id={"seq": lax.rem(me + i, n)}, device_id_type=MESH)
        return 0

    lax.fori_loop(1, n, greet, 0)
    k_load = pltpu.make_async_copy(k_hbm, kbuf.at[me], load.at[0])
    v_load = pltpu.make_async_copy(v_hbm, vbuf.at[me], load.at[1])
    q_load = pltpu.make_async_copy(q_hbm, q_ref, load.at[2])
    small = [
        pltpu.make_async_copy(src, dst, load.at[3 + i])
        for i, (src, dst) in enumerate((
            (order_hbm, order_ref), (qb_hbm, qb_ref), (kb_hbm, kb_ref), (vb_hbm, vb_ref), (tab_hbm, tab_ref),
        ))
    ]
    for c in small + [k_load, v_load, q_load]:
        c.start()

    lane = lax.broadcasted_iota(jnp.int32, (1, HEAD), 1)

    def placed(values):
        size = values.shape[1]
        spots = HEAD // size
        return jnp.where(lane // size == me % spots, jnp.concatenate([values] * spots, axis=1), 0.0)

    def row(ref):
        return ref[...].astype(jnp.float32)[None, :]

    for c in small:
        c.wait()
    pack_ref[...] = jnp.zeros_like(pack_ref)
    q_row = row(qb_ref)
    if qper >= HEAD:
        for i in range(qper // HEAD):
            pack_ref[i : i + 1, :] = q_row[:, i * HEAD : (i + 1) * HEAD]
    else:
        pack_ref[0:1, :] = placed(q_row)
    pack_ref[2:3, :] = placed(row(kb_ref))
    pack_ref[3:4, :] = placed(row(vb_ref))
    qpos = (lane % FRAME_TOK).astype(jnp.float32)
    for f in range(frames):
        frame = order_ref[f].astype(jnp.float32)
        pack_ref[8 - frames + f : 9 - frames + f, :] = jnp.full((1, HEAD), 1.0, jnp.float32) * frame
        qpos = qpos + jnp.where((lane % rows) // FRAME_TOK == f, frame * FRAME_TOK, 0.0)
    pbuf[me] = pack_ref[...]
    tab = tab_ref[...]
    q_cos, q_sin = cos_sin(pack_ref[8 - frames :, :], tab)
    fold = math.log2(math.e) / math.sqrt(HEAD)
    q_cos, q_sin = q_cos * fold, q_sin * fold
    k_load.wait()
    v_load.wait()
    pl.semaphore_wait(barrier, n - 1)

    def pack_copy(i, s):
        return pltpu.make_async_remote_copy(
            src_ref=pack_ref,
            dst_ref=pbuf.at[s],
            send_sem=psend.at[i],
            recv_sem=precv.at[s],
            device_id={"seq": lax.rem(me + i, n)},
            device_id_type=MESH,
        )

    def push(i, _):
        pack_copy(i, me).start()
        return 0

    lax.fori_loop(1, n, push, 0)
    for t in range(PIECES):
        fan(t, me, (0, 1, 2, 3, 4), True)

    acc[...] = jnp.zeros_like(acc)
    den[...] = jnp.zeros_like(den)
    top[...] = jnp.full_like(top, NEG)

    def pulled(i, _):
        pack_copy(i, lax.rem(me + i, n)).wait_recv()
        return 0

    lax.fori_loop(1, n, pulled, 0)
    q_load.wait()

    for h in range(QH):
        if qper >= HEAD:
            per = qper // HEAD
            bias = pbuf[h // per, h % per : h % per + 1, :]
        else:
            parts = HEAD // qper
            bias = sum(pbuf[h * parts + i, 0:1, :] for i in range(parts))
        x = q_ref[:, h * HEAD : (h + 1) * HEAD].astype(jnp.float32) + bias
        at = (h % RATIO) * rows
        qs[h // RATIO, at : at + rows, :] = spin(x, q_cos, q_sin).astype(jnp.bfloat16)
    share = n // KVH
    k_bias = [sum(pbuf[g * share + i, 2:3, :] for i in range(share)) for g in range(KVH)]
    v_bias = [sum(pbuf[g * share + i, 3:4, :] for i in range(share)) for g in range(KVH)]
    within = lax.broadcasted_iota(jnp.int32, (FRAME_TOK, HEAD), 0).astype(jnp.float32)

    def chunk(first):
        for j in range(4):
            s = first + j
            order = pbuf[s][8 - frames :, :]
            cosine, sine = cos_sin(order, tab)
            for f in range(frames):
                kpos = order[f : f + 1, :] * FRAME_TOK + within
                at = j * rows + f * FRAME_TOK
                hide[at : at + FRAME_TOK, :] = jnp.where(kpos <= qpos, 0.0, NEG)
            for g in range(KVH):
                cols = slice(g * HEAD, (g + 1) * HEAD)
                x = kbuf[s, :, cols].astype(jnp.float32) + k_bias[g]
                ksc[g, j * rows : (j + 1) * rows, :] = spin(x, cosine, sine).astype(jnp.bfloat16)
                y = vbuf[s, :, cols].astype(jnp.float32) + v_bias[g]
                vsc[g, j * rows : (j + 1) * rows, :] = y.astype(jnp.bfloat16)
        for g in range(KVH):
            scores = lax.dot_general(
                ksc[g], qs[g], (((1,), (1,)), ((), ())), preferred_element_type=jnp.float32
            )
            mask = hide[...]
            scores = scores + jnp.concatenate([mask] * (scores.shape[1] // HEAD), axis=1)
            old = top[g]
            new = jnp.maximum(old, jnp.max(scores, axis=0, keepdims=True))
            expo = jnp.exp2(scores - new)
            factor = jnp.exp2(old - new)
            top[g] = new
            den[g] = den[g] * factor + jnp.sum(expo, axis=0, keepdims=True)
            acc[g] = acc[g] * factor + lax.dot_general(
                vsc[g], expo.astype(jnp.bfloat16), (((0,), (0,)), ((), ())),
                preferred_element_type=jnp.float32,
            )

    low = a < A // 2
    mirror = jnp.where(low, a, A - 1 - a)

    def step(d, _):
        along_a(d + 1, True)
        along_b(d, True)
        near = jnp.where(d % 2 == 1, -((d + 1) // 2), d // 2)
        plane = mirror + jnp.where(d <= 2 * mirror, near, d - mirror)
        plane = jnp.where(low, plane, A - 1 - plane)
        for y in range(B):
            for t in range(PIECES):
                arrive(t, slot(plane, y, 1 - core))
        if 2 * B == 4:
            chunk(plane * 4)
        else:
            def part(i, _):
                chunk(plane * 2 * B + i * 4)
                return 0

            lax.fori_loop(0, 2 * B // 4, part, 0)
        return 0

    lax.fori_loop(0, A, step, 0)

    for g in range(KVH):
        mixed = acc[g] * (1.0 / den[g])
        flat = mixed.T.astype(jnp.bfloat16)
        for r in range(RATIO):
            h = g * RATIO + r
            o_ref[:, h * HEAD : (h + 1) * HEAD] = flat[r * rows : (r + 1) * rows, :]

    for t in range(PIECES):
        fan(t, me, (0, 1, 2, 3, 4), False)

    def drain(d, _):
        along_a(d + 1, False)
        along_b(d, False)
        return 0

    lax.fori_loop(0, A, drain, 0)

    def pushed(i, _):
        pack_copy(i, me).wait_send()
        return 0

    lax.fori_loop(1, n, pushed, 0)


def line_tables():
    rows = tables()
    pair = np.arange(HEAD) % HALF
    temporal = pair < PAIRS_T
    rows[0:32, temporal] = 0.0
    rows[32] = np.where(temporal, rows[32], 0.0)
    rows[33] = np.where(temporal, 1.0, 0.0)
    rows[34] = np.where(temporal, np.where(np.arange(HEAD) < HALF, -1.0, 1.0), 0.0)
    return rows


def circle(x):
    k = jnp.round(x * (2.0 / math.pi))
    r = x - k * 1.5703125
    r = r - k * (math.pi / 2.0 - 1.5703125)
    w = r * r
    s = r + r * w * (-1.6666654611e-1 + w * (8.3321608736e-3 - w * 1.9515295891e-4))
    c = 1.0 - 0.5 * w + w * w * (4.166664568298827e-2 + w * (-1.388731625493765e-3 + w * 2.443315711809948e-5))
    turn = k - 4.0 * jnp.floor(k * 0.25)
    odd = jnp.logical_or(turn == 1.0, turn == 3.0)
    cosine = jnp.where(odd, s, c)
    sine = jnp.where(odd, c, s)
    cosine = jnp.where(jnp.logical_or(turn == 1.0, turn == 2.0), -cosine, cosine)
    sine = jnp.where(turn >= 2.0, -sine, sine)
    return cosine, sine


def line_kernel(
    n,
    q_hbm, k_hbm, v_hbm, qb_hbm, kb_hbm, vb_hbm, order_hbm, tab_hbm,
    o_ref,
    qb_ref, kb_ref, vb_ref, order_ref, tab_ref,
    q_ref, kv, pbuf, ctab, stab, ftab, qs, acc, top, den, ksc, hide, obuf,
    recv, send, precv, psend, qsem, osem, load, entered,
):
    me = lax.axis_index("seq")
    rows = k_hbm.shape[0]
    frames = rows // FRAME_TOK
    half = KVH // 2
    wide = half * HEAD
    qwide = QH * HEAD // 2
    core = me % 2
    y = (me // 2) % 2
    z = me // 4
    sib = me + 1 - 2 * core
    low = z < 2
    end = jnp.logical_or(z == 0, z == 3)
    mid = jnp.logical_not(end)

    def slot(a, b, c):
        return (a * 2 + b) * 2 + c

    def up(i):
        return jnp.where(low, i, 3 - i)

    Z0, Z1, Z2, Z3 = up(0), up(1), up(2), up(3)

    def to(s):
        return dict(device_id={"seq": s}, device_id_type=MESH)

    def part(c, size):
        return pl.ds(pl.multiple_of(c * size, size), size)

    barrier = pltpu.get_barrier_semaphore()

    def greet(other, _):
        @pl.when(other != me)
        def _():
            pl.semaphore_signal(barrier, inc=1, **to(other))

        return 0

    def tell(other, _):
        pl.semaphore_signal(entered.at[z], inc=1, **to(other))
        return 0

    def above(i):
        @pl.when(z + i < 4)
        def _():
            pl.semaphore_wait(entered.at[jnp.minimum(z + i, 3)], 4)

    lax.fori_loop(4 * z, n, greet, 0)
    small = [
        pltpu.make_async_copy(src, dst, load.at[i])
        for i, (src, dst) in enumerate((
            (order_hbm, order_ref), (qb_hbm, qb_ref), (kb_hbm, kb_ref), (vb_hbm, vb_ref), (tab_hbm, tab_ref),
        ))
    ]
    mine = [
        pltpu.make_async_copy(k_hbm.at[:, part(core, wide)], kv.at[me], load.at[5]),
        pltpu.make_async_copy(v_hbm.at[:, part(core, wide)], kv.at[n + me], load.at[6]),
        pltpu.make_async_copy(q_hbm.at[:, part(core, qwide)], q_ref.at[0], load.at[7]),
    ]
    for c in small + mine:
        c.start()

    lane = lax.broadcasted_iota(jnp.int32, (1, HEAD), 1)
    group = lane // (HEAD // KVH)

    def row(ref):
        return ref[...].astype(jnp.float32)[None, :]

    def placed(values, at):
        return jnp.where(group == at % KVH, jnp.concatenate([values] * KVH, axis=1), 0.0)

    pl.semaphore_wait(barrier, 4 * z + 3)

    def own(t, dz, dy, dc, relay=False):
        at = (2 + t if relay else t) * n + me
        return pltpu.make_async_remote_copy(
            src_ref=(k_hbm, v_hbm)[t].at[:, part(dc, wide)],
            dst_ref=kv.at[at],
            send_sem=send.at[0],
            recv_sem=recv.at[at],
            **to(slot(dz, dy, 1 if relay else dc)),
        )

    def passed(source, target, s):
        return pltpu.make_async_remote_copy(
            src_ref=kv.at[source],
            dst_ref=kv.at[target],
            send_sem=send.at[1],
            recv_sem=recv.at[target],
            **to(s),
        )

    sent = [[0, 0] for _ in range(4)]

    def own_to(planes, t, dz, dy, relay):
        for dc in (0, 1):
            own(t, dz, dy, dc, relay and dc == 0).start()
        for p in planes:
            sent[p][0] += 2

    def arrive(t, s):
        passed(t * n + s, t * n + s, sib).wait_recv()

    def pack_copy(i, s):
        return pltpu.make_async_remote_copy(
            src_ref=pbuf.at[:, pl.ds(s, 1)],
            dst_ref=pbuf.at[:, pl.ds(s, 1)],
            send_sem=psend,
            recv_sem=precv.at[s],
            **to(lax.rem(me + i, n)),
        )

    def push(upward):
        def act(other, _):
            @pl.when(other != me)
            def _():
                pack_copy(other - me + n, me).start()

            return 0

        lax.fori_loop(*((4 * z + 4, n) if upward else (0, 4 * z + 4)), act, 0)

    def ways(t):
        pl.when(z > 0)(lambda: own_to((1, 2, 3), t, z - 1, y, True))
        if t == 0:
            own_to((0, 1, 2, 3), t, z, 1 - y, False)
        else:
            pl.when(end)(lambda: own_to((0, 3), t, z, 1 - y, True))
            pl.when(mid)(lambda: own_to((1, 2), t, z, 1 - y, False))

    ways(0)
    lax.fori_loop(0, 4 * z, tell, 0)
    for c in small:
        c.wait()
    q_row = row(qb_ref)
    pbuf[0, pl.ds(me, 1), :] = q_row[:, :HEAD]
    pbuf[1, pl.ds(me, 1), :] = q_row[:, HEAD:]
    third = placed(row(kb_ref), me) + placed(row(vb_ref), me + 1)
    for f in range(frames):
        third = third + jnp.where(lane == (me + 2) % KVH * (HEAD // KVH) + f, order_ref[f].astype(jnp.float32), 0.0)
    pbuf[2, pl.ds(me, 1), :] = third
    push(False)
    ways(1)
    q_send = pltpu.make_async_remote_copy(
        src_ref=q_hbm.at[:, part(1 - core, qwide)], dst_ref=q_ref.at[1],
        send_sem=qsem.at[0], recv_sem=qsem.at[1], **to(sib),
    )
    q_send.start()
    for t in (0, 1):
        own(t, z, y, 1 - core).start()
        for r in sent:
            r[0] += 1

    ORDER = (1, 0)
    def role(plane, steps):
        def forward():
            for t, s, targets in steps:
                for kind in (2 + t, t):
                    source = kind * n + s
                    passed(source, source, sib).wait_recv()
                    for dz, dy, relay in targets:
                        if kind == t or relay:
                            passed(source, source, slot(dz, dy, 1)).start()
                        else:
                            passed(source, t * n + s, slot(dz, dy, 0)).start()
                        sent[plane][1] += 1
                    if kind != t:
                        passed(source, t * n + s, sib).start()
                        sent[plane][1] += 1

        def take():
            for t, s, _ in steps:
                arrive(t, s)

        pl.when(jnp.logical_and(z == plane, core == 1))(forward)
        pl.when(jnp.logical_and(z == plane, core == 0))(take)

    def both(t, dz, dy, targets):
        return [(t, slot(dz, dy, k), targets) for k in ORDER]

    across = (z, 1 - y, False)

    def gather(t, dz, dy):
        for k in ORDER:
            arrive(t, slot(dz, dy, k))

    above(1)
    for t in (0, 1):
        pl.when(z < 3)(lambda: own_to((0, 1, 2), t, z + 1, y, True))
    relay = [(p, y, True) for p in range(4)]
    last = [(p, y, False) for p in range(4)]
    role(0, both(0, 1, y, [across]))
    role(1, both(0, 2, y, [relay[0], across]))
    role(2, both(0, 3, y, [relay[1], across]))
    role(3, both(1, 3, 1 - y, [relay[1], last[2]]))
    above(2)
    above(3)
    push(True)
    role(0, both(1, 0, 1 - y, [relay[2], last[1]]) + both(1, 1, y, [across]))
    role(1, both(1, 2, y, [relay[0], across]) + both(0, 0, y, [relay[2], across]))
    role(2, both(1, 3, y, [relay[1]]) + both(0, 1, y, [relay[3], across]))
    role(3, both(0, 2, y, [across]) + both(1, 2, y, [across]))

    def pulled(i, _):
        pack_copy(i, lax.rem(me + i, n)).wait_recv()
        return 0

    lax.fori_loop(1, n, pulled, 0)
    tab = tab_ref[...]
    third = pbuf[2]
    at = lax.broadcasted_iota(jnp.int32, (n, HEAD), 0)
    spot = lax.broadcasted_iota(jnp.int32, (n, HEAD), 1) - (at + 2) % KVH * (HEAD // KVH)
    for f in range(frames):
        frame = jnp.sum(jnp.where(spot == f, third, 0.0), axis=1, keepdims=True)
        frame = jnp.broadcast_to(frame, (n, HEAD))
        cosine, sine = circle(frame * tab[32:33, :])
        ctab[f] = cosine * tab[33:34, :]
        stab[f] = sine * tab[34:35, :]
        ftab[f] = frame * FRAME_TOK

    def bias_row(g, turn):
        got = jnp.zeros((1, HEAD), jnp.float32)
        for i in range(KVH):
            piece = pbuf[2, pl.ds((core * half + g) * KVH + i, 1), :]
            got = got + jnp.where(group == (i + turn) % KVH, piece, 0.0)
        return got if turn == 0 else pltpu.roll(got, HEAD - turn * (HEAD // KVH), 1)

    k_bias = [bias_row(g, 0) for g in range(half)]
    v_bias = [bias_row(g, 1) for g in range(half)]

    def angles(s):
        cosines = [ctab[f, pl.ds(s, 1), :] + tab[0:16, :] for f in range(frames)]
        sines = [stab[f, pl.ds(s, 1), :] + tab[16:32, :] for f in range(frames)]
        return jnp.concatenate(cosines, axis=0), jnp.concatenate(sines, axis=0)

    fold = math.log2(math.e) / math.sqrt(HEAD)
    q_cos, q_sin, q_pos = [], [], []
    for s in (sib, me):
        cosine, sine = angles(s)
        q_cos.append(cosine * fold)
        q_sin.append(sine * fold)
        qpos = (lane % FRAME_TOK).astype(jnp.float32)
        for f in range(frames):
            qpos = qpos + jnp.where(lane % rows // FRAME_TOK == f, ftab[f, pl.ds(s, 1), :], 0.0)
        q_pos.append(qpos)
    blocks = RATIO * rows // HEAD
    within = lax.broadcasted_iota(jnp.int32, (FRAME_TOK, HEAD), 0).astype(jnp.float32)

    def turn_keys(first, count, at):
        for j in range(count):
            s = first + j
            cosine, sine = angles(s)
            for f in range(frames):
                kpos = ftab[f, pl.ds(s, 1), :] + within
                r = at + j * rows + f * FRAME_TOK
                for k in range(2):
                    hide[k, r : r + FRAME_TOK, :] = jnp.where(kpos <= q_pos[k], 0.0, NEG)
            for g in range(half):
                x = kv[s, :, g * HEAD : (g + 1) * HEAD].astype(jnp.float32) + k_bias[g]
                r = at + j * rows
                ksc[g, r : r + rows, :] = spin(x, cosine, sine).astype(jnp.bfloat16)

    def attend(g, k, spans, at, fresh, finish=None):
        vals = jnp.concatenate([
            kv[pl.ds(n + first, count), :, g * HEAD : (g + 1) * HEAD].reshape(count * rows, HEAD)
            for first, count in spans
        ], axis=0)
        keys = slice(at, at + vals.shape[0])
        mask = hide[k, keys, :]
        for b in range(k * blocks, (k + 1) * blocks):
            cols = slice(b * HEAD, (b + 1) * HEAD)
            scores = lax.dot_general(
                ksc[g, keys, :], qs[g, cols, :], (((1,), (1,)), ((), ())), preferred_element_type=jnp.float32
            )
            scores = scores + mask
            new = jnp.max(scores, axis=0, keepdims=True)
            if not fresh:
                old = top[g, :, cols]
                new = jnp.maximum(old, new)
            expo = jnp.exp2(scores - new)
            total = jnp.sum(expo, axis=0, keepdims=True)
            mixed = lax.dot_general(
                vals, expo.astype(jnp.bfloat16), (((0,), (0,)), ((), ())), preferred_element_type=jnp.float32
            )
            if finish is not None:
                factor = jnp.exp2(old - new)
                scale = 1.0 / (den[g, :, cols] * factor + total)
                finish(b - k * blocks, (acc[g, :, cols] * factor + mixed) * scale)
                continue
            top[g, :, cols] = new
            if fresh:
                den[g, :, cols] = total
                acc[g, :, cols] = mixed
            else:
                factor = jnp.exp2(old - new)
                den[g, :, cols] = den[g, :, cols] * factor + total
                acc[g, :, cols] = acc[g, :, cols] * factor + mixed

    def chunk(spans, at, fresh):
        for g in range(half):
            for k in range(2):
                attend(g, k, spans, at, fresh)

    mine[2].wait()
    q_send.wait_recv()
    for k in range(2):
        for h in range(QH // 2):
            bias = pbuf[h % 2, pl.ds(core * (n // 2) + h // 2, 1), :]
            x = q_ref[1 - k, :, h * HEAD : (h + 1) * HEAD].astype(jnp.float32) + bias
            r = (k * RATIO + h % RATIO) * rows
            qs[h // RATIO, r : r + rows, :] = spin(x, q_cos[k], q_sin[k]).astype(jnp.bfloat16)

    for c in mine[:2]:
        c.wait()
    arrive(0, sib)
    gather(0, z, 1 - y)
    turn_keys(z * 4, 4, 0)
    arrive(1, sib)
    near = jnp.where(end, Z1, Z0)
    role(0, both(0, 2, y, [across]))
    role(1, both(0, 3, y, [relay[0], across]) + both(1, 0, y, [relay[2]]))
    role(2, both(1, 1, y, [relay[3], across]) + both(0, 0, y, [relay[3], across]))
    role(3, both(0, 1, y, [across]))
    pl.when(mid)(lambda: gather(1, z, 1 - y))
    chunk([(z * 4, 4)], 0, True)
    role(0, both(1, 2, y, [across]))
    role(1, both(1, 3, y, [last[0]]))
    role(2, both(1, 0, y, [last[3]]))
    role(3, both(1, 1, y, [across]))
    role(0, both(0, 3, y, [across]))
    role(1, both(1, 3, 1 - y, [last[0]]))
    role(2, both(1, 0, 1 - y, [last[3]]))
    role(3, both(0, 0, y, [across]))
    gather(0, near, 1 - y)
    turn_keys(near * 4, 4, 4 * rows)
    gather(1, near, 1 - y)
    chunk([(near * 4, 4)], 4 * rows, False)
    here = [(slot(p, y, 0), 2) for p in (Z2, Z3)]
    over = [(slot(p, 1 - y, 0), 2) for p in (Z2, Z3)]
    for i, (first, count) in enumerate(here):
        turn_keys(first, count, (8 + 2 * i) * rows)
    pl.when(end)(lambda: gather(1, Z3, y))
    chunk(here, 8 * rows, False)
    for i, (first, count) in enumerate(over):
        gather(0, (Z2, Z3)[i], 1 - y)
        turn_keys(first, count, (12 + 2 * i) * rows)
    gather(1, Z2, 1 - y)
    pl.when(end)(lambda: gather(1, Z3, 1 - y))

    out = []
    for k in range(2):
        for g in range(half):
            def finish(b, mixed, g=g, k=k):
                flat = (mixed.T + v_bias[g]).astype(jnp.bfloat16)
                for i in range(HEAD // rows):
                    h = b * (HEAD // rows) + i
                    piece = flat[i * rows : (i + 1) * rows, :]
                    if k == 0:
                        obuf[g, :, h * HEAD : (h + 1) * HEAD] = piece
                    else:
                        at = core * qwide + (g * RATIO + h) * HEAD
                        o_ref[:, pl.ds(pl.multiple_of(at, HEAD), HEAD)] = piece

            attend(g, k, over, 12 * rows, False, finish)
            if k == 0:
                at = core * qwide + g * RATIO * HEAD
                c = pltpu.make_async_remote_copy(
                    src_ref=obuf.at[g],
                    dst_ref=o_ref.at[:, pl.ds(pl.multiple_of(at, HEAD), RATIO * HEAD)],
                    send_sem=osem.at[g], recv_sem=osem.at[half + g], **to(sib),
                )
                c.start()
                out.append(c)

    def drain(plane_at, i):
        size = kv.at[pl.ds(0, sent[plane_at][i])]
        pltpu.make_async_copy(size, size, send.at[i]).wait()

    for plane_at in range(4):
        pl.when(z == plane_at)(functools.partial(drain, plane_at, 0))
        pl.when(jnp.logical_and(z == plane_at, core == 1))(functools.partial(drain, plane_at, 1))
    size = pbuf.at[:, pl.ds(0, n - 1)]
    pltpu.make_async_copy(size, size, psend).wait()
    q_send.wait_send()
    for c in out:
        c.wait()


def on_line(n, query, keys, values, query_bias, key_bias, value_projection_bias, frame_order):
    rows = keys.shape[0]
    half = KVH // 2
    frames = rows // FRAME_TOK
    wide = RATIO * 2 * rows
    return pl.pallas_call(
        functools.partial(line_kernel, n),
        out_shape=jax.ShapeDtypeStruct(query.shape, jnp.bfloat16),
        in_specs=[pl.BlockSpec(memory_space=pltpu.HBM)] * 8,
        out_specs=pl.BlockSpec(memory_space=pltpu.VMEM),
        scratch_shapes=[
            pltpu.VMEM(query_bias.shape, jnp.bfloat16),
            pltpu.VMEM(key_bias.shape, jnp.bfloat16),
            pltpu.VMEM(key_bias.shape, jnp.bfloat16),
            pltpu.SMEM(frame_order.shape, jnp.int32),
            pltpu.VMEM((40, HEAD), jnp.float32),
            pltpu.VMEM((2, rows, QH * HEAD // 2), jnp.bfloat16),
            pltpu.VMEM((4 * n, rows, half * HEAD), jnp.bfloat16),
            pltpu.VMEM((3, n, HEAD), jnp.float32),
            pltpu.VMEM((frames, n, HEAD), jnp.float32),
            pltpu.VMEM((frames, n, HEAD), jnp.float32),
            pltpu.VMEM((frames, n, HEAD), jnp.float32),
            pltpu.VMEM((half, wide, HEAD), jnp.bfloat16),
            pltpu.VMEM((half, HEAD, wide), jnp.float32),
            pltpu.VMEM((half, 1, wide), jnp.float32),
            pltpu.VMEM((half, 1, wide), jnp.float32),
            pltpu.VMEM((half, n * rows, HEAD), jnp.bfloat16),
            pltpu.VMEM((2, n * rows, HEAD), jnp.float32),
            pltpu.VMEM((half, rows, RATIO * HEAD), jnp.bfloat16),
            pltpu.SemaphoreType.DMA((4 * n,)),
            pltpu.SemaphoreType.DMA((2,)),
            pltpu.SemaphoreType.DMA((n,)),
            pltpu.SemaphoreType.DMA,
            pltpu.SemaphoreType.DMA((2,)),
            pltpu.SemaphoreType.DMA((2 * half,)),
            pltpu.SemaphoreType.DMA((8,)),
            pltpu.SemaphoreType.REGULAR((4,)),
        ],
        compiler_params=pltpu.CompilerParams(vmem_limit_bytes=24 << 20, collective_id=1, has_side_effects=True),
    )(*(
        pltpu.with_memory_space_constraint(x, pltpu.HBM)
        for x in (
            query, keys, values, query_bias, key_bias, value_projection_bias, frame_order,
            jnp.asarray(line_tables()),
        )
    ))


def on_device(n, query, keys, values, query_bias, key_bias, value_projection_bias, frame_order):
    chips = n // 2
    B = 1
    while B * B * 4 <= chips:
        B *= 2
    A = chips // B
    rows = keys.shape[0]
    qper = query_bias.shape[0]
    wide = RATIO * rows
    keys_at_once = 4 * rows
    whole = pl.BlockSpec(memory_space=pltpu.VMEM)
    far = pl.BlockSpec(memory_space=pltpu.HBM)
    return pl.pallas_call(
        functools.partial(kernel, A, B, n, qper),
        out_shape=jax.ShapeDtypeStruct(query.shape, jnp.bfloat16),
        in_specs=[far] * 8,
        out_specs=whole,
        scratch_shapes=[
            pltpu.VMEM(query_bias.shape, jnp.bfloat16),
            pltpu.VMEM(key_bias.shape, jnp.bfloat16),
            pltpu.VMEM(key_bias.shape, jnp.bfloat16),
            pltpu.SMEM(frame_order.shape, jnp.int32),
            pltpu.VMEM((40, HEAD), jnp.float32),
            pltpu.VMEM(query.shape, jnp.bfloat16),
            pltpu.VMEM((8, HEAD), jnp.float32),
            pltpu.VMEM((n, rows, KVH * HEAD), jnp.bfloat16),
            pltpu.VMEM((n, rows, KVH * HEAD), jnp.bfloat16),
            pltpu.VMEM((n, 8, HEAD), jnp.float32),
            pltpu.VMEM((KVH, wide, HEAD), jnp.bfloat16),
            pltpu.VMEM((KVH, HEAD, wide), jnp.float32),
            pltpu.VMEM((KVH, 1, wide), jnp.float32),
            pltpu.VMEM((KVH, 1, wide), jnp.float32),
            pltpu.VMEM((KVH, keys_at_once, HEAD), jnp.bfloat16),
            pltpu.VMEM((KVH, keys_at_once, HEAD), jnp.bfloat16),
            pltpu.VMEM((keys_at_once, HEAD), jnp.float32),
            pltpu.SemaphoreType.DMA((PIECES, n)),
            pltpu.SemaphoreType.DMA((PIECES, 5, n)),
            pltpu.SemaphoreType.DMA((n,)),
            pltpu.SemaphoreType.DMA((n,)),
            pltpu.SemaphoreType.DMA((8,)),
        ],
        compiler_params=pltpu.CompilerParams(vmem_limit_bytes=(16 if n <= 32 else 48) << 20, collective_id=0, has_side_effects=True),
    )(*(
        pltpu.with_memory_space_constraint(x, pltpu.HBM)
        for x in (
            query, keys, values, query_bias, key_bias, value_projection_bias, frame_order,
            jnp.asarray(tables()),
        )
    ))


def solution(mesh):
    placed = (
        P(("groups", "seq"), None),
        P(("groups", "seq"), None),
        P(("groups", "seq"), None),
        P("seq"),
        P("seq"),
        P("seq"),
        P(("groups", "seq")),
    )
    n = mesh.shape["seq"]
    return jax.shard_map(
        functools.partial(on_line if n == 16 else on_device, n),
        mesh=mesh,
        in_specs=placed,
        out_specs=P(("groups", "seq"), None),
        check_vma=False,
    )
```
